32 devices in a mesh: seq: 4 (over y, x), exp: 8 (over z, core).
Axes of the slice: x: 2, y: 2, z: 4, core: 2. Of those that a mesh axis runs over, the one named last changes fastest.
Arguments:
- layer_input: bfloat16 [8192, 1024], P(('seq', 'exp')), may hold values from -6 to 6
- doc_ids: int32 [4, 2048], P('seq'), may hold values from 0 to 3, never falling along the last dimension, each value on 1 to 1024 neighbouring positions
- expert_routes: int32 [8192, 8], P(('seq', 'exp')), may hold values from 0 to 31, all different within a row; in each aligned block of 256 rows (0 to 255, 256 to 511, ...) at most 128 rows name the same one
- attn_gain: bfloat16 [1024], P(('seq', 'exp')), may hold values from 0.5 to 1.5
- query_weight: bfloat16 [1024, 1024], P(('seq', 'exp')), may hold values from -0.1875 to 0.1875
- key_projection_weight: bfloat16 [1024, 512], P(('seq', 'exp')), may hold values from -0.1875 to 0.1875
- value_projection_weight: bfloat16 [1024, 512], P(('seq', 'exp')), may hold values from -0.1875 to 0.1875
- out_weight: bfloat16 [1024, 1024], P(('seq', 'exp')), may hold values from -0.75 to 0.75
- ffn_gain: bfloat16 [1024], P(('seq', 'exp')), may hold values from 0.5 to 1.5
- router_weight: bfloat16 [1024, 32], P(('seq', 'exp')), may hold values from -0.09375 to 0.09375
- gate_weight: bfloat16 [32, 1024, 512], P('exp', 'seq'), may hold values from -0.1875 to 0.1875
- up_weight: bfloat16 [32, 1024, 512], P('exp', 'seq'), may hold values from -0.1875 to 0.1875
- down_weight: bfloat16 [32, 512, 1024], P('exp', 'seq'), may hold values from -1 to 1
- out_cotangent: bfloat16 [8192, 1024], P(('seq', 'exp')), may hold values from -6 to 6
Outputs:
- layer_output: bfloat16 [8192, 1024], P(('seq', 'exp'))
- input_grad: float32 [8192, 1024], P(('seq', 'exp'))
- attn_gain_grad: float32 [1024], P(('seq', 'exp'))
- query_grad: float32 [1024, 1024], P(('seq', 'exp'))
- key_grad: float32 [1024, 512], P(('seq', 'exp'))
- value_grad: float32 [1024, 512], P(('seq', 'exp'))
- out_weight_grad: float32 [1024, 1024], P(('seq', 'exp'))
- ffn_gain_grad: float32 [1024], P(('seq', 'exp'))
- router_grad: float32 [1024, 32], P(('seq', 'exp'))
- gate_grad: float32 [32, 1024, 512], P('exp', 'seq')
- up_grad: float32 [32, 1024, 512], P('exp', 'seq')
- down_grad: float32 [32, 512, 1024], P('exp', 'seq')
The draws below stay inside these ranges and needn't reach their ends.
Inputs may be any that keep to these rules, and one draw needn't show every extreme that they name: `doc_ids`: within each packed row the document numbers never fall; each document holds at most half of 2048 tokens, and one holds exactly that many. `expert_routes`: each token names 8 different experts. Among the 256 tokens of one device no expert is named more than 128 times, and in every draw some device's tokens name some expert exactly 128 times.
All inputs are finite; a program needn't handle non-finite values.
Results may differ from the reference program's by a relative error of at most 0.017.
Values may be sent and summed in bfloat16 or wider, within the bound.
No kernel may reach another device: no remote copies, remote signals or barrier semaphores. Data moves between devices by JAX's collectives and lax.ppermute only.
A program may use at most 256 MiB of HBM per device.

```python
import math
import jax
import jax.numpy as jnp
import numpy as np
from jax import lax

MODEL_WIDTH = 1024
QUERY_HEADS = 16
KEY_VALUE_HEADS = 8
HEAD_SIZE = 64
FF = 512
EXPERTS = 32
TOPK = 8
TOK_DEV = 256
DOCS = 4
KBLOCK = 512
ROW_TOKENS = 2048
PACKED_ROWS = 4
TOTAL_TOKENS = 8192
CAP = 128


def block_levels(stream_key, dims, cuts, low, largest):
    loudness = 1.0
    for axis_at, shards_of in cuts:
        steps = jax.random.uniform(jax.random.fold_in(jax.random.fold_in(stream_key, 6), axis_at), (shards_of,), jnp.float32, low / len(cuts), largest / len(cuts))
        loudness = loudness * jnp.repeat(jnp.exp(steps), dims[axis_at] // shards_of).reshape((-1,) + (1,) * (len(dims) - 1 - axis_at))
    return loudness


def profile(count, total, limit, lean):
    loads = [(1 << 20) // math.isqrt(standing ** lean) + 1 for standing in range(2, count + 1)]
    spare, given = total - limit - (count - 1), [1] * (count - 1)
    while spare > 0:
        movable = [i for i in range(count - 1) if given[i] < limit]
        pool, remaining = sum([loads[i] for i in movable]), spare
        for i in movable:
            more = min(limit - given[i], max(1, remaining * loads[i] // pool), spare)
            given[i] = given[i] + more
            spare = spare - more
    return np.array([limit] + given)


def uneven_parts(key, number_of, total, most, lean):
    if number_of == 2:
        one = jax.random.randint(key, (), max(1, total - most), min(most, total - 1) + 1)
        return jnp.stack([one, total - one])
    lengths = jnp.asarray(profile(number_of, total, most, lean), jnp.int32)
    couples = (number_of - 1) // 2
    giver, sink = lengths[1:1 + 2 * couples:2], lengths[2:2 + 2 * couples:2]
    slack = jnp.minimum(giver - 1, most - sink)
    passed = jax.random.randint(jax.random.fold_in(key, 1), (couples,), 0, 1 << 20) % (slack + 1)
    lengths = lengths.at[1:1 + 2 * couples:2].set(giver - passed).at[2:2 + 2 * couples:2].set(sink + passed)
    return lengths[jax.random.permutation(jax.random.fold_in(key, 2), number_of)]


def routed_block(stream_key, own, number, rows, count, top, most, skew):
    ranking = jax.random.permutation(stream_key, count)
    crowded, usual = portions_of(count, rows * top, most, skew, True), portions_of(count, rows * top, most, skew, False)
    places = jnp.arange(count)

    def named(sizes, turn):
        used = int((sizes > 0).sum())
        fixed = max(1, used // 4)
        shifted = fixed + (places - fixed + turn * (used - fixed)) % max(1, count - fixed)
        return jnp.zeros((count,), jnp.int32).at[ranking[jnp.where(places < fixed, places, shifted)]].set(jnp.asarray(sizes, jnp.int32))

    sizes = jnp.where(number % 4 == 0, named(crowded, number // 4), named(usual, number - number // 4 - 1))
    mixed = jax.random.permutation(jax.random.fold_in(own, 3), count)
    giver, sink = mixed[0:count // 2 * 2:2], mixed[1:count // 2 * 2:2]
    room = jnp.minimum(sizes[giver] - 1, most - sizes[sink]) // 2
    room = jnp.where((giver == ranking[0]) | (sink == ranking[0]) | (sizes[sink] == 0), 0, jnp.maximum(room, 0))
    shifted = jax.random.randint(jax.random.fold_in(own, 4), (count // 2,), 0, 1 << 20) % (room + 1)
    sizes = sizes.at[giver].add(-shifted).at[sink].add(shifted)
    items = jnp.searchsorted(jnp.cumsum(sizes), jnp.arange(rows * top), side="right").astype(jnp.int32)
    grid = items.reshape(top, rows).T
    grid = grid[jax.random.permutation(jax.random.fold_in(own, 1), rows)]
    turn = jax.random.randint(jax.random.fold_in(own, 2), (rows, 1), 0, top)
    return jnp.take_along_axis(grid, (jnp.arange(top)[None, :] + turn) % top, axis=1)


def portions_of(count, total, reach, slope, full):
    portions = [(1 << 20) // math.isqrt(standing ** slope) + 1 for standing in range(1, count + 1)]
    largest = reach if full else min(reach, max(-(-total // count), total * portions[0] // sum(portions)))
    least = 1 if total - largest >= count - 1 else 0
    holding, surplus = [largest] + [least] * (count - 1), total - largest - least * (count - 1)
    while surplus > 0:
        candidates = [i for i in range(1, count) if holding[i] < largest] or [i for i in range(1, count) if holding[i] < reach]
        whole, left = sum([portions[i] for i in candidates]), surplus
        for i in candidates:
            extra = min(reach - holding[i], max(1, left * portions[i] // whole), surplus)
            holding[i] = holding[i] + extra
            surplus = surplus - extra
    return np.array(holding)


def centred(stream_key, extent, spread, most, pieces=(), held_as=jnp.bfloat16):
    values = spread * jax.random.normal(stream_key, extent, jnp.float32)
    if pieces:
        values = values * block_levels(stream_key, extent, pieces, -0.22, 0.18)
    return jnp.clip(values, -most, most).astype(held_as)


def setup_inputs(seed: int = 0) -> dict:
    key_of = jax.random.split(jax.random.key(seed), 15)
    layer_input = centred(key_of[0], (TOTAL_TOKENS, MODEL_WIDTH), 1.0, 6.0, ((0, 32),))
    doc_ids = jax.vmap(lambda own: jnp.searchsorted(jnp.cumsum(uneven_parts(own, DOCS, ROW_TOKENS, ROW_TOKENS // 2, 0)), jnp.arange(ROW_TOKENS), side="right"))(jax.random.split(key_of[1], PACKED_ROWS)).reshape((PACKED_ROWS, ROW_TOKENS)).astype(jnp.int32)
    expert_routes_keys = jax.random.split(jax.random.fold_in(key_of[2], 1), TOTAL_TOKENS // TOK_DEV)
    expert_routes_turns = jax.random.permutation(jax.random.fold_in(key_of[2], 3), TOTAL_TOKENS // TOK_DEV)
    expert_routes = jax.vmap(lambda own, number: routed_block(jax.random.fold_in(key_of[2], 2), own, number, TOK_DEV, EXPERTS, TOPK, CAP, 1))(expert_routes_keys, expert_routes_turns).reshape((TOTAL_TOKENS, TOPK))
    attn_gain = jnp.clip(1.0 + 0.1 * jax.random.normal(key_of[3], (MODEL_WIDTH,), jnp.float32), 0.5, 1.5).astype(jnp.bfloat16)
    query_weight = centred(key_of[4], (MODEL_WIDTH, QUERY_HEADS * HEAD_SIZE), MODEL_WIDTH ** -0.5, 0.1875, ((0, 32),))
    key_projection_weight = centred(key_of[5], (MODEL_WIDTH, KEY_VALUE_HEADS * HEAD_SIZE), MODEL_WIDTH ** -0.5, 0.1875, ((0, 32),))
    value_projection_weight = centred(key_of[6], (MODEL_WIDTH, KEY_VALUE_HEADS * HEAD_SIZE), MODEL_WIDTH ** -0.5, 0.1875, ((0, 32),))
    out_weight = centred(key_of[7], (QUERY_HEADS * HEAD_SIZE, MODEL_WIDTH), (QUERY_HEADS * HEAD_SIZE // 16) ** -0.5, 0.75, ((0, 32),))
    ffn_gain = jnp.clip(1.0 + 0.1 * jax.random.normal(key_of[8], (MODEL_WIDTH,), jnp.float32), 0.5, 1.5).astype(jnp.bfloat16)
    router_weight = centred(key_of[9], (MODEL_WIDTH, EXPERTS), (4 * MODEL_WIDTH) ** -0.5, 0.09375, ((0, 32),))
    gate_weight = centred(key_of[10], (EXPERTS, MODEL_WIDTH, FF), MODEL_WIDTH ** -0.5, 0.1875, ((0, 8), (1, 4)))
    up_weight = centred(key_of[11], (EXPERTS, MODEL_WIDTH, FF), MODEL_WIDTH ** -0.5, 0.1875, ((0, 8), (1, 4)))
    down_weight = centred(key_of[12], (EXPERTS, FF, MODEL_WIDTH), (FF // 16) ** -0.5, 1.0, ((0, 8), (1, 4)))
    out_cotangent = centred(key_of[13], (TOTAL_TOKENS, MODEL_WIDTH), 1.0, 6.0, ((0, 32),))
    return {"layer_input": layer_input, "doc_ids": doc_ids, "expert_routes": expert_routes, "attn_gain": attn_gain, "query_weight": query_weight, "key_projection_weight": key_projection_weight, "value_projection_weight": value_projection_weight, "out_weight": out_weight, "ffn_gain": ffn_gain, "router_weight": router_weight, "gate_weight": gate_weight, "up_weight": up_weight, "down_weight": down_weight, "out_cotangent": out_cotangent}


eps_norm = 1e-06
rope_base = 10000.0
score_masked = -1e+30
highest = lax.Precision.HIGHEST

@jax.custom_vjp
def reduced_precision(v):
    return lax.optimization_barrier(v.astype(jnp.bfloat16)).astype(jnp.float32)

@jax.custom_vjp
def reduced_backward(v):
    return v

def low_keep(v):
    return (reduced_precision(v), None)

def low_pass(kept, grad):
    return (grad,)

def back_keep(v):
    return (v, None)

def back_low(kept, grad):
    return (reduced_precision(grad),)
reduced_precision.defvjp(low_keep, low_pass)
reduced_backward.defvjp(back_keep, back_low)

def elementwise_product(left, right):
    return jnp.dot(left, right, precision=highest, preferred_element_type=jnp.float32)

def rms_scale(values, gain_vec):
    return values * lax.rsqrt(lax.optimization_barrier(jnp.mean(values * values, axis=-1, keepdims=True)) + eps_norm) * gain_vec

def doc_positions(seg_row):
    length = seg_row.shape[0]
    places = jnp.arange(length, dtype=jnp.int32)
    starts = jnp.concatenate([jnp.ones((1,), dtype=jnp.bool_), seg_row[1:] != seg_row[:-1]])
    first_place = lax.cummax(jnp.where(starts, places, 0).astype(jnp.int32), axis=0)
    return places - first_place

def apply_rotary(values, token_positions, direction):
    half_size = values.shape[-1] // 2
    inv_freq = rope_base ** (-2.0 * jnp.arange(half_size, dtype=jnp.float32) / values.shape[-1])
    angles = token_positions.astype(jnp.float32)[:, None] * inv_freq[None, :]
    cosine = jnp.cos(angles)[:, None, :]
    sine_part = direction * jnp.sin(angles)[:, None, :]
    first_half = values[..., :half_size]
    second_half = values[..., half_size:]
    return jnp.concatenate([first_half * cosine - second_half * sine_part, second_half * cosine + first_half * sine_part], axis=-1)

def slot_tables(route_rows, expert_count, capacity):
    flat_routes = route_rows.reshape(-1)
    pair_count = flat_routes.shape[0]
    member = (flat_routes[:, None] == jnp.arange(expert_count, dtype=jnp.int32)[None, :]).astype(jnp.int32)
    slot_rank = lax.optimization_barrier(jnp.sum(jnp.cumsum(member, axis=0) * member, axis=1)) - 1
    pair_slot = flat_routes * capacity + slot_rank
    sources = jnp.zeros((expert_count * capacity,), jnp.int32).at[pair_slot].set(jnp.arange(pair_count, dtype=jnp.int32))
    filled = jnp.zeros((expert_count * capacity,), jnp.int32).at[pair_slot].set(jnp.ones((pair_count,), jnp.int32))
    return (pair_slot, sources, filled)

def row_attention(query_row, key_per_row, value_per_row, seg_row):
    row_length = query_row.shape[0]
    blocks_total = row_length // KBLOCK
    key_expanded = jnp.repeat(key_per_row, QUERY_HEADS // KEY_VALUE_HEADS, axis=1)
    value_expanded = jnp.repeat(value_per_row, QUERY_HEADS // KEY_VALUE_HEADS, axis=1)
    key_place = jnp.arange(row_length, dtype=jnp.int32)
    score_scale = HEAD_SIZE ** (-0.5)

    def query_block(block_start):
        query_rows = lax.dynamic_slice_in_dim(query_row, block_start, KBLOCK, 0)
        query_place = block_start + jnp.arange(KBLOCK, dtype=jnp.int32)
        query_doc = lax.dynamic_slice_in_dim(seg_row, block_start, KBLOCK, 0)
        visible = (seg_row[None, :] == query_doc[:, None]) & (key_place[None, :] <= query_place[:, None])
        raw_scores = reduced_backward(jnp.einsum('qhd,khd->hqk', query_rows, key_expanded, precision=highest))
        scores = jnp.where(visible[None], raw_scores * score_scale, score_masked)
        log_total = jax.nn.logsumexp(scores, axis=-1, keepdims=True)
        weights = reduced_precision(jnp.where(visible[None], jnp.exp(scores - log_total), 0.0))
        mixed_heads = jnp.einsum('hqk,khd->qhd', weights, value_expanded, precision=highest)
        return reduced_precision(reduced_backward(mixed_heads)).reshape(KBLOCK, QUERY_HEADS * HEAD_SIZE)
    block_starts = KBLOCK * jnp.arange(blocks_total, dtype=jnp.int32)
    return lax.map(jax.checkpoint(query_block), block_starts).reshape(row_length, QUERY_HEADS * HEAD_SIZE)

def reference(layer_input, doc_ids, expert_routes, attn_gain, query_weight, key_projection_weight, value_projection_weight, out_weight, ffn_gain, router_weight, gate_weight, up_weight, down_weight, out_cotangent):
    token_positions = jax.vmap(doc_positions)(doc_ids).reshape(-1)
    span_count = TOTAL_TOKENS // TOK_DEV
    tables = jax.vmap(lambda route_rows: slot_tables(route_rows, EXPERTS, CAP))(expert_routes.reshape(span_count, TOK_DEV, TOPK))
    sources = tables[1]
    filled = tables[2]
    span_first = jnp.arange(span_count, dtype=jnp.int32)[:, None, None]
    by_expert = sources.reshape(span_count, EXPERTS, CAP)
    token_of = (span_first * TOK_DEV + by_expert // TOPK).transpose(1, 0, 2).reshape(EXPERTS, span_count * CAP)
    pair_of = (span_first * (TOK_DEV * TOPK) + by_expert).transpose(1, 0, 2).reshape(EXPERTS, span_count * CAP)
    used_of = filled.reshape(span_count, EXPERTS, CAP).transpose(1, 0, 2).reshape(EXPERTS, span_count * CAP).astype(jnp.float32)
    picker = (expert_routes[:, :, None] == jnp.arange(EXPERTS, dtype=jnp.int32)[None, None, :]).astype(jnp.float32)

    def forward(inputs, gain_one, query_mat, key_matrix, value_matrix, out_mat, gain_two, router_mat, gate_mat, up_mat, down_mat):
        normalized_input = reduced_precision(rms_scale(inputs, gain_one))
        query_lin = reduced_backward(elementwise_product(normalized_input, query_mat)).reshape(TOTAL_TOKENS, QUERY_HEADS, HEAD_SIZE)
        key_linear = reduced_backward(elementwise_product(normalized_input, key_matrix)).reshape(TOTAL_TOKENS, KEY_VALUE_HEADS, HEAD_SIZE)
        value_reduced = reduced_precision(reduced_backward(elementwise_product(normalized_input, value_matrix))).reshape(PACKED_ROWS, ROW_TOKENS, KEY_VALUE_HEADS, HEAD_SIZE)
        query_low = reduced_precision(apply_rotary(query_lin, token_positions, 1.0)).reshape(PACKED_ROWS, ROW_TOKENS, QUERY_HEADS, HEAD_SIZE)
        key_reduced = reduced_precision(apply_rotary(key_linear, token_positions, 1.0)).reshape(PACKED_ROWS, ROW_TOKENS, KEY_VALUE_HEADS, HEAD_SIZE)
        mixed_all = lax.map(jax.checkpoint(lambda packed: row_attention(packed[0], packed[1], packed[2], packed[3])), (query_low, key_reduced, value_reduced, doc_ids)).reshape(TOTAL_TOKENS, QUERY_HEADS * HEAD_SIZE)
        branch = reduced_backward(elementwise_product(mixed_all, out_mat))
        middle = inputs + branch
        normed_two = reduced_precision(rms_scale(middle, gain_two))
        logits = reduced_backward(elementwise_product(normed_two, router_mat))
        chosen = jnp.einsum('tke,te->tk', picker, logits, precision=highest)
        gate_flat = jax.nn.softmax(chosen, axis=-1).reshape(-1)

        def expert_step(moe_total, stacked):
            gate_one, up_one, down_one, token_rows, pair_rows, used_rows = stacked
            rows_in = reduced_backward(normed_two[token_rows]) * used_rows[:, None]
            gate_pre = reduced_backward(elementwise_product(rows_in, gate_one))
            up_pre = reduced_backward(elementwise_product(rows_in, up_one))
            hidden = reduced_precision(jax.nn.silu(gate_pre) * up_pre)
            rows_out = reduced_precision(reduced_backward(elementwise_product(hidden, down_one)))
            scaled = (gate_flat[pair_rows] * used_rows)[:, None] * rows_out
            return (moe_total.at[token_rows].add(scaled), None)
        moe_sum = lax.scan(jax.checkpoint(expert_step), jnp.zeros((TOTAL_TOKENS, MODEL_WIDTH), jnp.float32), (gate_mat, up_mat, down_mat, token_of, pair_of, used_of))[0]
        return middle + moe_sum
    float_args = tuple((array_in.astype(jnp.float32) for array_in in (layer_input, attn_gain, query_weight, key_projection_weight, value_projection_weight, out_weight, ffn_gain, router_weight, gate_weight, up_weight, down_weight)))
    result, pullback = jax.vjp(forward, *float_args)
    gradients = pullback(out_cotangent.astype(jnp.float32))
    return (result.astype(jnp.bfloat16), gradients[0], gradients[1], gradients[2], gradients[3], gradients[4], gradients[5], gradients[6], gradients[7], gradients[8], gradients[9], gradients[10])
```

```python
import functools

import jax
import jax.numpy as jnp
from jax import lax
from jax.experimental import pallas as pl
from jax.experimental.pallas import tpu as pltpu
from jax.sharding import PartitionSpec as P

MODEL_WIDTH = 1024
QUERY_HEADS = 16
KEY_VALUE_HEADS = 8
HEAD_SIZE = 64
FF = 512
EXPERTS = 32
TOPK = 8
DOCS = 4
CAP = 128

BLOCK = 256
COT_EARLY = 96
LANES = 128
GROUP = QUERY_HEADS // KEY_VALUE_HEADS
PACK = GROUP * HEAD_SIZE

eps_norm = 1e-06
rope_base = 10000.0
score_masked = -1e30
score_scale = HEAD_SIZE**-0.5
f32 = jnp.float32
bf16 = jnp.bfloat16
VMEM_LIMIT = 60 * 1024 * 1024


def dot_nn(a, b):
    return lax.dot_general(a, b, (((1,), (0,)), ((), ())), preferred_element_type=f32)


def dot_nt(a, b):
    return lax.dot_general(a, b, (((1,), (1,)), ((), ())), preferred_element_type=f32)


def dot_tn(a, b):
    return lax.dot_general(a, b, (((0,), (0,)), ((), ())), preferred_element_type=f32)


def swap_halves(v):
    lane = lax.broadcasted_iota(jnp.int32, v.shape, 1)
    half = HEAD_SIZE // 2
    return jnp.where(
        lane % HEAD_SIZE < half, pltpu.roll(v, PACK - half, 1), pltpu.roll(v, half, 1)
    )


def head_stack(v):
    lane = lax.broadcasted_iota(jnp.int32, v.shape, 1)
    zero = jnp.zeros_like(v)
    return jnp.concatenate(
        [jnp.where(lane < HEAD_SIZE, v, zero), jnp.where(lane >= HEAD_SIZE, v, zero)], axis=0
    )


def visible_from(block_key, block_query, start_row):
    shape = (BLOCK, GROUP * BLOCK)
    key_place = block_key * BLOCK + lax.broadcasted_iota(jnp.int32, shape, 0)
    lane = lax.broadcasted_iota(jnp.int32, shape, 1)
    query_place = block_query * BLOCK + lane % BLOCK
    return (key_place >= start_row) & (key_place <= query_place)


def attention_forward_kernel(
    first_block,
    x_ref,
    weight_ref,
    gain_ref,
    cos_ref,
    sin_ref,
    start_ref,
    normed_ref,
    query_ref,
    key_ref,
    value_ref,
    mixed_ref,
    mixed_t_ref,
    log_ref,
    key_all,
    value_all,
):
    i = pl.program_id(0)
    x = x_ref[...].astype(f32)
    normed = (
        x * lax.rsqrt(jnp.mean(x * x, axis=-1, keepdims=True) + eps_norm) * gain_ref[...]
    ).astype(bf16)
    normed_ref[...] = normed
    lin = dot_nn(normed, weight_ref[...])
    cosine, sine = cos_ref[...], sin_ref[...]
    query_lin, key_lin = lin[:, :PACK], lin[:, PACK : 2 * PACK]
    query = (query_lin * cosine + swap_halves(query_lin) * sine).astype(bf16)
    key = (key_lin * cosine + swap_halves(key_lin) * sine).astype(bf16)
    value = lin[:, 2 * PACK :].astype(bf16)
    query_ref[...] = query
    key_ref[...] = key
    value_ref[...] = value
    rows = pl.ds(pl.multiple_of(i * BLOCK, BLOCK), BLOCK)
    key_all[rows, :] = key
    value_all[rows, :] = value
    query_two = head_stack(query * jnp.asarray(score_scale, bf16))
    start_row = start_ref[0]
    start_two = jnp.concatenate([start_row] * GROUP, axis=1)

    def visit(j, carry):
        run_max, run_sum, acc = carry
        here = pl.ds(pl.multiple_of(j * BLOCK, BLOCK), BLOCK)
        scores = dot_nt(key_all[here, :], query_two)
        scores = jnp.where(visible_from(j, i, start_two), scores, score_masked)
        new_max = jnp.maximum(run_max, jnp.max(scores, axis=0, keepdims=True))
        shrink = jnp.exp(run_max - new_max)
        weights = jnp.exp(scores - new_max)
        run_sum = run_sum * shrink + jnp.sum(weights, axis=0, keepdims=True)
        acc = acc * shrink + dot_tn(value_all[here, :], weights.astype(bf16))
        return new_max, run_sum, acc

    width = GROUP * BLOCK
    run_max, run_sum, acc = lax.fori_loop(
        first_block[i],
        i + 1,
        visit,
        (
            jnp.full((1, width), score_masked, f32),
            jnp.zeros((1, width), f32),
            jnp.zeros((PACK, width), f32),
        ),
    )
    acc = acc * (1.0 / run_sum)
    mixed_t = jnp.concatenate([acc[:HEAD_SIZE, :BLOCK], acc[HEAD_SIZE:, BLOCK:]], axis=0)
    mixed_t_ref[0] = mixed_t
    mixed_ref[...] = mixed_t.T.astype(bf16)
    log_ref[0] = run_max + jnp.log(run_sum)


def attention_forward(first_block, x_row, weight, gain, cosine, sine, start):
    tokens = x_row.shape[0]
    blocks = tokens // BLOCK
    row = lambda i, *_: (i, 0)
    page = lambda i, *_: (i, 0, 0)
    whole = lambda i, *_: (0, 0)
    return pl.pallas_call(
        attention_forward_kernel,
        grid_spec=pltpu.PrefetchScalarGridSpec(
            num_scalar_prefetch=1,
            grid=(blocks,),
            in_specs=[
                pl.BlockSpec((BLOCK, MODEL_WIDTH), row),
                pl.BlockSpec(weight.shape, whole),
                pl.BlockSpec((1, MODEL_WIDTH), whole),
                pl.BlockSpec((BLOCK, PACK), row),
                pl.BlockSpec((BLOCK, PACK), row),
                pl.BlockSpec((1, 1, BLOCK), page),
            ],
            out_specs=[
                pl.BlockSpec((BLOCK, MODEL_WIDTH), row),
                pl.BlockSpec((BLOCK, PACK), row),
                pl.BlockSpec((BLOCK, PACK), row),
                pl.BlockSpec((BLOCK, PACK), row),
                pl.BlockSpec((BLOCK, PACK), row),
                pl.BlockSpec((1, PACK, BLOCK), page),
                pl.BlockSpec((1, 1, GROUP * BLOCK), page),
            ],
            scratch_shapes=[pltpu.VMEM((tokens, PACK), bf16), pltpu.VMEM((tokens, PACK), bf16)],
        ),
        out_shape=[
            jax.ShapeDtypeStruct((tokens, MODEL_WIDTH), bf16),
            jax.ShapeDtypeStruct((tokens, PACK), bf16),
            jax.ShapeDtypeStruct((tokens, PACK), bf16),
            jax.ShapeDtypeStruct((tokens, PACK), bf16),
            jax.ShapeDtypeStruct((tokens, PACK), bf16),
            jax.ShapeDtypeStruct((blocks, PACK, BLOCK), f32),
            jax.ShapeDtypeStruct((blocks, 1, GROUP * BLOCK), f32),
        ],
        cost_estimate=cost(
            tokens * (2 * MODEL_WIDTH * 3 * PACK + 8 * PACK * tokens), tokens * MODEL_WIDTH * 4
        ),
        compiler_params=pltpu.CompilerParams(vmem_limit_bytes=VMEM_LIMIT),
        name="attention_forward",
    )(first_block, x_row, weight, gain, cosine, sine, start)


def attention_backward_kernel(
    first_block,
    query_ref,
    grad_ref,
    mixed_t_ref,
    log_ref,
    start_ref,
    cos_ref,
    sin_ref,
    key_ref,
    value_ref,
    lin_grad_ref,
    key_acc,
    value_acc,
):
    i = pl.program_id(0)
    blocks = pl.num_programs(0)

    @pl.when(i == 0)
    def _():
        key_acc[...] = jnp.zeros_like(key_acc)
        value_acc[...] = jnp.zeros_like(value_acc)

    query_two = head_stack(query_ref[...] * jnp.asarray(score_scale, bf16))
    grad = grad_ref[...]
    grad_two = head_stack(grad)
    product = mixed_t_ref[0] * grad.astype(f32).T
    delta = jnp.concatenate(
        [
            jnp.sum(product[:HEAD_SIZE], axis=0, keepdims=True),
            jnp.sum(product[HEAD_SIZE:], axis=0, keepdims=True),
        ],
        axis=1,
    )
    log_total = log_ref[0]
    start_two = jnp.concatenate([start_ref[0]] * GROUP, axis=1)

    def visit(j, query_acc):
        here = pl.ds(pl.multiple_of(j * BLOCK, BLOCK), BLOCK)
        key = key_ref[here, :]
        scores = dot_nt(key, query_two)
        probs = jnp.where(visible_from(j, i, start_two), jnp.exp(scores - log_total), 0.0)
        prob_grad = dot_nt(value_ref[here, :], grad_two)
        score_grad = (probs * (prob_grad - delta)).astype(bf16)
        value_acc[here, :] += dot_nn(probs.astype(bf16), grad_two)
        key_acc[here, :] += dot_nn(score_grad, query_two)
        return query_acc + dot_tn(score_grad, key)

    query_acc = lax.fori_loop(
        first_block[i], i + 1, visit, jnp.zeros((GROUP * BLOCK, PACK), f32)
    )
    lane = lax.broadcasted_iota(jnp.int32, (BLOCK, PACK), 1)
    rotated = jnp.where(lane < HEAD_SIZE, query_acc[:BLOCK], query_acc[BLOCK:]) * score_scale
    rows = pl.ds(pl.multiple_of(i * BLOCK, BLOCK), BLOCK)
    lin_grad_ref[rows, :PACK] = (
        rotated * cos_ref[rows, :] - swap_halves(rotated) * sin_ref[rows, :]
    ).astype(bf16)

    @pl.when(i == blocks - 1)
    def _():
        def finish(b, carry):
            here = pl.ds(pl.multiple_of(b * BLOCK, BLOCK), BLOCK)
            key_sum = key_acc[here, :]
            key_sum = key_sum + pltpu.roll(key_sum, HEAD_SIZE, 1)
            value_sum = value_acc[here, :]
            value_sum = value_sum + pltpu.roll(value_sum, HEAD_SIZE, 1)
            key_lin = key_sum * cos_ref[here, :] - swap_halves(key_sum) * sin_ref[here, :]
            lin_grad_ref[here, PACK:] = jnp.where(lane < HEAD_SIZE, key_lin, value_sum).astype(bf16)
            return carry

        lax.fori_loop(0, blocks, finish, 0)


def attention_backward(first_block, query, grad, mixed_t, log_total, start, cosine, sine, key, value):
    tokens = query.shape[0]
    blocks = tokens // BLOCK
    row = lambda i, *_: (i, 0)
    page = lambda i, *_: (i, 0, 0)
    whole = lambda i, *_: (0, 0)
    return pl.pallas_call(
        attention_backward_kernel,
        grid_spec=pltpu.PrefetchScalarGridSpec(
            num_scalar_prefetch=1,
            grid=(blocks,),
            in_specs=[
                pl.BlockSpec((BLOCK, PACK), row),
                pl.BlockSpec((BLOCK, PACK), row),
                pl.BlockSpec((1, PACK, BLOCK), page),
                pl.BlockSpec((1, 1, GROUP * BLOCK), page),
                pl.BlockSpec((1, 1, BLOCK), page),
                pl.BlockSpec((tokens, PACK), whole),
                pl.BlockSpec((tokens, PACK), whole),
                pl.BlockSpec((tokens, PACK), whole),
                pl.BlockSpec((tokens, PACK), whole),
            ],
            out_specs=pl.BlockSpec((tokens, 2 * PACK), whole),
            scratch_shapes=[pltpu.VMEM((tokens, PACK), f32), pltpu.VMEM((tokens, PACK), f32)],
        ),
        out_shape=jax.ShapeDtypeStruct((tokens, 2 * PACK), bf16),
        cost_estimate=cost(20 * tokens * tokens * PACK, tokens * PACK * 28),
        compiler_params=pltpu.CompilerParams(vmem_limit_bytes=VMEM_LIMIT),
        name="attention_backward",
    )(first_block, query, grad, mixed_t, log_total, start, cosine, sine, key, value)


def middle_kernel(
    home,
    mixed_ref,
    x_ref,
    weight_ref,
    gain_ref,
    router_ref,
    routes_ref,
    normed_ref,
    probs_ref,
    probs_t_ref,
    home_middle_ref,
    home_mixed_ref,
    home_normed_ref,
    home_probs_ref,
):
    i = pl.program_id(0)
    mixed = jnp.concatenate([mixed_ref[h] for h in range(KEY_VALUE_HEADS)], axis=1)
    middle = x_ref[...].astype(f32) + dot_nn(mixed, weight_ref[...])
    normed = (
        middle
        * lax.rsqrt(jnp.mean(middle * middle, axis=-1, keepdims=True) + eps_norm)
        * gain_ref[...]
    ).astype(bf16)
    normed_ref[...] = normed
    logits = dot_nn(normed, router_ref[...])
    routes = routes_ref[...]
    lane = lax.broadcasted_iota(jnp.int32, logits.shape, 1)
    member = jnp.zeros_like(logits)
    for k in range(TOPK):
        member = jnp.where(lane == routes[:, k : k + 1], 1.0, member)
    chosen = jnp.where(member > 0, logits, score_masked)
    raised = jnp.exp(chosen - jnp.max(chosen, axis=-1, keepdims=True)) * member
    probs = raised / jnp.sum(raised, axis=-1, keepdims=True)
    probs_ref[...] = probs
    probs_t_ref[...] = probs.T[:EXPERTS]

    @pl.when(i == home[0])
    def _():
        home_middle_ref[...] = middle
        home_mixed_ref[...] = mixed
        home_normed_ref[...] = normed
        home_probs_ref[...] = probs


def middle_forward(home, mixed, x_row, weight, gain, router, routes):
    tokens = x_row.shape[0]
    row = lambda i, *_: (i, 0)
    whole = lambda i, *_: (0, 0)
    return pl.pallas_call(
        middle_kernel,
        grid_spec=pltpu.PrefetchScalarGridSpec(
            num_scalar_prefetch=1,
            grid=(tokens // BLOCK,),
            in_specs=[
                pl.BlockSpec((KEY_VALUE_HEADS, BLOCK, PACK), lambda i, *_: (0, i, 0)),
                pl.BlockSpec((BLOCK, MODEL_WIDTH), row),
                pl.BlockSpec((MODEL_WIDTH, MODEL_WIDTH), whole),
                pl.BlockSpec((1, MODEL_WIDTH), whole),
                pl.BlockSpec((MODEL_WIDTH, LANES), whole),
                pl.BlockSpec((BLOCK, TOPK), row),
            ],
            out_specs=[
                pl.BlockSpec((BLOCK, MODEL_WIDTH), row),
                pl.BlockSpec((BLOCK, LANES), row),
                pl.BlockSpec((EXPERTS, BLOCK), lambda i, *_: (0, i)),
                pl.BlockSpec((BLOCK, MODEL_WIDTH), whole),
                pl.BlockSpec((BLOCK, MODEL_WIDTH), whole),
                pl.BlockSpec((BLOCK, MODEL_WIDTH), whole),
                pl.BlockSpec((BLOCK, LANES), whole),
            ],
        ),
        out_shape=[
            jax.ShapeDtypeStruct((tokens, MODEL_WIDTH), bf16),
            jax.ShapeDtypeStruct((tokens, LANES), f32),
            jax.ShapeDtypeStruct((EXPERTS, tokens), f32),
            jax.ShapeDtypeStruct((BLOCK, MODEL_WIDTH), f32),
            jax.ShapeDtypeStruct((BLOCK, MODEL_WIDTH), bf16),
            jax.ShapeDtypeStruct((BLOCK, MODEL_WIDTH), bf16),
            jax.ShapeDtypeStruct((BLOCK, LANES), f32),
        ],
        cost_estimate=cost(
            2 * tokens * MODEL_WIDTH * (MODEL_WIDTH + LANES), tokens * MODEL_WIDTH * 6
        ),
        compiler_params=pltpu.CompilerParams(vmem_limit_bytes=VMEM_LIMIT),
        name="middle_forward",
    )(home, mixed, x_row, weight, gain, router, routes)


def cost(flops, moved):
    return pl.CostEstimate(flops=int(flops), transcendentals=0, bytes_accessed=int(moved))


def column_of(values, lane_wanted):
    lane = lax.broadcasted_iota(jnp.int32, values.shape, 1)
    return jnp.sum(
        jnp.where(lane == lane_wanted, values, jnp.zeros_like(values)), axis=-1, keepdims=True
    )


def expert_rows_kernel(shards, experts, group, place, *refs):
    normed_ref, cot_a_ref, cot_b_ref, probs_ref, probs_t_ref, slot_row_ref, slot_col_ref = refs[:7]
    weight_refs = [refs[7 + n * shards : 7 + (n + 1) * shards] for n in range(4)]
    (
        moe_ref,
        row_ref,
        weigh_ref,
        rows_ref,
        out_grad_ref,
        hidden_ref,
        gate_low_ref,
        up_low_ref,
        gate_all,
        up_all,
        down_all,
        out_all,
        back_all,
        sems,
    ) = refs[7 + 4 * shards :]
    first_expert, me = place[0], place[1]
    wide, narrow = MODEL_WIDTH // shards, FF // shards
    half = MODEL_WIDTH // 2

    def copies(e):
        made = []
        for j in range(shards):
            tall = pl.ds(pl.multiple_of((j ^ me) * wide, wide), wide)
            short = pl.ds(pl.multiple_of((j ^ me) * narrow, narrow), narrow)
            places = (
                gate_all.at[e, tall, :],
                up_all.at[e, tall, :],
                down_all.at[e, short, :half],
                down_all.at[e, short, half:],
            )
            for n in range(4):
                made.append(
                    pltpu.make_async_copy(weight_refs[n][j].at[e], places[n], sems.at[e, 4 * j + n])
                )
        return made

    @pl.when(pl.program_id(0) == 0)
    def _():
        for e in range(experts):
            for copy in copies(e):
                copy.start()

    slot_place = lax.broadcasted_iota(jnp.int32, (CAP, BLOCK), 0)
    slot_lane = lax.broadcasted_iota(jnp.int32, (BLOCK, CAP), 1)
    early, late = COT_EARLY, BLOCK - COT_EARLY
    cots = [
        jnp.concatenate(
            [
                cot_a_ref[b * early : (b + 1) * early, :],
                cot_b_ref[b * late : (b + 1) * late, :],
            ],
            axis=0,
        )
        for b in range(group)
    ]
    for e in range(experts):

        @pl.when(pl.program_id(0) == 0)
        def _():
            for copy in copies(e):
                copy.wait()

        picked, cot_picked = [], []
        hits = []
        for b in range(group):
            hit = slot_place == slot_row_ref[0, e * group + b : e * group + b + 1, :]
            hits.append(hit)
            pick = hit.astype(f32).astype(bf16)
            prob_row = probs_t_ref[pl.ds(first_expert + e, 1), b * BLOCK : (b + 1) * BLOCK]
            prob_slot = jnp.sum(jnp.where(hit, prob_row, 0.0), axis=-1, keepdims=True)
            picked.append(dot_nn(pick, normed_ref[b * BLOCK : (b + 1) * BLOCK, :]).astype(bf16))
            cot_picked.append((dot_nn(pick, cots[b]) * prob_slot).astype(bf16))
        rows = jnp.concatenate(picked, axis=0)
        out_grad = jnp.concatenate(cot_picked, axis=0)
        rows_ref[e] = rows
        out_grad_ref[e] = out_grad
        gate_pre = dot_nn(rows, gate_all[e])
        up_pre = dot_nn(rows, up_all[e])
        hidden_grad = dot_nt(out_grad, down_all[e])
        logistic = 1.0 / (1.0 + jnp.exp(-gate_pre))
        silu = gate_pre * logistic
        hidden = (silu * up_pre).astype(bf16)
        gate_low = (
            hidden_grad * up_pre * (logistic * (1.0 + gate_pre * (1.0 - logistic)))
        ).astype(bf16)
        up_low = (hidden_grad * silu).astype(bf16)
        hidden_ref[e] = hidden
        gate_low_ref[e] = gate_low
        up_low_ref[e] = up_low
        weigh = jnp.sum(hidden_grad * hidden.astype(f32), axis=-1, keepdims=True)
        out = dot_nn(hidden, down_all[e]).astype(bf16)
        row_grad = (dot_nt(gate_low, gate_all[e]) + dot_nt(up_low, up_all[e])).astype(bf16)
        for b in range(group):
            inside = slice(b * CAP, (b + 1) * CAP)
            out_all[b, e * CAP : (e + 1) * CAP, :] = out[inside]
            back_all[b, e * CAP : (e + 1) * CAP, :] = row_grad[inside]
            weigh_ref[0, e * group + b : e * group + b + 1, :] = jnp.sum(
                jnp.where(hits[b], weigh[inside], 0.0), axis=0, keepdims=True
            )
    for b in range(group):
        tokens = slice(b * BLOCK, (b + 1) * BLOCK)
        slot_cols, probs = slot_col_ref[tokens, :], probs_ref[tokens, :]
        plain, scaled = [], []
        for e in range(experts):
            hit = slot_lane == column_of(slot_cols, e)
            plain.append(hit.astype(f32).astype(bf16))
            scaled.append(jnp.where(hit, column_of(probs, first_expert + e), 0.0).astype(bf16))
        moe_ref[tokens, :] = dot_nn(jnp.concatenate(scaled, axis=1), out_all[b]).astype(bf16)
        row_ref[tokens, :] = dot_nn(jnp.concatenate(plain, axis=1), back_all[b]).astype(bf16)


def expert_rows(place, normed, cot_a, cot_b, probs, probs_t, slot_rows, slot_cols, weights, group):
    tokens = normed.shape[0]
    shards, experts = len(weights) // 4, weights[0].shape[0]
    span, slots = group * BLOCK, group * CAP
    steps = tokens // span
    row = lambda g, *_: (g, 0)
    page = lambda g, *_: (g, 0, 0)
    spread = lambda g, *_: (0, g, 0)
    total = tokens // BLOCK * CAP
    return pl.pallas_call(
        functools.partial(expert_rows_kernel, shards, experts, group),
        grid_spec=pltpu.PrefetchScalarGridSpec(
            num_scalar_prefetch=1,
            grid=(steps,),
            in_specs=[
                pl.BlockSpec((span, MODEL_WIDTH), row),
                pl.BlockSpec((group * COT_EARLY, MODEL_WIDTH), row),
                pl.BlockSpec((group * (BLOCK - COT_EARLY), MODEL_WIDTH), row),
                pl.BlockSpec((span, LANES), row),
                pl.BlockSpec((EXPERTS, span), lambda g, *_: (0, g)),
                pl.BlockSpec((1, experts * group, BLOCK), page),
                pl.BlockSpec((span, LANES), row),
            ]
            + [pl.BlockSpec(memory_space=pl.ANY)] * (4 * shards),
            out_specs=[
                pl.BlockSpec((span, MODEL_WIDTH), row),
                pl.BlockSpec((span, MODEL_WIDTH), row),
                pl.BlockSpec((1, experts * group, BLOCK), page),
                pl.BlockSpec((experts, slots, MODEL_WIDTH), spread),
                pl.BlockSpec((experts, slots, MODEL_WIDTH), spread),
                pl.BlockSpec((experts, slots, FF), spread),
                pl.BlockSpec((experts, slots, FF), spread),
                pl.BlockSpec((experts, slots, FF), spread),
            ],
            scratch_shapes=[
                pltpu.VMEM((experts, MODEL_WIDTH, FF), bf16),
                pltpu.VMEM((experts, MODEL_WIDTH, FF), bf16),
                pltpu.VMEM((experts, FF, MODEL_WIDTH), bf16),
                pltpu.VMEM((group, experts * CAP, MODEL_WIDTH), bf16),
                pltpu.VMEM((group, experts * CAP, MODEL_WIDTH), bf16),
                pltpu.SemaphoreType.DMA((experts, 4 * shards)),
            ],
        ),
        out_shape=[
            jax.ShapeDtypeStruct((tokens, MODEL_WIDTH), bf16),
            jax.ShapeDtypeStruct((tokens, MODEL_WIDTH), bf16),
            jax.ShapeDtypeStruct((steps, experts * group, BLOCK), f32),
            jax.ShapeDtypeStruct((experts, total, MODEL_WIDTH), bf16),
            jax.ShapeDtypeStruct((experts, total, MODEL_WIDTH), bf16),
            jax.ShapeDtypeStruct((experts, total, FF), bf16),
            jax.ShapeDtypeStruct((experts, total, FF), bf16),
            jax.ShapeDtypeStruct((experts, total, FF), bf16),
        ],
        cost_estimate=cost(
            12 * experts * total * MODEL_WIDTH * FF + 8 * experts * total * MODEL_WIDTH * BLOCK,
            experts * (3 * MODEL_WIDTH * FF + total * (2 * MODEL_WIDTH + 3 * FF)) * 2
            + tokens * MODEL_WIDTH * 8,
        ),
        compiler_params=pltpu.CompilerParams(vmem_limit_bytes=VMEM_LIMIT),
        name="expert_rows",
    )(place, normed, cot_a, cot_b, probs, probs_t, slot_rows, slot_cols, *weights)


def expert_weights_kernel(shards, place, *refs):
    rows_ref, out_grad_ref, hidden_ref, gate_low_ref, up_low_ref = refs[:5]
    outs, (gate_acc, up_acc, down_acc) = refs[5:17], refs[17:]
    me, c = place[1], pl.program_id(1)
    rows = rows_ref[0]
    for acc, left, right in (
        (gate_acc, rows, gate_low_ref[0]),
        (up_acc, rows, up_low_ref[0]),
        (down_acc, hidden_ref[0], out_grad_ref[0]),
    ):
        part = dot_tn(left, right)

        @pl.when(c == 0)
        def _():
            acc[...] = part

        @pl.when(c > 0)
        def _():
            acc[...] += part

    wide, narrow = MODEL_WIDTH // shards, FF // shards
    half = MODEL_WIDTH // 2

    @pl.when(c == pl.num_programs(1) - 1)
    def _():
        for side in range(2):
            square = (gate_acc, up_acc)[side]
            order = exchange_order(shards, side)
            for n, j in enumerate(order):
                kind, at = divmod(n, shards // 2)
                base = (j ^ me) * wide
                low = pl.ds(pl.multiple_of(base, narrow), narrow)
                high = pl.ds(pl.multiple_of(base + narrow, narrow), narrow)
                short = pl.ds(pl.multiple_of((j ^ me) * narrow, narrow), narrow)
                pieces = (
                    square[low, :],
                    square[high, :],
                    down_acc[short, side * half : (side + 1) * half],
                )
                for piece, value in enumerate(pieces):
                    outs[6 * side + 2 * piece + kind][at, 0] = value.astype(bf16)


def exchange_order(shards, side):
    first = (1, 2)[side]
    stay = [j for j in range(shards) if not j & first]
    return stay + [j ^ first for j in stay]


def expert_weights(place, rows, out_grad, hidden, gate_low, up_low, shards):
    experts, total = rows.shape[:2]
    chunk = min(total, 1024)
    narrow = FF // shards
    spec = lambda width: pl.BlockSpec((1, chunk, width), lambda e, c, *_: (e, c, 0))
    return pl.pallas_call(
        functools.partial(expert_weights_kernel, shards),
        grid_spec=pltpu.PrefetchScalarGridSpec(
            num_scalar_prefetch=1,
            grid=(experts, total // chunk),
            in_specs=[spec(MODEL_WIDTH), spec(MODEL_WIDTH), spec(FF), spec(FF), spec(FF)],
            out_specs=[
                pl.BlockSpec((shards // 2, 1, narrow, FF), lambda e, c, *_: (0, e, 0, 0))
            ]
            * 12,
            scratch_shapes=[
                pltpu.VMEM((MODEL_WIDTH, FF), f32),
                pltpu.VMEM((MODEL_WIDTH, FF), f32),
                pltpu.VMEM((FF, MODEL_WIDTH), f32),
            ],
        ),
        out_shape=[jax.ShapeDtypeStruct((shards // 2, experts, narrow, FF), bf16)] * 12,
        cost_estimate=cost(
            6 * experts * total * MODEL_WIDTH * FF,
            experts * (total * (2 * MODEL_WIDTH + 3 * FF) + 3 * MODEL_WIDTH * FF) * 2,
        ),
        compiler_params=pltpu.CompilerParams(vmem_limit_bytes=VMEM_LIMIT),
        name="expert_weights",
    )(place, rows, out_grad, hidden, gate_low, up_low)


def along_seq(value, distance, shards):
    return lax.ppermute(value, "seq", [(i, i ^ distance) for i in range(shards)])


def gather_over_seq(value, shards):
    me = lax.axis_index("seq")
    held = jnp.stack([value] + [along_seq(value, k, shards) for k in range(1, shards)])
    return jnp.stack(
        [lax.dynamic_index_in_dim(held, s ^ me, 0, keepdims=False) for s in range(shards)]
    )


def sum_over_seq(value, shards):
    me = lax.axis_index("seq")
    part = lambda j: lax.dynamic_index_in_dim(value, j ^ me, 0, keepdims=False)
    sent = along_seq(jnp.stack([part(1), part(3)]), 1, shards).astype(f32)
    passed = (part(2).astype(f32) + sent[1]).astype(value.dtype)
    return part(0).astype(f32) + sent[0] + along_seq(passed, 2, shards).astype(f32)


def swap_over(value, axes):
    return lax.all_to_all(value, axes, split_axis=0, concat_axis=0, tiled=True)


def after(value, *others):
    return lax.optimization_barrier((value,) + others)[0]


def on_device(
    shards,
    ranks,
    layer_input,
    doc_ids,
    expert_routes,
    attn_gain,
    query_weight,
    key_projection_weight,
    value_projection_weight,
    out_weight,
    ffn_gain,
    router_weight,
    gate_weight,
    up_weight,
    down_weight,
    out_cotangent,
):
    local = layer_input.shape[0]
    tokens = doc_ids.shape[1]
    copies = ranks // KEY_VALUE_HEADS
    experts = gate_weight.shape[0]
    rows = query_weight.shape[0]
    blocks = tokens // BLOCK
    rank = lax.axis_index("exp")
    me = lax.axis_index("seq")
    head_width = GROUP * HEAD_SIZE
    wide, narrow, half = MODEL_WIDTH // shards, FF // shards, MODEL_WIDTH // 2

    x_row = lax.all_gather(layer_input, "exp", axis=0, tiled=True)

    by_head = jnp.concatenate(
        [
            query_weight.reshape(rows, KEY_VALUE_HEADS, head_width),
            key_projection_weight.reshape(rows, KEY_VALUE_HEADS, HEAD_SIZE),
            value_projection_weight.reshape(rows, KEY_VALUE_HEADS, HEAD_SIZE),
        ],
        axis=2,
    )
    own_width = by_head.shape[2]
    per_row = local * TOPK // rows
    small = jnp.concatenate(
        [
            router_weight,
            attn_gain[:, None],
            ffn_gain[:, None],
            jnp.zeros((rows, -(EXPERTS + 2 + per_row) % LANES), bf16),
            expert_routes.astype(bf16).reshape(rows, per_row),
        ],
        axis=1,
    )
    to_send = jnp.concatenate(
        [
            jnp.repeat(by_head.transpose(1, 0, 2), copies, axis=0),
            jnp.broadcast_to(small[None], (ranks,) + small.shape),
        ],
        axis=2,
    )
    got = swap_over(to_send, "exp").reshape(ranks * rows, -1)
    routes_row = got[:, got.shape[1] - per_row :].reshape(tokens, TOPK)
    routes_row = routes_row.astype(jnp.int32)
    weights = gather_over_seq(got[:, : own_width + LANES], shards).reshape(MODEL_WIDTH, -1)
    own_weight = weights[:, :own_width]
    small_all = weights[:, own_width:]
    gain_one = small_all[:, EXPERTS].astype(f32)[None]
    gain_two = small_all[:, EXPERTS + 1].astype(f32)[None]
    lane = jnp.arange(LANES)[None, :]
    router_mat = jnp.where(lane < EXPERTS, small_all, 0)
    key_part = own_weight[:, head_width : head_width + HEAD_SIZE]
    value_part = own_weight[:, head_width + HEAD_SIZE :]
    wide_weight = jnp.concatenate(
        [own_weight[:, :head_width]] + [key_part] * GROUP + [value_part] * GROUP, axis=1
    )

    left_weight, right_weight = down_weight[:, :, :half], down_weight[:, :, half:]
    near_gate, near_up = along_seq(gate_weight, 1, shards), along_seq(up_weight, 2, shards)

    seg_row = doc_ids[0]
    smaller = jnp.sum(
        (seg_row[None, :] < jnp.arange(DOCS, dtype=jnp.int32)[:, None]).astype(jnp.int32), axis=1
    )
    start = jnp.sum(
        jnp.where(seg_row[None, :] == jnp.arange(DOCS)[:, None], smaller[:, None], 0), axis=0
    ).astype(jnp.int32)
    positions = (jnp.arange(tokens, dtype=jnp.int32) - start).astype(f32)
    half_head = HEAD_SIZE // 2
    inv_freq = rope_base ** (-2.0 * jnp.arange(half_head, dtype=f32) / HEAD_SIZE)
    angles = positions[:, None] * inv_freq[None, :]
    cos_half, sin_half = jnp.cos(angles), jnp.sin(angles)
    cosine = jnp.concatenate([cos_half] * (2 * GROUP), axis=1)
    sine = jnp.concatenate([-sin_half, sin_half] * GROUP, axis=1)
    first_block = start[::BLOCK] // BLOCK
    start_blocks = start.reshape(blocks, 1, BLOCK)

    first_expert = rank * experts
    own_ids = first_expert + jnp.arange(experts, dtype=jnp.int32)
    own_member = jnp.any(routes_row.T[None] == own_ids[:, None, None], axis=1)
    own_member = own_member.reshape(experts, blocks, BLOCK)
    triangle = (jnp.arange(BLOCK)[:, None] <= jnp.arange(BLOCK)[None, :]).astype(bf16)
    counts = jnp.dot(
        own_member.reshape(experts * blocks, BLOCK).astype(bf16),
        triangle,
        preferred_element_type=f32,
    ).reshape(experts, blocks, BLOCK)
    slots = jnp.where(own_member, counts.astype(jnp.int32) - 1, -1)
    group = 2
    slot_rows = (
        slots.reshape(experts, blocks // group, group, BLOCK)
        .transpose(1, 0, 2, 3)
        .reshape(blocks // group, experts * group, BLOCK)
    )
    slot_cols = jnp.pad(
        slots.reshape(experts, tokens).T, ((0, 0), (0, LANES - experts)), constant_values=-1
    )
    place = jnp.stack([first_expert, me])

    x_row, near_gate, near_up = lax.optimization_barrier((x_row, near_gate, near_up))
    cot_a = lax.all_gather(after(out_cotangent[:COT_EARLY], got), "exp", axis=0, tiled=True)
    out_rows = lax.all_gather(after(out_weight, got), "exp", axis=0, tiled=True)
    x_row, out_rows = lax.optimization_barrier((x_row, out_rows))
    left_weight, right_weight = lax.optimization_barrier((left_weight, right_weight, near_gate))[:2]
    near_left, near_right = along_seq(left_weight, 1, shards), along_seq(right_weight, 2, shards)
    next_left, next_right = along_seq(left_weight, 2, shards), along_seq(right_weight, 1, shards)

    normed_row, query_low, key_low, value_low, mixed_own, mixed_t, log_total = attention_forward(
        first_block, x_row, wide_weight, gain_one, cosine, sine, start_blocks
    )
    share = tokens // copies
    part = lax.rem(rank, copies) * share
    (
        mixed_own,
        cot_a,
        near_left,
        near_right,
        next_left,
        next_right,
    ) = lax.optimization_barrier(
        (mixed_own, cot_a, near_left, near_right, next_left, next_right)
    )
    mixed_part = lax.dynamic_slice_in_dim(mixed_own, part, share) if copies > 1 else mixed_own
    mixed_row = lax.all_gather(mixed_part, "exp", axis=0, tiled=True)
    cot_b = lax.all_gather(
        after(out_cotangent[COT_EARLY:], mixed_own), "exp", axis=0, tiled=True
    )
    out_mat = gather_over_seq(after(out_rows, mixed_own), shards).reshape(MODEL_WIDTH, -1)
    gate_weight, up_weight = lax.optimization_barrier((gate_weight, up_weight, near_left))[:2]
    next_gate, next_up = along_seq(gate_weight, 2, shards), along_seq(up_weight, 1, shards)
    far_left = along_seq(after(near_left, mixed_own), 2, shards)
    far_right = along_seq(after(near_right, mixed_own), 1, shards)
    mixed_row, out_mat, next_gate, next_up, far_left, far_right = lax.optimization_barrier(
        (mixed_row, out_mat, next_gate, next_up, far_left, far_right)
    )
    far_gate = along_seq(after(near_gate, next_gate), 2, shards)
    far_up = along_seq(after(near_up, next_up), 1, shards)
    mixed_row = mixed_row.reshape(KEY_VALUE_HEADS, tokens, head_width)
    (
        normed_two_row,
        probs_row,
        probs_t,
        middle,
        mixed_home,
        normed_two_home,
        probs_home,
    ) = middle_forward(rank[None], mixed_row, x_row, out_mat, gain_two, router_mat, routes_row)
    normed_two_row, far_gate, far_up = lax.optimization_barrier((normed_two_row, far_gate, far_up))
    weight_all = lax.all_gather(
        (lambda w: lax.dynamic_slice_in_dim(w, lax.rem(rank, copies) * (MODEL_WIDTH // copies), MODEL_WIDTH // copies) if copies > 1 else w)(
            after(own_weight, normed_two_row)
        ),
        "exp",
        axis=0,
        tiled=True,
    ).reshape(KEY_VALUE_HEADS, MODEL_WIDTH, own_width)

    moe_part, row_part, weigh, *kept = expert_rows(
        place,
        normed_two_row,
        cot_a,
        cot_b,
        probs_row,
        probs_t,
        slot_rows,
        slot_cols,
        [gate_weight, near_gate, next_gate, far_gate]
        + [up_weight, next_up, near_up, far_up]
        + [left_weight, near_left, next_left, far_left]
        + [right_weight, next_right, near_right, far_right],
        group,
    )
    row_part, weight_all = lax.optimization_barrier((row_part, weight_all))
    row_sum = lax.psum_scatter(row_part, "exp", scatter_dimension=0, tiled=True)
    weigh_home = swap_over(
        weigh.reshape(blocks // group, experts, group, BLOCK)
        .transpose(0, 2, 1, 3)
        .reshape(ranks, experts, local),
        "exp",
    )
    weigh_home = weigh_home.reshape(EXPERTS, local).T
    pieces = expert_weights(place, *kept, shards)
    stay, go = pieces[0::2], pieces[1::2]
    *go, weigh_home = lax.optimization_barrier((*go, weigh_home))

    def first_exchange(piece, since):
        a, b = go[piece], go[3 + piece]
        if since is not None:
            a, b = after(a, since), after(b, since)
        return along_seq(a, 1, shards), along_seq(b, 2, shards)

    come_0 = first_exchange(0, None)
    row_sum, come_0 = lax.optimization_barrier((after(row_sum, go[0]), come_0))
    come_1 = first_exchange(1, row_sum)

    out_grad = out_cotangent.astype(f32)
    probs_own = probs_home[:, :EXPERTS]
    logits_low = (
        weigh_home - probs_own * jnp.sum(weigh_home, axis=1, keepdims=True)
    ).astype(bf16)
    router_part = dot_tn(normed_two_home, logits_low)
    normed_two_grad = row_sum.astype(f32) + dot_nt(logits_low, router_mat[:, :EXPERTS])
    scale_two = lax.rsqrt(jnp.mean(middle * middle, axis=-1, keepdims=True) + eps_norm)
    gain_two_part = jnp.sum(normed_two_grad * middle * scale_two, axis=0)
    through = gain_two * normed_two_grad
    middle_grad = (
        out_grad
        + scale_two * through
        - middle * scale_two**3 * jnp.mean(middle * through, axis=-1, keepdims=True)
    )
    branch_low = middle_grad.astype(bf16)
    mixed_grad = dot_nt(branch_low, out_mat).astype(bf16)
    mixed_grad_row = swap_over(
        jnp.repeat(
            mixed_grad.reshape(local, KEY_VALUE_HEADS, head_width).transpose(1, 0, 2), copies, axis=0
        ),
        "exp",
    ).reshape(tokens, head_width)

    out_part = dot_tn(mixed_home, branch_low).astype(bf16)
    out_part = out_part.reshape(shards, ranks, rows, MODEL_WIDTH).transpose(1, 0, 2, 3)
    out_part = lax.psum_scatter(
        out_part.reshape(MODEL_WIDTH, MODEL_WIDTH), "exp", scatter_dimension=0, tiled=True
    )
    moe_sum = lax.psum_scatter(
        after(moe_part, mixed_grad_row), "exp", scatter_dimension=0, tiled=True
    )

    mixed_grad_row, come_1 = lax.optimization_barrier((mixed_grad_row, come_1))
    come_2 = first_exchange(2, mixed_grad_row)

    lin_low = attention_backward(
        first_block,
        query_low,
        mixed_grad_row,
        mixed_t,
        log_total,
        start_blocks,
        cosine,
        sine,
        key_low,
        value_low,
    )
    lin_low, come_2, out_part = lax.optimization_barrier((lin_low, come_2, out_part))

    come = (come_0, come_1, come_2)
    halves = []
    for side, step in ((0, 2), (1, 1)):
        mine = [
            stay[3 * side + n].astype(f32) + come[n][side].astype(f32) for n in range(3)
        ]
        passed = along_seq(jnp.stack([m[1].astype(bf16) for m in mine]), step, shards)
        halves.append([m[0] + passed[n].astype(f32) for n, m in enumerate(mine)])
    gate_grad, up_grad = (jnp.concatenate(h[:2], axis=1) for h in halves)
    down_grad = jnp.concatenate([halves[0][2], halves[1][2]], axis=2)
    out_weight_grad = sum_over_seq(out_part.reshape(shards, rows, MODEL_WIDTH), shards)
    lin_home = swap_over(lin_low.reshape(ranks, local, own_width), "exp")
    own_rows = lax.dynamic_slice_in_dim(normed_row, part, share) if copies > 1 else normed_row
    own_lin = lax.dynamic_slice_in_dim(lin_low, part, share) if copies > 1 else lin_low
    weight_part = dot_tn(own_rows, own_lin)
    weight_part = jnp.concatenate(
        [
            weight_part,
            router_part,
            gain_two_part[:, None],
            jnp.zeros((MODEL_WIDTH, LANES - EXPERTS - 1), f32),
        ],
        axis=1,
    ).astype(bf16)
    weight_sum = sum_over_seq(weight_part.reshape(shards, ranks * rows, -1), shards).astype(bf16)
    weight_sum, lin_home = lax.optimization_barrier((weight_sum, lin_home))
    weight_home = swap_over(weight_sum.reshape(ranks, rows, -1), "exp").astype(f32)
    tail = jnp.sum(weight_home[:, :, own_width:], axis=0)
    router_grad = tail[:, :EXPERTS]
    ffn_gain_grad = tail[:, EXPERTS]
    weight_home = jnp.sum(
        weight_home[:, :, :own_width].reshape(KEY_VALUE_HEADS, copies, rows, own_width), axis=1
    ).transpose(1, 0, 2)
    lin_home = lin_home.reshape(KEY_VALUE_HEADS, copies, local, own_width)[:, 0]
    normed_grad = sum(dot_nt(lin_home[h], weight_all[h]) for h in range(KEY_VALUE_HEADS))
    inputs = layer_input.astype(f32)
    scale_one = lax.rsqrt(jnp.mean(inputs * inputs, axis=-1, keepdims=True) + eps_norm)
    through_one = gain_one * normed_grad
    input_grad = (
        middle_grad
        + scale_one * through_one
        - inputs * scale_one**3 * jnp.mean(inputs * through_one, axis=-1, keepdims=True)
    )

    query_grad = weight_home[:, :, :head_width].reshape(rows, -1)
    key_grad = weight_home[:, :, head_width : head_width + HEAD_SIZE].reshape(rows, -1)
    value_grad = weight_home[:, :, head_width + HEAD_SIZE :].reshape(rows, -1)
    attn_gain_grad = jnp.sum(weight_home * by_head.astype(f32), axis=(1, 2)) / attn_gain.astype(f32)

    layer_output = (middle + moe_sum.astype(f32)).astype(bf16)
    return (
        layer_output,
        input_grad,
        attn_gain_grad,
        query_grad,
        key_grad,
        value_grad,
        out_weight_grad,
        ffn_gain_grad,
        router_grad,
        gate_grad,
        up_grad,
        down_grad,
    )


def solution(mesh):
    tokens_2d = P(("seq", "exp"), None)
    vector = P(("seq", "exp"))
    expert = P("exp", "seq", None)
    return jax.shard_map(
        functools.partial(on_device, mesh.shape["seq"], mesh.shape["exp"]),
        mesh=mesh,
        in_specs=(
            tokens_2d,
            P("seq", None),
            tokens_2d,
            vector,
            tokens_2d,
            tokens_2d,
            tokens_2d,
            tokens_2d,
            vector,
            tokens_2d,
            expert,
            expert,
            expert,
            tokens_2d,
        ),
        out_specs=(
            tokens_2d,
            tokens_2d,
            vector,
            tokens_2d,
            tokens_2d,
            tokens_2d,
            tokens_2d,
            vector,
            tokens_2d,
            expert,
            expert,
            expert,
        ),
        check_vma=False,
    )
```

```python
import functools

import jax
import jax.numpy as jnp
from jax import lax
from jax.experimental import pallas as pl
from jax.experimental.pallas import tpu as pltpu
from jax.sharding import PartitionSpec as P

MODEL_WIDTH = 1024
QUERY_HEADS = 16
KEY_VALUE_HEADS = 8
HEAD_SIZE = 64
FF = 512
EXPERTS = 32
TOPK = 8
DOCS = 4
CAP = 128

BLOCK = 256
COT_EARLY = 96
MID = 512
SUB = 256
LANES = 128
GROUP = QUERY_HEADS // KEY_VALUE_HEADS
PACK = GROUP * HEAD_SIZE

eps_norm = 1e-06
rope_base = 10000.0
score_masked = -1e30
score_scale = HEAD_SIZE**-0.5
f32 = jnp.float32
bf16 = jnp.bfloat16
VMEM_LIMIT = 60 * 1024 * 1024


def dot_nn(a, b):
    return lax.dot_general(a, b, (((1,), (0,)), ((), ())), preferred_element_type=f32)


def dot_nt(a, b):
    return lax.dot_general(a, b, (((1,), (1,)), ((), ())), preferred_element_type=f32)


def dot_tn(a, b):
    return lax.dot_general(a, b, (((0,), (0,)), ((), ())), preferred_element_type=f32)


def swap_halves(v):
    lane = lax.broadcasted_iota(jnp.int32, v.shape, 1)
    half = HEAD_SIZE // 2
    return jnp.where(
        lane % HEAD_SIZE < half, pltpu.roll(v, PACK - half, 1), pltpu.roll(v, half, 1)
    )


def head_stack(v):
    lane = lax.broadcasted_iota(jnp.int32, v.shape, 1)
    zero = jnp.zeros_like(v)
    return jnp.concatenate(
        [jnp.where(lane < HEAD_SIZE, v, zero), jnp.where(lane >= HEAD_SIZE, v, zero)], axis=0
    )


def visible_from(block_key, block_query, start_row):
    shape = (BLOCK, GROUP * BLOCK)
    key_place = block_key * BLOCK + lax.broadcasted_iota(jnp.int32, shape, 0)
    lane = lax.broadcasted_iota(jnp.int32, shape, 1)
    query_place = block_query * BLOCK + lane % BLOCK
    return (key_place >= start_row) & (key_place <= query_place)


def attention_forward_kernel(
    first_block,
    x_ref,
    weight_ref,
    gain_ref,
    cos_ref,
    sin_ref,
    start_ref,
    normed_ref,
    query_ref,
    key_ref,
    value_ref,
    mixed_ref,
    mixed_t_ref,
    log_ref,
    key_all,
    value_all,
):
    i = pl.program_id(0)
    x = x_ref[...].astype(f32)
    normed = (
        x * lax.rsqrt(jnp.mean(x * x, axis=-1, keepdims=True) + eps_norm) * gain_ref[...]
    ).astype(bf16)
    normed_ref[...] = normed
    lin = dot_nn(normed, weight_ref[...])
    cosine, sine = cos_ref[...], sin_ref[...]
    query_lin, key_lin = lin[:, :PACK], lin[:, PACK : 2 * PACK]
    query = (query_lin * cosine + swap_halves(query_lin) * sine).astype(bf16)
    key = (key_lin * cosine + swap_halves(key_lin) * sine).astype(bf16)
    value = lin[:, 2 * PACK :].astype(bf16)
    query_ref[...] = query
    key_ref[...] = key
    value_ref[...] = value
    rows = pl.ds(pl.multiple_of(i * BLOCK, BLOCK), BLOCK)
    key_all[rows, :] = key
    value_all[rows, :] = value
    query_two = head_stack(query * jnp.asarray(score_scale, bf16))
    start_row = start_ref[0]
    start_two = jnp.concatenate([start_row] * GROUP, axis=1)

    def visit(j, carry):
        run_max, run_sum, acc = carry
        here = pl.ds(pl.multiple_of(j * BLOCK, BLOCK), BLOCK)
        scores = dot_nt(key_all[here, :], query_two)
        scores = jnp.where(visible_from(j, i, start_two), scores, score_masked)
        new_max = jnp.maximum(run_max, jnp.max(scores, axis=0, keepdims=True))
        shrink = jnp.exp(run_max - new_max)
        weights = jnp.exp(scores - new_max)
        run_sum = run_sum * shrink + jnp.sum(weights, axis=0, keepdims=True)
        acc = acc * shrink + dot_tn(value_all[here, :], weights.astype(bf16))
        return new_max, run_sum, acc

    width = GROUP * BLOCK
    run_max, run_sum, acc = lax.fori_loop(
        first_block[i],
        i + 1,
        visit,
        (
            jnp.full((1, width), score_masked, f32),
            jnp.zeros((1, width), f32),
            jnp.zeros((PACK, width), f32),
        ),
    )
    acc = acc * (1.0 / run_sum)
    mixed_t = jnp.concatenate([acc[:HEAD_SIZE, :BLOCK], acc[HEAD_SIZE:, BLOCK:]], axis=0)
    mixed_t_ref[0] = mixed_t
    mixed_ref[...] = mixed_t.T.astype(bf16)
    log_ref[0] = run_max + jnp.log(run_sum)


def attention_forward(first_block, x_row, weight, gain, cosine, sine, start):
    tokens = x_row.shape[0]
    blocks = tokens // BLOCK
    row = lambda i, *_: (i, 0)
    page = lambda i, *_: (i, 0, 0)
    whole = lambda i, *_: (0, 0)
    return pl.pallas_call(
        attention_forward_kernel,
        grid_spec=pltpu.PrefetchScalarGridSpec(
            num_scalar_prefetch=1,
            grid=(blocks,),
            in_specs=[
                pl.BlockSpec((BLOCK, MODEL_WIDTH), row),
                pl.BlockSpec(weight.shape, whole),
                pl.BlockSpec((1, MODEL_WIDTH), whole),
                pl.BlockSpec((BLOCK, PACK), row),
                pl.BlockSpec((BLOCK, PACK), row),
                pl.BlockSpec((1, 1, BLOCK), page),
            ],
            out_specs=[
                pl.BlockSpec((BLOCK, MODEL_WIDTH), row),
                pl.BlockSpec((BLOCK, PACK), row),
                pl.BlockSpec((BLOCK, PACK), row),
                pl.BlockSpec((BLOCK, PACK), row),
                pl.BlockSpec((BLOCK, PACK), row),
                pl.BlockSpec((1, PACK, BLOCK), page),
                pl.BlockSpec((1, 1, GROUP * BLOCK), page),
            ],
            scratch_shapes=[pltpu.VMEM((tokens, PACK), bf16), pltpu.VMEM((tokens, PACK), bf16)],
        ),
        out_shape=[
            jax.ShapeDtypeStruct((tokens, MODEL_WIDTH), bf16),
            jax.ShapeDtypeStruct((tokens, PACK), bf16),
            jax.ShapeDtypeStruct((tokens, PACK), bf16),
            jax.ShapeDtypeStruct((tokens, PACK), bf16),
            jax.ShapeDtypeStruct((tokens, PACK), bf16),
            jax.ShapeDtypeStruct((blocks, PACK, BLOCK), f32),
            jax.ShapeDtypeStruct((blocks, 1, GROUP * BLOCK), f32),
        ],
        cost_estimate=cost(
            tokens * (2 * MODEL_WIDTH * 3 * PACK + 8 * PACK * tokens), tokens * MODEL_WIDTH * 4
        ),
        compiler_params=pltpu.CompilerParams(vmem_limit_bytes=VMEM_LIMIT),
        name="attention_forward",
    )(first_block, x_row, weight, gain, cosine, sine, start)


def attention_backward_kernel(
    shards,
    copies,
    first_block,
    place,
    query_ref,
    grad_ref,
    mixed_t_ref,
    log_ref,
    start_ref,
    cos_ref,
    sin_ref,
    key_ref,
    value_ref,
    small_ref,
    *refs,
):
    normed_refs, (lin_grad_ref, stay_ref, go_ref, key_acc, value_acc) = refs[:shards], refs[shards:]
    i = pl.program_id(0)
    blocks = pl.num_programs(0)

    @pl.when(i == 0)
    def _():
        key_acc[...] = jnp.zeros_like(key_acc)
        value_acc[...] = jnp.zeros_like(value_acc)

    query_two = head_stack(query_ref[...] * jnp.asarray(score_scale, bf16))
    grad = grad_ref[...]
    grad_two = head_stack(grad)
    product = mixed_t_ref[0] * grad.astype(f32).T
    delta = jnp.concatenate(
        [
            jnp.sum(product[:HEAD_SIZE], axis=0, keepdims=True),
            jnp.sum(product[HEAD_SIZE:], axis=0, keepdims=True),
        ],
        axis=1,
    )
    log_total = log_ref[0]
    start_two = jnp.concatenate([start_ref[0]] * GROUP, axis=1)

    def visit(j, query_acc):
        here = pl.ds(pl.multiple_of(j * BLOCK, BLOCK), BLOCK)
        key = key_ref[here, :]
        scores = dot_nt(key, query_two)
        probs = jnp.where(visible_from(j, i, start_two), jnp.exp(scores - log_total), 0.0)
        prob_grad = dot_nt(value_ref[here, :], grad_two)
        score_grad = (probs * (prob_grad - delta)).astype(bf16)
        value_acc[here, :] += dot_nn(probs.astype(bf16), grad_two)
        key_acc[here, :] += dot_nn(score_grad, query_two)
        return query_acc + dot_tn(score_grad, key)

    query_acc = lax.fori_loop(
        first_block[i], i + 1, visit, jnp.zeros((GROUP * BLOCK, PACK), f32)
    )
    lane = lax.broadcasted_iota(jnp.int32, (BLOCK, PACK), 1)
    rotated = jnp.where(lane < HEAD_SIZE, query_acc[:BLOCK], query_acc[BLOCK:]) * score_scale
    rows = pl.ds(pl.multiple_of(i * BLOCK, BLOCK), BLOCK)
    lin_grad_ref[rows, :PACK] = (
        rotated * cos_ref[rows, :] - swap_halves(rotated) * sin_ref[rows, :]
    ).astype(bf16)

    @pl.when(i == blocks - 1)
    def _():
        def finish(b, carry):
            here = pl.ds(pl.multiple_of(b * BLOCK, BLOCK), BLOCK)
            key_sum = key_acc[here, :]
            key_sum = key_sum + pltpu.roll(key_sum, HEAD_SIZE, 1)
            value_sum = value_acc[here, :]
            value_sum = value_sum + pltpu.roll(value_sum, HEAD_SIZE, 1)
            key_lin = key_sum * cos_ref[here, :] - swap_halves(key_sum) * sin_ref[here, :]
            lin_grad_ref[here, PACK:] = jnp.where(lane < HEAD_SIZE, key_lin, value_sum).astype(bf16)
            return carry

        lax.fori_loop(0, blocks, finish, 0)
        share = lin_grad_ref.shape[0] // copies
        own = lin_grad_ref[pl.ds(pl.multiple_of(place[1] * share, share), share), :]
        wide = MODEL_WIDTH // shards
        for n, j in enumerate(exchange_order(shards, 0)):
            out = (stay_ref, go_ref)[n // (shards // 2)]
            at = n % (shards // 2)
            out[at, :, : 2 * PACK] = dot_tn(normed_refs[n][...], own).astype(bf16)
            rows = pl.ds(pl.multiple_of((j ^ place[0]) * wide, wide), wide)
            out[at, :, 2 * PACK :] = small_ref[rows, :].astype(bf16)


def attention_backward(
    first_block,
    place,
    query,
    grad,
    mixed_t,
    log_total,
    start,
    cosine,
    sine,
    key,
    value,
    small,
    normed,
    shards,
    copies,
):
    tokens = query.shape[0]
    wide = MODEL_WIDTH // shards
    part = lambda j: pl.BlockSpec(
        (tokens // copies, wide), lambda i, first, place, j=j: (place[1], j ^ place[0])
    )
    out = (shards // 2, wide, 2 * PACK + LANES)
    blocks = tokens // BLOCK
    row = lambda i, *_: (i, 0)
    page = lambda i, *_: (i, 0, 0)
    whole = lambda i, *_: (0, 0)
    return pl.pallas_call(
        functools.partial(attention_backward_kernel, shards, copies),
        grid_spec=pltpu.PrefetchScalarGridSpec(
            num_scalar_prefetch=2,
            grid=(blocks,),
            in_specs=[
                pl.BlockSpec((BLOCK, PACK), row),
                pl.BlockSpec((BLOCK, PACK), row),
                pl.BlockSpec((1, PACK, BLOCK), page),
                pl.BlockSpec((1, 1, GROUP * BLOCK), page),
                pl.BlockSpec((1, 1, BLOCK), page),
                pl.BlockSpec((tokens, PACK), whole),
                pl.BlockSpec((tokens, PACK), whole),
                pl.BlockSpec((tokens, PACK), whole),
                pl.BlockSpec((tokens, PACK), whole),
                pl.BlockSpec((MODEL_WIDTH, LANES), whole),
            ]
            + [part(j) for j in exchange_order(shards, 0)],
            out_specs=[
                pl.BlockSpec((tokens, 2 * PACK), whole),
                pl.BlockSpec(out, lambda i, *_: (0, 0, 0)),
                pl.BlockSpec(out, lambda i, *_: (0, 0, 0)),
            ],
            scratch_shapes=[pltpu.VMEM((tokens, PACK), f32), pltpu.VMEM((tokens, PACK), f32)],
        ),
        out_shape=[
            jax.ShapeDtypeStruct((tokens, 2 * PACK), bf16),
            jax.ShapeDtypeStruct(out, bf16),
            jax.ShapeDtypeStruct(out, bf16),
        ],
        cost_estimate=cost(20 * tokens * tokens * PACK, tokens * PACK * 28),
        compiler_params=pltpu.CompilerParams(vmem_limit_bytes=VMEM_LIMIT),
        name="attention_backward",
    )(
        first_block,
        place,
        query,
        grad,
        mixed_t,
        log_total,
        start,
        cosine,
        sine,
        key,
        value,
        small,
        *([normed] * shards),
    )


def middle_kernel(
    home,
    mixed_ref,
    x_ref,
    weight_ref,
    gain_ref,
    router_ref,
    routes_ref,
    normed_ref,
    probs_ref,
    probs_t_ref,
    home_middle_ref,
    home_mixed_ref,
    home_normed_ref,
    home_probs_ref,
    keep_middle,
    keep_mixed,
):
    i = pl.program_id(0)
    parts = x_ref.shape[0] // SUB
    lane = lax.broadcasted_iota(jnp.int32, (SUB, LANES), 1)
    for n in range(parts):
        here = slice(n * SUB, (n + 1) * SUB)
        mixed = jnp.concatenate([mixed_ref[h, here] for h in range(KEY_VALUE_HEADS)], axis=1)
        middle = x_ref[here].astype(f32) + dot_nn(mixed, weight_ref[...])
        normed = (
            middle
            * lax.rsqrt(jnp.mean(middle * middle, axis=-1, keepdims=True) + eps_norm)
            * gain_ref[...]
        ).astype(bf16)
        normed_ref[here] = normed
        logits = dot_nn(normed, router_ref[...])
        routes = routes_ref[here]
        member = jnp.zeros_like(logits)
        for k in range(TOPK):
            member = jnp.where(lane == routes[:, k : k + 1], 1.0, member)
        chosen = jnp.where(member > 0, logits, score_masked)
        raised = jnp.exp(chosen - jnp.max(chosen, axis=-1, keepdims=True)) * member
        probs = raised / jnp.sum(raised, axis=-1, keepdims=True)
        probs_ref[here] = probs
        probs_t_ref[:, here] = probs.T[:EXPERTS]
        keep_middle[here] = middle
        keep_mixed[here] = mixed

    @pl.when(i == home[0] * BLOCK // x_ref.shape[0])
    def _():
        at = pl.ds(pl.multiple_of(home[0] * BLOCK % x_ref.shape[0], BLOCK), BLOCK)
        home_middle_ref[...] = keep_middle[at]
        home_mixed_ref[...] = keep_mixed[at]
        home_normed_ref[...] = normed_ref[at]
        home_probs_ref[...] = probs_ref[at]


def middle_forward(home, mixed, x_row, weight, gain, router, routes):
    tokens = x_row.shape[0]
    row = lambda i, *_: (i, 0)
    whole = lambda i, *_: (0, 0)
    return pl.pallas_call(
        middle_kernel,
        grid_spec=pltpu.PrefetchScalarGridSpec(
            num_scalar_prefetch=1,
            grid=(tokens // MID,),
            in_specs=[
                pl.BlockSpec((KEY_VALUE_HEADS, MID, PACK), lambda i, *_: (0, i, 0)),
                pl.BlockSpec((MID, MODEL_WIDTH), row),
                pl.BlockSpec((MODEL_WIDTH, MODEL_WIDTH), whole),
                pl.BlockSpec((1, MODEL_WIDTH), whole),
                pl.BlockSpec((MODEL_WIDTH, LANES), whole),
                pl.BlockSpec((MID, TOPK), row),
            ],
            out_specs=[
                pl.BlockSpec((MID, MODEL_WIDTH), row),
                pl.BlockSpec((MID, LANES), row),
                pl.BlockSpec((EXPERTS, MID), lambda i, *_: (0, i)),
                pl.BlockSpec((BLOCK, MODEL_WIDTH), whole),
                pl.BlockSpec((BLOCK, MODEL_WIDTH), whole),
                pl.BlockSpec((BLOCK, MODEL_WIDTH), whole),
                pl.BlockSpec((BLOCK, LANES), whole),
            ],
            scratch_shapes=[
                pltpu.VMEM((MID, MODEL_WIDTH), f32),
                pltpu.VMEM((MID, MODEL_WIDTH), bf16),
            ],
        ),
        out_shape=[
            jax.ShapeDtypeStruct((tokens, MODEL_WIDTH), bf16),
            jax.ShapeDtypeStruct((tokens, LANES), f32),
            jax.ShapeDtypeStruct((EXPERTS, tokens), f32),
            jax.ShapeDtypeStruct((BLOCK, MODEL_WIDTH), f32),
            jax.ShapeDtypeStruct((BLOCK, MODEL_WIDTH), bf16),
            jax.ShapeDtypeStruct((BLOCK, MODEL_WIDTH), bf16),
            jax.ShapeDtypeStruct((BLOCK, LANES), f32),
        ],
        cost_estimate=cost(
            2 * tokens * MODEL_WIDTH * (MODEL_WIDTH + LANES), tokens * MODEL_WIDTH * 6
        ),
        compiler_params=pltpu.CompilerParams(vmem_limit_bytes=VMEM_LIMIT),
        name="middle_forward",
    )(home, mixed, x_row, weight, gain, router, routes)


def cost(flops, moved):
    return pl.CostEstimate(flops=int(flops), transcendentals=0, bytes_accessed=int(moved))


def column_of(values, lane_wanted):
    lane = lax.broadcasted_iota(jnp.int32, values.shape, 1)
    return jnp.sum(
        jnp.where(lane == lane_wanted, values, jnp.zeros_like(values)), axis=-1, keepdims=True
    )


def expert_rows_kernel(shards, experts, group, place, *refs):
    normed_ref, cot_a_ref, cot_b_ref, probs_ref, probs_t_ref, slot_row_ref, slot_col_ref = refs[:7]
    weight_refs = [refs[7 + n * shards : 7 + (n + 1) * shards] for n in range(4)]
    (
        moe_ref,
        row_ref,
        weigh_ref,
        rows_ref,
        out_grad_ref,
        hidden_ref,
        gate_low_ref,
        up_low_ref,
        gate_all,
        up_all,
        down_all,
        out_all,
        back_all,
        sems,
    ) = refs[7 + 4 * shards :]
    first_expert, me = place[0], place[1]
    wide, narrow = MODEL_WIDTH // shards, FF // shards
    half = MODEL_WIDTH // 2

    def copies(e):
        made = []
        for j in range(shards):
            tall = pl.ds(pl.multiple_of((j ^ me) * wide, wide), wide)
            short = pl.ds(pl.multiple_of((j ^ me) * narrow, narrow), narrow)
            places = (
                gate_all.at[e, tall, :],
                up_all.at[e, tall, :],
                down_all.at[e, short, :half],
                down_all.at[e, short, half:],
            )
            for n in range(4):
                made.append(
                    pltpu.make_async_copy(weight_refs[n][j].at[e], places[n], sems.at[e, 4 * j + n])
                )
        return made

    @pl.when(pl.program_id(0) == 0)
    def _():
        for e in range(experts):
            for copy in copies(e):
                copy.start()

    slot_place = lax.broadcasted_iota(jnp.int32, (CAP, BLOCK), 0)
    slot_lane = lax.broadcasted_iota(jnp.int32, (BLOCK, CAP), 1)
    early, late = COT_EARLY, BLOCK - COT_EARLY
    cots = [
        jnp.concatenate(
            [
                cot_a_ref[b * early : (b + 1) * early, :],
                cot_b_ref[b * late : (b + 1) * late, :],
            ],
            axis=0,
        )
        for b in range(group)
    ]
    for e in range(experts):

        @pl.when(pl.program_id(0) == 0)
        def _():
            for copy in copies(e):
                copy.wait()

        picked, cot_picked = [], []
        hits = []
        for b in range(group):
            hit = slot_place == slot_row_ref[0, e * group + b : e * group + b + 1, :]
            hits.append(hit)
            pick = hit.astype(f32).astype(bf16)
            prob_row = probs_t_ref[pl.ds(first_expert + e, 1), b * BLOCK : (b + 1) * BLOCK]
            prob_slot = jnp.sum(jnp.where(hit, prob_row, 0.0), axis=-1, keepdims=True)
            picked.append(dot_nn(pick, normed_ref[b * BLOCK : (b + 1) * BLOCK, :]).astype(bf16))
            cot_picked.append((dot_nn(pick, cots[b]) * prob_slot).astype(bf16))
        rows = jnp.concatenate(picked, axis=0)
        out_grad = jnp.concatenate(cot_picked, axis=0)
        rows_ref[e] = rows
        out_grad_ref[e] = out_grad
        gate_pre = dot_nn(rows, gate_all[e])
        up_pre = dot_nn(rows, up_all[e])
        hidden_grad = dot_nt(out_grad, down_all[e])
        logistic = 1.0 / (1.0 + jnp.exp(-gate_pre))
        silu = gate_pre * logistic
        hidden = (silu * up_pre).astype(bf16)
        gate_low = (
            hidden_grad * up_pre * (logistic * (1.0 + gate_pre * (1.0 - logistic)))
        ).astype(bf16)
        up_low = (hidden_grad * silu).astype(bf16)
        hidden_ref[e] = hidden
        gate_low_ref[e] = gate_low
        up_low_ref[e] = up_low
        weigh = jnp.sum(hidden_grad * hidden.astype(f32), axis=-1, keepdims=True)
        out = dot_nn(hidden, down_all[e]).astype(bf16)
        row_grad = (dot_nt(gate_low, gate_all[e]) + dot_nt(up_low, up_all[e])).astype(bf16)
        for b in range(group):
            inside = slice(b * CAP, (b + 1) * CAP)
            out_all[b, e * CAP : (e + 1) * CAP, :] = out[inside]
            back_all[b, e * CAP : (e + 1) * CAP, :] = row_grad[inside]
            weigh_ref[0, e * group + b : e * group + b + 1, :] = jnp.sum(
                jnp.where(hits[b], weigh[inside], 0.0), axis=0, keepdims=True
            )
    for b in range(group):
        tokens = slice(b * BLOCK, (b + 1) * BLOCK)
        slot_cols, probs = slot_col_ref[tokens, :], probs_ref[tokens, :]
        plain, scaled = [], []
        for e in range(experts):
            hit = slot_lane == column_of(slot_cols, e)
            plain.append(hit.astype(f32).astype(bf16))
            scaled.append(jnp.where(hit, column_of(probs, first_expert + e), 0.0).astype(bf16))
        moe_ref[tokens, :] = dot_nn(jnp.concatenate(scaled, axis=1), out_all[b]).astype(bf16)
        row_ref[tokens, :] = dot_nn(jnp.concatenate(plain, axis=1), back_all[b]).astype(bf16)


def expert_rows(place, normed, cot_a, cot_b, probs, probs_t, slot_rows, slot_cols, weights, group):
    tokens = normed.shape[0]
    shards, experts = len(weights) // 4, weights[0].shape[0]
    span, slots = group * BLOCK, group * CAP
    steps = tokens // span
    row = lambda g, *_: (g, 0)
    page = lambda g, *_: (g, 0, 0)
    spread = lambda g, *_: (0, g, 0)
    total = tokens // BLOCK * CAP
    return pl.pallas_call(
        functools.partial(expert_rows_kernel, shards, experts, group),
        grid_spec=pltpu.PrefetchScalarGridSpec(
            num_scalar_prefetch=1,
            grid=(steps,),
            in_specs=[
                pl.BlockSpec((span, MODEL_WIDTH), row),
                pl.BlockSpec((group * COT_EARLY, MODEL_WIDTH), row),
                pl.BlockSpec((group * (BLOCK - COT_EARLY), MODEL_WIDTH), row),
                pl.BlockSpec((span, LANES), row),
                pl.BlockSpec((EXPERTS, span), lambda g, *_: (0, g)),
                pl.BlockSpec((1, experts * group, BLOCK), page),
                pl.BlockSpec((span, LANES), row),
            ]
            + [pl.BlockSpec(memory_space=pl.ANY)] * (4 * shards),
            out_specs=[
                pl.BlockSpec((span, MODEL_WIDTH), row),
                pl.BlockSpec((span, MODEL_WIDTH), row),
                pl.BlockSpec((1, experts * group, BLOCK), page),
                pl.BlockSpec((experts, slots, MODEL_WIDTH), spread),
                pl.BlockSpec((experts, slots, MODEL_WIDTH), spread),
                pl.BlockSpec((experts, slots, FF), spread),
                pl.BlockSpec((experts, slots, FF), spread),
                pl.BlockSpec((experts, slots, FF), spread),
            ],
            scratch_shapes=[
                pltpu.VMEM((experts, MODEL_WIDTH, FF), bf16),
                pltpu.VMEM((experts, MODEL_WIDTH, FF), bf16),
                pltpu.VMEM((experts, FF, MODEL_WIDTH), bf16),
                pltpu.VMEM((group, experts * CAP, MODEL_WIDTH), bf16),
                pltpu.VMEM((group, experts * CAP, MODEL_WIDTH), bf16),
                pltpu.SemaphoreType.DMA((experts, 4 * shards)),
            ],
        ),
        out_shape=[
            jax.ShapeDtypeStruct((tokens, MODEL_WIDTH), bf16),
            jax.ShapeDtypeStruct((tokens, MODEL_WIDTH), bf16),
            jax.ShapeDtypeStruct((steps, experts * group, BLOCK), f32),
            jax.ShapeDtypeStruct((experts, total, MODEL_WIDTH), bf16),
            jax.ShapeDtypeStruct((experts, total, MODEL_WIDTH), bf16),
            jax.ShapeDtypeStruct((experts, total, FF), bf16),
            jax.ShapeDtypeStruct((experts, total, FF), bf16),
            jax.ShapeDtypeStruct((experts, total, FF), bf16),
        ],
        cost_estimate=cost(
            12 * experts * total * MODEL_WIDTH * FF + 8 * experts * total * MODEL_WIDTH * BLOCK,
            experts * (3 * MODEL_WIDTH * FF + total * (2 * MODEL_WIDTH + 3 * FF)) * 2
            + tokens * MODEL_WIDTH * 8,
        ),
        compiler_params=pltpu.CompilerParams(vmem_limit_bytes=VMEM_LIMIT),
        name="expert_rows",
    )(place, normed, cot_a, cot_b, probs, probs_t, slot_rows, slot_cols, *weights)


def expert_weights_kernel(shards, place, *refs):
    rows_ref, out_grad_ref, hidden_ref, gate_low_ref, up_low_ref = refs[:5]
    outs, (gate_acc, up_acc, down_acc) = refs[5:17], refs[17:]
    me, c = place[1], pl.program_id(1)
    rows = rows_ref[0]
    for acc, left, right in (
        (gate_acc, rows, gate_low_ref[0]),
        (up_acc, rows, up_low_ref[0]),
        (down_acc, hidden_ref[0], out_grad_ref[0]),
    ):
        part = dot_tn(left, right)

        @pl.when(c == 0)
        def _():
            acc[...] = part

        @pl.when(c > 0)
        def _():
            acc[...] += part

    wide, narrow = MODEL_WIDTH // shards, FF // shards
    half = MODEL_WIDTH // 2

    @pl.when(c == pl.num_programs(1) - 1)
    def _():
        for side in range(2):
            square = (gate_acc, up_acc)[side]
            order = exchange_order(shards, side)
            for n, j in enumerate(order):
                kind, at = divmod(n, shards // 2)
                base = (j ^ me) * wide
                low = pl.ds(pl.multiple_of(base, narrow), narrow)
                high = pl.ds(pl.multiple_of(base + narrow, narrow), narrow)
                short = pl.ds(pl.multiple_of((j ^ me) * narrow, narrow), narrow)
                pieces = (
                    square[low, :],
                    square[high, :],
                    down_acc[short, side * half : (side + 1) * half],
                )
                for piece, value in enumerate(pieces):
                    outs[6 * side + 2 * piece + kind][at, 0] = value.astype(bf16)


def exchange_order(shards, side):
    first = (1, 2)[side]
    stay = [j for j in range(shards) if not j & first]
    return stay + [j ^ first for j in stay]


def expert_weights(place, rows, out_grad, hidden, gate_low, up_low, shards):
    experts, total = rows.shape[:2]
    chunk = min(total, 1024)
    narrow = FF // shards
    spec = lambda width: pl.BlockSpec((1, chunk, width), lambda e, c, *_: (e, c, 0))
    return pl.pallas_call(
        functools.partial(expert_weights_kernel, shards),
        grid_spec=pltpu.PrefetchScalarGridSpec(
            num_scalar_prefetch=1,
            grid=(experts, total // chunk),
            in_specs=[spec(MODEL_WIDTH), spec(MODEL_WIDTH), spec(FF), spec(FF), spec(FF)],
            out_specs=[
                pl.BlockSpec((shards // 2, 1, narrow, FF), lambda e, c, *_: (0, e, 0, 0))
            ]
            * 12,
            scratch_shapes=[
                pltpu.VMEM((MODEL_WIDTH, FF), f32),
                pltpu.VMEM((MODEL_WIDTH, FF), f32),
                pltpu.VMEM((FF, MODEL_WIDTH), f32),
            ],
        ),
        out_shape=[jax.ShapeDtypeStruct((shards // 2, experts, narrow, FF), bf16)] * 12,
        cost_estimate=cost(
            6 * experts * total * MODEL_WIDTH * FF,
            experts * (total * (2 * MODEL_WIDTH + 3 * FF) + 3 * MODEL_WIDTH * FF) * 2,
        ),
        compiler_params=pltpu.CompilerParams(vmem_limit_bytes=VMEM_LIMIT),
        name="expert_weights",
    )(place, rows, out_grad, hidden, gate_low, up_low)


def along_seq(value, distance, shards):
    return lax.ppermute(value, "seq", [(i, i ^ distance) for i in range(shards)])


def gather_over_seq(value, shards):
    me = lax.axis_index("seq")
    held = jnp.stack([value] + [along_seq(value, k, shards) for k in range(1, shards)])
    return jnp.stack(
        [lax.dynamic_index_in_dim(held, s ^ me, 0, keepdims=False) for s in range(shards)]
    )


def sum_over_seq(value, shards):
    me = lax.axis_index("seq")
    part = lambda j: lax.dynamic_index_in_dim(value, j ^ me, 0, keepdims=False)
    sent = along_seq(jnp.stack([part(1), part(3)]), 1, shards).astype(f32)
    passed = (part(2).astype(f32) + sent[1]).astype(value.dtype)
    return part(0).astype(f32) + sent[0] + along_seq(passed, 2, shards).astype(f32)


def swap_over(value, axes):
    return lax.all_to_all(value, axes, split_axis=0, concat_axis=0, tiled=True)


def after(value, *others):
    return lax.optimization_barrier((value,) + others)[0]


def on_device(
    shards,
    ranks,
    layer_input,
    doc_ids,
    expert_routes,
    attn_gain,
    query_weight,
    key_projection_weight,
    value_projection_weight,
    out_weight,
    ffn_gain,
    router_weight,
    gate_weight,
    up_weight,
    down_weight,
    out_cotangent,
):
    local = layer_input.shape[0]
    tokens = doc_ids.shape[1]
    copies = ranks // KEY_VALUE_HEADS
    experts = gate_weight.shape[0]
    rows = query_weight.shape[0]
    blocks = tokens // BLOCK
    rank = lax.axis_index("exp")
    me = lax.axis_index("seq")
    head_width = GROUP * HEAD_SIZE
    wide, narrow, half = MODEL_WIDTH // shards, FF // shards, MODEL_WIDTH // 2

    x_row = lax.all_gather(layer_input, "exp", axis=0, tiled=True)

    by_head = jnp.concatenate(
        [
            query_weight.reshape(rows, KEY_VALUE_HEADS, head_width),
            key_projection_weight.reshape(rows, KEY_VALUE_HEADS, HEAD_SIZE),
            value_projection_weight.reshape(rows, KEY_VALUE_HEADS, HEAD_SIZE),
        ],
        axis=2,
    )
    own_width = by_head.shape[2]
    per_row = local * TOPK // rows
    small = jnp.concatenate(
        [
            router_weight,
            attn_gain[:, None],
            ffn_gain[:, None],
            jnp.zeros((rows, -(EXPERTS + 2 + per_row) % LANES), bf16),
            expert_routes.astype(bf16).reshape(rows, per_row),
        ],
        axis=1,
    )
    to_send = jnp.concatenate(
        [
            jnp.repeat(by_head.transpose(1, 0, 2), copies, axis=0),
            jnp.broadcast_to(small[None], (ranks,) + small.shape),
        ],
        axis=2,
    )
    got = swap_over(to_send, "exp").reshape(ranks * rows, -1)
    routes_row = got[:, got.shape[1] - per_row :].reshape(tokens, TOPK)
    routes_row = routes_row.astype(jnp.int32)
    weights = gather_over_seq(got[:, : own_width + LANES], shards).reshape(MODEL_WIDTH, -1)
    own_weight = weights[:, :own_width]
    small_all = weights[:, own_width:]
    gain_one = small_all[:, EXPERTS].astype(f32)[None]
    gain_two = small_all[:, EXPERTS + 1].astype(f32)[None]
    lane = jnp.arange(LANES)[None, :]
    router_mat = jnp.where(lane < EXPERTS, small_all, 0)
    key_part = own_weight[:, head_width : head_width + HEAD_SIZE]
    value_part = own_weight[:, head_width + HEAD_SIZE :]
    wide_weight = jnp.concatenate(
        [own_weight[:, :head_width]] + [key_part] * GROUP + [value_part] * GROUP, axis=1
    )

    left_weight, right_weight = down_weight[:, :, :half], down_weight[:, :, half:]
    near_gate, near_up = along_seq(gate_weight, 1, shards), along_seq(up_weight, 2, shards)

    seg_row = doc_ids[0]
    smaller = jnp.sum(
        (seg_row[None, :] < jnp.arange(DOCS, dtype=jnp.int32)[:, None]).astype(jnp.int32), axis=1
    )
    start = jnp.sum(
        jnp.where(seg_row[None, :] == jnp.arange(DOCS)[:, None], smaller[:, None], 0), axis=0
    ).astype(jnp.int32)
    positions = (jnp.arange(tokens, dtype=jnp.int32) - start).astype(f32)
    half_head = HEAD_SIZE // 2
    inv_freq = rope_base ** (-2.0 * jnp.arange(half_head, dtype=f32) / HEAD_SIZE)
    angles = positions[:, None] * inv_freq[None, :]
    cos_half, sin_half = jnp.cos(angles), jnp.sin(angles)
    cosine = jnp.concatenate([cos_half] * (2 * GROUP), axis=1)
    sine = jnp.concatenate([-sin_half, sin_half] * GROUP, axis=1)
    first_block = start[::BLOCK] // BLOCK
    start_blocks = start.reshape(blocks, 1, BLOCK)

    first_expert = rank * experts
    own_ids = first_expert + jnp.arange(experts, dtype=jnp.int32)
    own_member = jnp.any(routes_row.T[None] == own_ids[:, None, None], axis=1)
    own_member = own_member.reshape(experts, blocks, BLOCK)
    triangle = (jnp.arange(BLOCK)[:, None] <= jnp.arange(BLOCK)[None, :]).astype(bf16)
    counts = jnp.dot(
        own_member.reshape(experts * blocks, BLOCK).astype(bf16),
        triangle,
        preferred_element_type=f32,
    ).reshape(experts, blocks, BLOCK)
    slots = jnp.where(own_member, counts.astype(jnp.int32) - 1, -1)
    group = 2
    slot_rows = (
        slots.reshape(experts, blocks // group, group, BLOCK)
        .transpose(1, 0, 2, 3)
        .reshape(blocks // group, experts * group, BLOCK)
    )
    slot_cols = jnp.pad(
        slots.reshape(experts, tokens).T, ((0, 0), (0, LANES - experts)), constant_values=-1
    )
    place = jnp.stack([first_expert, me])

    key_place = jnp.stack([me, lax.rem(rank, copies)])
    x_row, near_gate, near_up, slot_rows, slot_cols, place, key_place, routes_row = (
        lax.optimization_barrier(
            (x_row, near_gate, near_up, slot_rows, slot_cols, place, key_place, routes_row)
        )
    )
    cot_a = lax.all_gather(after(out_cotangent[:COT_EARLY], got), "exp", axis=0, tiled=True)
    out_rows = lax.all_gather(after(out_weight, got), "exp", axis=0, tiled=True)
    x_row, out_rows = lax.optimization_barrier((x_row, out_rows))
    left_weight, right_weight = lax.optimization_barrier((left_weight, right_weight, near_gate))[:2]
    near_left, near_right = along_seq(left_weight, 1, shards), along_seq(right_weight, 2, shards)
    next_left, next_right = along_seq(left_weight, 2, shards), along_seq(right_weight, 1, shards)

    normed_row, query_low, key_low, value_low, mixed_own, mixed_t, log_total = attention_forward(
        first_block, x_row, wide_weight, gain_one, cosine, sine, start_blocks
    )
    share = tokens // copies
    part = lax.rem(rank, copies) * share
    (
        mixed_own,
        cot_a,
        near_left,
        near_right,
        next_left,
        next_right,
    ) = lax.optimization_barrier(
        (mixed_own, cot_a, near_left, near_right, next_left, next_right)
    )
    mixed_part = lax.dynamic_slice_in_dim(mixed_own, part, share) if copies > 1 else mixed_own
    mixed_row = lax.all_gather(mixed_part, "exp", axis=0, tiled=True)
    cot_b = lax.all_gather(
        after(out_cotangent[COT_EARLY:], mixed_own), "exp", axis=0, tiled=True
    )
    out_mat = gather_over_seq(after(out_rows, mixed_own), shards).reshape(MODEL_WIDTH, -1)
    gate_weight, up_weight = lax.optimization_barrier((gate_weight, up_weight, near_left))[:2]
    next_gate, next_up = along_seq(gate_weight, 2, shards), along_seq(up_weight, 1, shards)
    far_left = along_seq(after(near_left, mixed_own), 2, shards)
    far_right = along_seq(after(near_right, mixed_own), 1, shards)
    mixed_row, out_mat, next_gate, next_up, far_left, far_right = lax.optimization_barrier(
        (mixed_row, out_mat, next_gate, next_up, far_left, far_right)
    )
    far_gate = along_seq(after(near_gate, next_gate), 2, shards)
    far_up = along_seq(after(near_up, next_up), 1, shards)
    mixed_row = mixed_row.reshape(KEY_VALUE_HEADS, tokens, head_width)
    (
        normed_two_row,
        probs_row,
        probs_t,
        middle,
        mixed_home,
        normed_two_home,
        probs_home,
    ) = middle_forward(rank[None], mixed_row, x_row, out_mat, gain_two, router_mat, routes_row)
    normed_two_row, far_gate, far_up = lax.optimization_barrier((normed_two_row, far_gate, far_up))
    weight_all = lax.all_gather(
        (lambda w: lax.dynamic_slice_in_dim(w, lax.rem(rank, copies) * (MODEL_WIDTH // copies), MODEL_WIDTH // copies) if copies > 1 else w)(
            after(own_weight, normed_two_row)
        ),
        "exp",
        axis=0,
        tiled=True,
    ).reshape(KEY_VALUE_HEADS, MODEL_WIDTH, own_width)

    moe_part, row_part, weigh, *kept = expert_rows(
        place,
        normed_two_row,
        cot_a,
        cot_b,
        probs_row,
        probs_t,
        slot_rows,
        slot_cols,
        [gate_weight, near_gate, next_gate, far_gate]
        + [up_weight, next_up, near_up, far_up]
        + [left_weight, near_left, next_left, far_left]
        + [right_weight, next_right, near_right, far_right],
        group,
    )
    mixed_turned = (
        mixed_home.reshape(local, shards, ranks, rows)
        .transpose(0, 2, 1, 3)
        .reshape(local, MODEL_WIDTH)
    )
    row_part, weight_all, mixed_turned = lax.optimization_barrier(
        (row_part, weight_all, mixed_turned)
    )
    row_sum = lax.psum_scatter(row_part, "exp", scatter_dimension=0, tiled=True)
    pieces = expert_weights(place, *kept, shards)
    stay, go = pieces[0::2], pieces[1::2]
    weigh_home = swap_over(
        after(weigh, go[0]).reshape(blocks // group, experts, group, BLOCK)
        .transpose(0, 2, 1, 3)
        .reshape(ranks, experts, local),
        "exp",
    )
    weigh_home = weigh_home.reshape(EXPERTS, local).T

    def first_exchange(piece, since):
        a, b = go[piece], go[3 + piece]
        if since is not None:
            a, b = after(a, since), after(b, since)
        return along_seq(a, 1, shards), along_seq(b, 2, shards)

    come_0 = first_exchange(0, None)
    row_sum, come_0, weigh_home = lax.optimization_barrier(
        (after(row_sum, go[0]), come_0, weigh_home)
    )
    come_1 = first_exchange(1, row_sum)

    out_grad = out_cotangent.astype(f32)
    probs_own = probs_home[:, :EXPERTS]
    logits_low = (
        weigh_home - probs_own * jnp.sum(weigh_home, axis=1, keepdims=True)
    ).astype(bf16)
    router_part = dot_tn(normed_two_home, logits_low)
    normed_two_grad = row_sum.astype(f32) + dot_nt(logits_low, router_mat[:, :EXPERTS])
    scale_two = lax.rsqrt(jnp.mean(middle * middle, axis=-1, keepdims=True) + eps_norm)
    gain_two_part = jnp.sum(normed_two_grad * middle * scale_two, axis=0)
    through = gain_two * normed_two_grad
    middle_grad = (
        out_grad
        + scale_two * through
        - middle * scale_two**3 * jnp.mean(middle * through, axis=-1, keepdims=True)
    )
    branch_low = middle_grad.astype(bf16)
    mixed_grad = dot_nt(branch_low, out_mat).astype(bf16)
    mixed_grad_row = swap_over(
        jnp.repeat(
            mixed_grad.reshape(local, KEY_VALUE_HEADS, head_width).transpose(1, 0, 2), copies, axis=0
        ),
        "exp",
    ).reshape(tokens, head_width)

    out_part = dot_tn(mixed_turned, branch_low).astype(bf16)
    out_part = lax.psum_scatter(out_part, "exp", scatter_dimension=0, tiled=True)
    moe_sum = lax.psum_scatter(
        after(moe_part, mixed_grad_row), "exp", scatter_dimension=0, tiled=True
    )

    mixed_grad_row, come_1 = lax.optimization_barrier((mixed_grad_row, come_1))
    come_2 = first_exchange(2, mixed_grad_row)

    come = [come_0, come_1, come_2]
    add = lambda x, y: x.astype(f32) + y.astype(f32)
    kept_parts = lambda side, n: stay[3 * side + n][0].astype(f32) + come[n][side][0].astype(f32)

    def pass_on(side, pieces, since):
        parts = [
            (stay[3 * side + n][1].astype(f32) + come[n][side][1].astype(f32)).astype(bf16)
            for n in pieces
        ]
        parts = after(jnp.stack(parts) if len(parts) > 1 else parts[0][None], since)
        return along_seq(parts, (2, 1)[side], shards)

    early_a, early_b = pass_on(0, (0,), mixed_grad_row), pass_on(1, (0,), mixed_grad_row)
    small_part = jnp.concatenate(
        [router_part, gain_two_part[:, None], jnp.zeros((MODEL_WIDTH, LANES - EXPERTS - 1), f32)],
        axis=1,
    )
    lin_low, weight_stay, weight_go = attention_backward(
        first_block,
        key_place,
        query_low,
        mixed_grad_row,
        mixed_t,
        log_total,
        start_blocks,
        cosine,
        sine,
        key_low,
        value_low,
        small_part,
        normed_row,
        shards,
        copies,
    )
    lin_home = swap_over(lin_low.reshape(ranks, local, own_width), "exp")
    weight_come = along_seq(weight_go, 1, shards)
    weight_come, come_2, early_a, early_b, out_part = lax.optimization_barrier(
        (weight_come, come_2, early_a, early_b, out_part)
    )
    come[2] = come_2
    weight_pass = along_seq(add(weight_stay[1], weight_come[1]).astype(bf16), 2, shards)
    weight_sum = (
        add(weight_stay[0], weight_come[0]) + weight_pass.astype(f32)
    ).astype(bf16)
    late_a, late_b = pass_on(0, (1, 2), weight_sum), pass_on(1, (1, 2), weight_sum)
    out_weight_grad = sum_over_seq(out_part.reshape(shards, rows, MODEL_WIDTH), shards)
    weight_sum, lin_home = lax.optimization_barrier((weight_sum, lin_home))
    weight_home = swap_over(weight_sum.reshape(ranks, rows, -1), "exp").astype(f32)
    weight_home, late_a, late_b = lax.optimization_barrier((weight_home, late_a, late_b))
    halves = [
        [
            kept_parts(side, n) + passed.astype(f32)
            for n, passed in enumerate((early[0], late[0], late[1]))
        ]
        for side, (early, late) in enumerate(((early_a, late_a), (early_b, late_b)))
    ]
    gate_grad, up_grad = (jnp.concatenate(h[:2], axis=1) for h in halves)
    down_grad = jnp.concatenate([halves[0][2], halves[1][2]], axis=2)
    tail = jnp.sum(weight_home[:, :, own_width:], axis=0)
    router_grad = tail[:, :EXPERTS]
    ffn_gain_grad = tail[:, EXPERTS]
    weight_home = jnp.sum(
        weight_home[:, :, :own_width].reshape(KEY_VALUE_HEADS, copies, rows, own_width), axis=1
    ).transpose(1, 0, 2)
    lin_home = lin_home.reshape(KEY_VALUE_HEADS, copies, local, own_width)[:, 0]
    normed_grad = sum(dot_nt(lin_home[h], weight_all[h]) for h in range(KEY_VALUE_HEADS))
    inputs = layer_input.astype(f32)
    scale_one = lax.rsqrt(jnp.mean(inputs * inputs, axis=-1, keepdims=True) + eps_norm)
    through_one = gain_one * normed_grad
    input_grad = (
        middle_grad
        + scale_one * through_one
        - inputs * scale_one**3 * jnp.mean(inputs * through_one, axis=-1, keepdims=True)
    )

    query_grad = weight_home[:, :, :head_width].reshape(rows, -1)
    key_grad = weight_home[:, :, head_width : head_width + HEAD_SIZE].reshape(rows, -1)
    value_grad = weight_home[:, :, head_width + HEAD_SIZE :].reshape(rows, -1)
    attn_gain_grad = jnp.sum(weight_home * by_head.astype(f32), axis=(1, 2)) / attn_gain.astype(f32)

    layer_output = (middle + moe_sum.astype(f32)).astype(bf16)
    return (
        layer_output,
        input_grad,
        attn_gain_grad,
        query_grad,
        key_grad,
        value_grad,
        out_weight_grad,
        ffn_gain_grad,
        router_grad,
        gate_grad,
        up_grad,
        down_grad,
    )


def solution(mesh):
    tokens_2d = P(("seq", "exp"), None)
    vector = P(("seq", "exp"))
    expert = P("exp", "seq", None)
    return jax.shard_map(
        functools.partial(on_device, mesh.shape["seq"], mesh.shape["exp"]),
        mesh=mesh,
        in_specs=(
            tokens_2d,
            P("seq", None),
            tokens_2d,
            vector,
            tokens_2d,
            tokens_2d,
            tokens_2d,
            tokens_2d,
            vector,
            tokens_2d,
            expert,
            expert,
            expert,
            tokens_2d,
        ),
        out_specs=(
            tokens_2d,
            tokens_2d,
            vector,
            tokens_2d,
            tokens_2d,
            tokens_2d,
            tokens_2d,
            vector,
            tokens_2d,
            expert,
            expert,
            expert,
        ),
        check_vma=False,
    )
```

```python
import functools

import jax
import jax.numpy as jnp
from jax import lax
from jax.experimental import pallas as pl
from jax.experimental.pallas import tpu as pltpu
from jax.sharding import PartitionSpec as P

MODEL_WIDTH = 1024
QUERY_HEADS = 16
KEY_VALUE_HEADS = 8
HEAD_SIZE = 64
FF = 512
EXPERTS = 32
TOPK = 8
DOCS = 4
CAP = 128

BLOCK = 256
COT_EARLY = 96
MID = 512
SUB = 256
LANES = 128
GROUP = QUERY_HEADS // KEY_VALUE_HEADS
PACK = GROUP * HEAD_SIZE

eps_norm = 1e-06
rope_base = 10000.0
score_masked = -1e30
score_scale = HEAD_SIZE**-0.5
f32 = jnp.float32
bf16 = jnp.bfloat16
VMEM_LIMIT = 60 * 1024 * 1024


def dot_nn(a, b):
    return lax.dot_general(a, b, (((1,), (0,)), ((), ())), preferred_element_type=f32)


def dot_nt(a, b):
    return lax.dot_general(a, b, (((1,), (1,)), ((), ())), preferred_element_type=f32)


def dot_tn(a, b):
    return lax.dot_general(a, b, (((0,), (0,)), ((), ())), preferred_element_type=f32)


def swap_halves(v):
    lane = lax.broadcasted_iota(jnp.int32, v.shape, 1)
    half = HEAD_SIZE // 2
    return jnp.where(
        lane % HEAD_SIZE < half, pltpu.roll(v, PACK - half, 1), pltpu.roll(v, half, 1)
    )


def head_stack(v):
    lane = lax.broadcasted_iota(jnp.int32, v.shape, 1)
    zero = jnp.zeros_like(v)
    return jnp.concatenate(
        [jnp.where(lane < HEAD_SIZE, v, zero), jnp.where(lane >= HEAD_SIZE, v, zero)], axis=0
    )


def visible_from(block_key, block_query, start_row):
    shape = (BLOCK, GROUP * BLOCK)
    key_place = block_key * BLOCK + lax.broadcasted_iota(jnp.int32, shape, 0)
    lane = lax.broadcasted_iota(jnp.int32, shape, 1)
    query_place = block_query * BLOCK + lane % BLOCK
    return (key_place >= start_row) & (key_place <= query_place)


def attention_forward_kernel(
    first_block,
    x_ref,
    weight_ref,
    gain_ref,
    cos_ref,
    sin_ref,
    start_ref,
    normed_ref,
    query_ref,
    key_ref,
    value_ref,
    mixed_ref,
    mixed_t_ref,
    log_ref,
    key_all,
    value_all,
):
    i = pl.program_id(0)
    x = x_ref[...].astype(f32)
    normed = (
        x * lax.rsqrt(jnp.mean(x * x, axis=-1, keepdims=True) + eps_norm) * gain_ref[...]
    ).astype(bf16)
    normed_ref[...] = normed
    lin = dot_nn(normed, weight_ref[...])
    cosine, sine = cos_ref[...], sin_ref[...]
    query_lin, key_lin = lin[:, :PACK], lin[:, PACK : 2 * PACK]
    query = (query_lin * cosine + swap_halves(query_lin) * sine).astype(bf16)
    key = (key_lin * cosine + swap_halves(key_lin) * sine).astype(bf16)
    value = lin[:, 2 * PACK :].astype(bf16)
    query_ref[...] = query
    key_ref[...] = key
    value_ref[...] = value
    rows = pl.ds(pl.multiple_of(i * BLOCK, BLOCK), BLOCK)
    key_all[rows, :] = key
    value_all[rows, :] = value
    query_two = head_stack(query * jnp.asarray(score_scale, bf16))
    start_row = start_ref[0]
    start_two = jnp.concatenate([start_row] * GROUP, axis=1)

    def visit(j, carry):
        run_max, run_sum, acc = carry
        here = pl.ds(pl.multiple_of(j * BLOCK, BLOCK), BLOCK)
        scores = dot_nt(key_all[here, :], query_two)
        scores = jnp.where(visible_from(j, i, start_two), scores, score_masked)
        new_max = jnp.maximum(run_max, jnp.max(scores, axis=0, keepdims=True))
        shrink = jnp.exp(run_max - new_max)
        weights = jnp.exp(scores - new_max)
        run_sum = run_sum * shrink + jnp.sum(weights, axis=0, keepdims=True)
        acc = acc * shrink + dot_tn(value_all[here, :], weights.astype(bf16))
        return new_max, run_sum, acc

    width = GROUP * BLOCK
    run_max, run_sum, acc = lax.fori_loop(
        first_block[i],
        i + 1,
        visit,
        (
            jnp.full((1, width), score_masked, f32),
            jnp.zeros((1, width), f32),
            jnp.zeros((PACK, width), f32),
        ),
    )
    acc = acc * (1.0 / run_sum)
    mixed_t = jnp.concatenate([acc[:HEAD_SIZE, :BLOCK], acc[HEAD_SIZE:, BLOCK:]], axis=0)
    mixed_t_ref[0] = mixed_t
    mixed_ref[...] = mixed_t.T.astype(bf16)
    log_ref[0] = run_max + jnp.log(run_sum)


def attention_forward(first_block, x_row, weight, gain, cosine, sine, start):
    tokens = x_row.shape[0]
    blocks = tokens // BLOCK
    row = lambda i, *_: (i, 0)
    page = lambda i, *_: (i, 0, 0)
    whole = lambda i, *_: (0, 0)
    return pl.pallas_call(
        attention_forward_kernel,
        grid_spec=pltpu.PrefetchScalarGridSpec(
            num_scalar_prefetch=1,
            grid=(blocks,),
            in_specs=[
                pl.BlockSpec((BLOCK, MODEL_WIDTH), row),
                pl.BlockSpec(weight.shape, whole),
                pl.BlockSpec((1, MODEL_WIDTH), whole),
                pl.BlockSpec((BLOCK, PACK), row),
                pl.BlockSpec((BLOCK, PACK), row),
                pl.BlockSpec((1, 1, BLOCK), page),
            ],
            out_specs=[
                pl.BlockSpec((BLOCK, MODEL_WIDTH), row),
                pl.BlockSpec((BLOCK, PACK), row),
                pl.BlockSpec((BLOCK, PACK), row),
                pl.BlockSpec((BLOCK, PACK), row),
                pl.BlockSpec((BLOCK, PACK), row),
                pl.BlockSpec((1, PACK, BLOCK), page),
                pl.BlockSpec((1, 1, GROUP * BLOCK), page),
            ],
            scratch_shapes=[pltpu.VMEM((tokens, PACK), bf16), pltpu.VMEM((tokens, PACK), bf16)],
        ),
        out_shape=[
            jax.ShapeDtypeStruct((tokens, MODEL_WIDTH), bf16),
            jax.ShapeDtypeStruct((tokens, PACK), bf16),
            jax.ShapeDtypeStruct((tokens, PACK), bf16),
            jax.ShapeDtypeStruct((tokens, PACK), bf16),
            jax.ShapeDtypeStruct((tokens, PACK), bf16),
            jax.ShapeDtypeStruct((blocks, PACK, BLOCK), f32),
            jax.ShapeDtypeStruct((blocks, 1, GROUP * BLOCK), f32),
        ],
        cost_estimate=cost(
            tokens * (2 * MODEL_WIDTH * 3 * PACK + 8 * PACK * tokens), tokens * MODEL_WIDTH * 4
        ),
        compiler_params=pltpu.CompilerParams(vmem_limit_bytes=VMEM_LIMIT),
        name="attention_forward",
    )(first_block, x_row, weight, gain, cosine, sine, start)


def attention_backward_kernel(
    shards,
    copies,
    first_block,
    place,
    query_ref,
    grad_ref,
    mixed_t_ref,
    log_ref,
    start_ref,
    cos_ref,
    sin_ref,
    key_ref,
    value_ref,
    small_ref,
    *refs,
):
    normed_refs, (lin_grad_ref, stay_ref, go_ref, key_acc, value_acc) = refs[:shards], refs[shards:]
    i = pl.program_id(0)
    blocks = pl.num_programs(0)

    @pl.when(i == 0)
    def _():
        key_acc[...] = jnp.zeros_like(key_acc)
        value_acc[...] = jnp.zeros_like(value_acc)

    query_two = head_stack(query_ref[...] * jnp.asarray(score_scale, bf16))
    grad = grad_ref[...]
    grad_two = head_stack(grad)
    product = mixed_t_ref[0] * grad.astype(f32).T
    delta = jnp.concatenate(
        [
            jnp.sum(product[:HEAD_SIZE], axis=0, keepdims=True),
            jnp.sum(product[HEAD_SIZE:], axis=0, keepdims=True),
        ],
        axis=1,
    )
    log_total = log_ref[0]
    start_two = jnp.concatenate([start_ref[0]] * GROUP, axis=1)

    def visit(j, query_acc):
        here = pl.ds(pl.multiple_of(j * BLOCK, BLOCK), BLOCK)
        key = key_ref[here, :]
        scores = dot_nt(key, query_two)
        probs = jnp.where(visible_from(j, i, start_two), jnp.exp(scores - log_total), 0.0)
        prob_grad = dot_nt(value_ref[here, :], grad_two)
        score_grad = (probs * (prob_grad - delta)).astype(bf16)
        value_acc[here, :] += dot_nn(probs.astype(bf16), grad_two)
        key_acc[here, :] += dot_nn(score_grad, query_two)
        return query_acc + dot_tn(score_grad, key)

    query_acc = lax.fori_loop(
        first_block[i], i + 1, visit, jnp.zeros((GROUP * BLOCK, PACK), f32)
    )
    lane = lax.broadcasted_iota(jnp.int32, (BLOCK, PACK), 1)
    rotated = jnp.where(lane < HEAD_SIZE, query_acc[:BLOCK], query_acc[BLOCK:]) * score_scale
    rows = pl.ds(pl.multiple_of(i * BLOCK, BLOCK), BLOCK)
    lin_grad_ref[rows, :PACK] = (
        rotated * cos_ref[rows, :] - swap_halves(rotated) * sin_ref[rows, :]
    ).astype(bf16)

    @pl.when(i == blocks - 1)
    def _():
        def finish(b, carry):
            here = pl.ds(pl.multiple_of(b * BLOCK, BLOCK), BLOCK)
            key_sum = key_acc[here, :]
            key_sum = key_sum + pltpu.roll(key_sum, HEAD_SIZE, 1)
            value_sum = value_acc[here, :]
            value_sum = value_sum + pltpu.roll(value_sum, HEAD_SIZE, 1)
            key_lin = key_sum * cos_ref[here, :] - swap_halves(key_sum) * sin_ref[here, :]
            lin_grad_ref[here, PACK:] = jnp.where(lane < HEAD_SIZE, key_lin, value_sum).astype(bf16)
            return carry

        lax.fori_loop(0, blocks, finish, 0)
        share = lin_grad_ref.shape[0] // copies
        own = lin_grad_ref[pl.ds(pl.multiple_of(place[1] * share, share), share), :]
        wide = MODEL_WIDTH // shards
        for n, j in enumerate(exchange_order(shards, 0)):
            out = (stay_ref, go_ref)[n // (shards // 2)]
            at = n % (shards // 2)
            out[at, :, : 2 * PACK] = dot_tn(normed_refs[n][...], own).astype(bf16)
            rows = pl.ds(pl.multiple_of((j ^ place[0]) * wide, wide), wide)
            out[at, :, 2 * PACK :] = small_ref[rows, :].astype(bf16)


def attention_backward(
    first_block,
    place,
    query,
    grad,
    mixed_t,
    log_total,
    start,
    cosine,
    sine,
    key,
    value,
    small,
    normed,
    shards,
    copies,
):
    tokens = query.shape[0]
    wide = MODEL_WIDTH // shards
    part = lambda j: pl.BlockSpec(
        (tokens // copies, wide), lambda i, first, place, j=j: (place[1], j ^ place[0])
    )
    out = (shards // 2, wide, 2 * PACK + LANES)
    blocks = tokens // BLOCK
    row = lambda i, *_: (i, 0)
    page = lambda i, *_: (i, 0, 0)
    whole = lambda i, *_: (0, 0)
    return pl.pallas_call(
        functools.partial(attention_backward_kernel, shards, copies),
        grid_spec=pltpu.PrefetchScalarGridSpec(
            num_scalar_prefetch=2,
            grid=(blocks,),
            in_specs=[
                pl.BlockSpec((BLOCK, PACK), row),
                pl.BlockSpec((BLOCK, PACK), row),
                pl.BlockSpec((1, PACK, BLOCK), page),
                pl.BlockSpec((1, 1, GROUP * BLOCK), page),
                pl.BlockSpec((1, 1, BLOCK), page),
                pl.BlockSpec((tokens, PACK), whole),
                pl.BlockSpec((tokens, PACK), whole),
                pl.BlockSpec((tokens, PACK), whole),
                pl.BlockSpec((tokens, PACK), whole),
                pl.BlockSpec((MODEL_WIDTH, LANES), whole),
            ]
            + [part(j) for j in exchange_order(shards, 0)],
            out_specs=[
                pl.BlockSpec((tokens, 2 * PACK), whole),
                pl.BlockSpec(out, lambda i, *_: (0, 0, 0)),
                pl.BlockSpec(out, lambda i, *_: (0, 0, 0)),
            ],
            scratch_shapes=[pltpu.VMEM((tokens, PACK), f32), pltpu.VMEM((tokens, PACK), f32)],
        ),
        out_shape=[
            jax.ShapeDtypeStruct((tokens, 2 * PACK), bf16),
            jax.ShapeDtypeStruct(out, bf16),
            jax.ShapeDtypeStruct(out, bf16),
        ],
        cost_estimate=cost(20 * tokens * tokens * PACK, tokens * PACK * 28),
        compiler_params=pltpu.CompilerParams(vmem_limit_bytes=VMEM_LIMIT),
        name="attention_backward",
    )(
        first_block,
        place,
        query,
        grad,
        mixed_t,
        log_total,
        start,
        cosine,
        sine,
        key,
        value,
        small,
        *([normed] * shards),
    )


def middle_kernel(
    home,
    mixed_ref,
    x_ref,
    weight_ref,
    gain_ref,
    router_ref,
    routes_ref,
    normed_ref,
    probs_ref,
    probs_t_ref,
    home_middle_ref,
    home_mixed_ref,
    home_normed_ref,
    home_probs_ref,
    keep_middle,
    keep_mixed,
):
    i = pl.program_id(0)
    parts = x_ref.shape[0] // SUB
    lane = lax.broadcasted_iota(jnp.int32, (SUB, LANES), 1)
    for n in range(parts):
        here = slice(n * SUB, (n + 1) * SUB)
        mixed = jnp.concatenate([mixed_ref[h, here] for h in range(KEY_VALUE_HEADS)], axis=1)
        middle = x_ref[here].astype(f32) + dot_nn(mixed, weight_ref[...])
        normed = (
            middle
            * lax.rsqrt(jnp.mean(middle * middle, axis=-1, keepdims=True) + eps_norm)
            * gain_ref[...]
        ).astype(bf16)
        normed_ref[here] = normed
        logits = dot_nn(normed, router_ref[...])
        routes = routes_ref[here]
        member = jnp.zeros_like(logits)
        for k in range(TOPK):
            member = jnp.where(lane == routes[:, k : k + 1], 1.0, member)
        chosen = jnp.where(member > 0, logits, score_masked)
        raised = jnp.exp(chosen - jnp.max(chosen, axis=-1, keepdims=True)) * member
        probs = raised / jnp.sum(raised, axis=-1, keepdims=True)
        probs_ref[here] = probs
        probs_t_ref[:, here] = probs.T[:EXPERTS]
        keep_middle[here] = middle
        keep_mixed[here] = mixed

    @pl.when(i == home[0] * BLOCK // x_ref.shape[0])
    def _():
        at = pl.ds(pl.multiple_of(home[0] * BLOCK % x_ref.shape[0], BLOCK), BLOCK)
        home_middle_ref[...] = keep_middle[at]
        home_mixed_ref[...] = keep_mixed[at]
        home_normed_ref[...] = normed_ref[at]
        home_probs_ref[...] = probs_ref[at]


def middle_forward(home, mixed, x_row, weight, gain, router, routes):
    tokens = x_row.shape[0]
    row = lambda i, *_: (i, 0)
    whole = lambda i, *_: (0, 0)
    return pl.pallas_call(
        middle_kernel,
        grid_spec=pltpu.PrefetchScalarGridSpec(
            num_scalar_prefetch=1,
            grid=(tokens // MID,),
            in_specs=[
                pl.BlockSpec((KEY_VALUE_HEADS, MID, PACK), lambda i, *_: (0, i, 0)),
                pl.BlockSpec((MID, MODEL_WIDTH), row),
                pl.BlockSpec((MODEL_WIDTH, MODEL_WIDTH), whole),
                pl.BlockSpec((1, MODEL_WIDTH), whole),
                pl.BlockSpec((MODEL_WIDTH, LANES), whole),
                pl.BlockSpec((MID, TOPK), row),
            ],
            out_specs=[
                pl.BlockSpec((MID, MODEL_WIDTH), row),
                pl.BlockSpec((MID, LANES), row),
                pl.BlockSpec((EXPERTS, MID), lambda i, *_: (0, i)),
                pl.BlockSpec((BLOCK, MODEL_WIDTH), whole),
                pl.BlockSpec((BLOCK, MODEL_WIDTH), whole),
                pl.BlockSpec((BLOCK, MODEL_WIDTH), whole),
                pl.BlockSpec((BLOCK, LANES), whole),
            ],
            scratch_shapes=[
                pltpu.VMEM((MID, MODEL_WIDTH), f32),
                pltpu.VMEM((MID, MODEL_WIDTH), bf16),
            ],
        ),
        out_shape=[
            jax.ShapeDtypeStruct((tokens, MODEL_WIDTH), bf16),
            jax.ShapeDtypeStruct((tokens, LANES), f32),
            jax.ShapeDtypeStruct((EXPERTS, tokens), f32),
            jax.ShapeDtypeStruct((BLOCK, MODEL_WIDTH), f32),
            jax.ShapeDtypeStruct((BLOCK, MODEL_WIDTH), bf16),
            jax.ShapeDtypeStruct((BLOCK, MODEL_WIDTH), bf16),
            jax.ShapeDtypeStruct((BLOCK, LANES), f32),
        ],
        cost_estimate=cost(
            2 * tokens * MODEL_WIDTH * (MODEL_WIDTH + LANES), tokens * MODEL_WIDTH * 6
        ),
        compiler_params=pltpu.CompilerParams(vmem_limit_bytes=VMEM_LIMIT),
        name="middle_forward",
    )(home, mixed, x_row, weight, gain, router, routes)


def cost(flops, moved):
    return pl.CostEstimate(flops=int(flops), transcendentals=0, bytes_accessed=int(moved))


def column_of(values, lane_wanted):
    lane = lax.broadcasted_iota(jnp.int32, values.shape, 1)
    return jnp.sum(
        jnp.where(lane == lane_wanted, values, jnp.zeros_like(values)), axis=-1, keepdims=True
    )


def expert_rows_kernel(shards, experts, group, place, *refs):
    normed_ref, cot_a_ref, cot_b_ref, probs_ref, probs_t_ref, slot_row_ref, slot_col_ref = refs[:7]
    weight_refs = [refs[7 + n * shards : 7 + (n + 1) * shards] for n in range(4)]
    (
        moe_ref,
        row_ref,
        weigh_ref,
        rows_ref,
        out_grad_ref,
        hidden_ref,
        gate_low_ref,
        up_low_ref,
        gate_all,
        up_all,
        down_all,
        out_all,
        back_all,
        sems,
    ) = refs[7 + 4 * shards :]
    first_expert, me = place[0], place[1]
    wide, narrow = MODEL_WIDTH // shards, FF // shards
    half = MODEL_WIDTH // 2

    def copies(e):
        made = []
        for j in range(shards):
            tall = pl.ds(pl.multiple_of((j ^ me) * wide, wide), wide)
            short = pl.ds(pl.multiple_of((j ^ me) * narrow, narrow), narrow)
            places = (
                gate_all.at[e, tall, :],
                up_all.at[e, tall, :],
                down_all.at[e, short, :half],
                down_all.at[e, short, half:],
            )
            for n in range(4):
                made.append(
                    pltpu.make_async_copy(weight_refs[n][j].at[e], places[n], sems.at[e, 4 * j + n])
                )
        return made

    @pl.when(pl.program_id(0) == 0)
    def _():
        for e in range(experts):
            for copy in copies(e):
                copy.start()

    slot_place = lax.broadcasted_iota(jnp.int32, (CAP, BLOCK), 0)
    slot_lane = lax.broadcasted_iota(jnp.int32, (BLOCK, CAP), 1)
    early, late = COT_EARLY, BLOCK - COT_EARLY
    cots = [
        jnp.concatenate(
            [
                cot_a_ref[b * early : (b + 1) * early, :],
                cot_b_ref[b * late : (b + 1) * late, :],
            ],
            axis=0,
        )
        for b in range(group)
    ]
    for e in range(experts):

        @pl.when(pl.program_id(0) == 0)
        def _():
            for copy in copies(e):
                copy.wait()

        picked, cot_picked = [], []
        hits = []
        for b in range(group):
            hit = slot_place == slot_row_ref[0, e * group + b : e * group + b + 1, :]
            hits.append(hit)
            pick = hit.astype(f32).astype(bf16)
            prob_row = probs_t_ref[pl.ds(first_expert + e, 1), b * BLOCK : (b + 1) * BLOCK]
            prob_slot = jnp.sum(jnp.where(hit, prob_row, 0.0), axis=-1, keepdims=True)
            picked.append(dot_nn(pick, normed_ref[b * BLOCK : (b + 1) * BLOCK, :]).astype(bf16))
            cot_picked.append((dot_nn(pick, cots[b]) * prob_slot).astype(bf16))
        rows = jnp.concatenate(picked, axis=0)
        out_grad = jnp.concatenate(cot_picked, axis=0)
        rows_ref[e] = rows
        out_grad_ref[e] = out_grad
        gate_pre = dot_nn(rows, gate_all[e])
        up_pre = dot_nn(rows, up_all[e])
        hidden_grad = dot_nt(out_grad, down_all[e])
        logistic = 1.0 / (1.0 + jnp.exp(-gate_pre))
        silu = gate_pre * logistic
        hidden = (silu * up_pre).astype(bf16)
        gate_low = (
            hidden_grad * up_pre * (logistic * (1.0 + gate_pre * (1.0 - logistic)))
        ).astype(bf16)
        up_low = (hidden_grad * silu).astype(bf16)
        hidden_ref[e] = hidden
        gate_low_ref[e] = gate_low
        up_low_ref[e] = up_low
        weigh = jnp.sum(hidden_grad * hidden.astype(f32), axis=-1, keepdims=True)
        out = dot_nn(hidden, down_all[e]).astype(bf16)
        row_grad = (dot_nt(gate_low, gate_all[e]) + dot_nt(up_low, up_all[e])).astype(bf16)
        for b in range(group):
            inside = slice(b * CAP, (b + 1) * CAP)
            out_all[b, e * CAP : (e + 1) * CAP, :] = out[inside]
            back_all[b, e * CAP : (e + 1) * CAP, :] = row_grad[inside]
            weigh_ref[0, e * group + b : e * group + b + 1, :] = jnp.sum(
                jnp.where(hits[b], weigh[inside], 0.0), axis=0, keepdims=True
            )
    for b in range(group):
        tokens = slice(b * BLOCK, (b + 1) * BLOCK)
        slot_cols, probs = slot_col_ref[tokens, :], probs_ref[tokens, :]
        plain, scaled = [], []
        for e in range(experts):
            hit = slot_lane == column_of(slot_cols, e)
            plain.append(hit.astype(f32).astype(bf16))
            scaled.append(jnp.where(hit, column_of(probs, first_expert + e), 0.0).astype(bf16))
        moe_ref[tokens, :] = dot_nn(jnp.concatenate(scaled, axis=1), out_all[b]).astype(bf16)
        row_ref[tokens, :] = dot_nn(jnp.concatenate(plain, axis=1), back_all[b]).astype(bf16)


def expert_rows(place, normed, cot_a, cot_b, probs, probs_t, slot_rows, slot_cols, weights, group):
    tokens = normed.shape[0]
    shards, experts = len(weights) // 4, weights[0].shape[0]
    span, slots = group * BLOCK, group * CAP
    steps = tokens // span
    row = lambda g, *_: (g, 0)
    page = lambda g, *_: (g, 0, 0)
    spread = lambda g, *_: (0, g, 0)
    total = tokens // BLOCK * CAP
    return pl.pallas_call(
        functools.partial(expert_rows_kernel, shards, experts, group),
        grid_spec=pltpu.PrefetchScalarGridSpec(
            num_scalar_prefetch=1,
            grid=(steps,),
            in_specs=[
                pl.BlockSpec((span, MODEL_WIDTH), row),
                pl.BlockSpec((group * COT_EARLY, MODEL_WIDTH), row),
                pl.BlockSpec((group * (BLOCK - COT_EARLY), MODEL_WIDTH), row),
                pl.BlockSpec((span, LANES), row),
                pl.BlockSpec((EXPERTS, span), lambda g, *_: (0, g)),
                pl.BlockSpec((1, experts * group, BLOCK), page),
                pl.BlockSpec((span, LANES), row),
            ]
            + [pl.BlockSpec(memory_space=pl.ANY)] * (4 * shards),
            out_specs=[
                pl.BlockSpec((span, MODEL_WIDTH), row),
                pl.BlockSpec((span, MODEL_WIDTH), row),
                pl.BlockSpec((1, experts * group, BLOCK), page),
                pl.BlockSpec((experts, slots, MODEL_WIDTH), spread),
                pl.BlockSpec((experts, slots, MODEL_WIDTH), spread),
                pl.BlockSpec((experts, slots, FF), spread),
                pl.BlockSpec((experts, slots, FF), spread),
                pl.BlockSpec((experts, slots, FF), spread),
            ],
            scratch_shapes=[
                pltpu.VMEM((experts, MODEL_WIDTH, FF), bf16),
                pltpu.VMEM((experts, MODEL_WIDTH, FF), bf16),
                pltpu.VMEM((experts, FF, MODEL_WIDTH), bf16),
                pltpu.VMEM((group, experts * CAP, MODEL_WIDTH), bf16),
                pltpu.VMEM((group, experts * CAP, MODEL_WIDTH), bf16),
                pltpu.SemaphoreType.DMA((experts, 4 * shards)),
            ],
        ),
        out_shape=[
            jax.ShapeDtypeStruct((tokens, MODEL_WIDTH), bf16),
            jax.ShapeDtypeStruct((tokens, MODEL_WIDTH), bf16),
            jax.ShapeDtypeStruct((steps, experts * group, BLOCK), f32),
            jax.ShapeDtypeStruct((experts, total, MODEL_WIDTH), bf16),
            jax.ShapeDtypeStruct((experts, total, MODEL_WIDTH), bf16),
            jax.ShapeDtypeStruct((experts, total, FF), bf16),
            jax.ShapeDtypeStruct((experts, total, FF), bf16),
            jax.ShapeDtypeStruct((experts, total, FF), bf16),
        ],
        cost_estimate=cost(
            12 * experts * total * MODEL_WIDTH * FF + 8 * experts * total * MODEL_WIDTH * BLOCK,
            experts * (3 * MODEL_WIDTH * FF + total * (2 * MODEL_WIDTH + 3 * FF)) * 2
            + tokens * MODEL_WIDTH * 8,
        ),
        compiler_params=pltpu.CompilerParams(vmem_limit_bytes=VMEM_LIMIT),
        name="expert_rows",
    )(place, normed, cot_a, cot_b, probs, probs_t, slot_rows, slot_cols, *weights)


def expert_weights_kernel(shards, place, *refs):
    rows_ref, out_grad_ref, hidden_ref, gate_low_ref, up_low_ref = refs[:5]
    outs, (gate_acc, up_acc, down_acc) = refs[5:17], refs[17:]
    me, c = place[1], pl.program_id(1)
    rows = rows_ref[0]
    for acc, left, right in (
        (gate_acc, rows, gate_low_ref[0]),
        (up_acc, rows, up_low_ref[0]),
        (down_acc, hidden_ref[0], out_grad_ref[0]),
    ):
        part = dot_tn(left, right)

        @pl.when(c == 0)
        def _():
            acc[...] = part

        @pl.when(c > 0)
        def _():
            acc[...] += part

    wide, narrow = MODEL_WIDTH // shards, FF // shards
    half = MODEL_WIDTH // 2

    @pl.when(c == pl.num_programs(1) - 1)
    def _():
        for side in range(2):
            square = (gate_acc, up_acc)[side]
            order = exchange_order(shards, side)
            for n, j in enumerate(order):
                kind, at = divmod(n, shards // 2)
                base = (j ^ me) * wide
                low = pl.ds(pl.multiple_of(base, narrow), narrow)
                high = pl.ds(pl.multiple_of(base + narrow, narrow), narrow)
                short = pl.ds(pl.multiple_of((j ^ me) * narrow, narrow), narrow)
                pieces = (
                    square[low, :],
                    square[high, :],
                    down_acc[short, side * half : (side + 1) * half],
                )
                for piece, value in enumerate(pieces):
                    outs[6 * side + 2 * piece + kind][at, 0] = value.astype(bf16)


def exchange_order(shards, side):
    first = (1, 2)[side]
    stay = [j for j in range(shards) if not j & first]
    return stay + [j ^ first for j in stay]


def expert_weights(place, rows, out_grad, hidden, gate_low, up_low, shards):
    experts, total = rows.shape[:2]
    chunk = min(total, 1024)
    narrow = FF // shards
    spec = lambda width: pl.BlockSpec((1, chunk, width), lambda e, c, *_: (e, c, 0))
    return pl.pallas_call(
        functools.partial(expert_weights_kernel, shards),
        grid_spec=pltpu.PrefetchScalarGridSpec(
            num_scalar_prefetch=1,
            grid=(experts, total // chunk),
            in_specs=[spec(MODEL_WIDTH), spec(MODEL_WIDTH), spec(FF), spec(FF), spec(FF)],
            out_specs=[
                pl.BlockSpec((shards // 2, 1, narrow, FF), lambda e, c, *_: (0, e, 0, 0))
            ]
            * 12,
            scratch_shapes=[
                pltpu.VMEM((MODEL_WIDTH, FF), f32),
                pltpu.VMEM((MODEL_WIDTH, FF), f32),
                pltpu.VMEM((FF, MODEL_WIDTH), f32),
            ],
        ),
        out_shape=[jax.ShapeDtypeStruct((shards // 2, experts, narrow, FF), bf16)] * 12,
        cost_estimate=cost(
            6 * experts * total * MODEL_WIDTH * FF,
            experts * (total * (2 * MODEL_WIDTH + 3 * FF) + 3 * MODEL_WIDTH * FF) * 2,
        ),
        compiler_params=pltpu.CompilerParams(vmem_limit_bytes=VMEM_LIMIT),
        name="expert_weights",
    )(place, rows, out_grad, hidden, gate_low, up_low)


def along_seq(value, distance, shards):
    return lax.ppermute(value, "seq", [(i, i ^ distance) for i in range(shards)])


def gather_over_seq(value, shards):
    me = lax.axis_index("seq")
    held = jnp.stack([value] + [along_seq(value, k, shards) for k in range(1, shards)])
    return jnp.stack(
        [lax.dynamic_index_in_dim(held, s ^ me, 0, keepdims=False) for s in range(shards)]
    )


def sum_over_seq(value, shards):
    me = lax.axis_index("seq")
    part = lambda j: lax.dynamic_index_in_dim(value, j ^ me, 0, keepdims=False)
    sent = along_seq(jnp.stack([part(1), part(3)]), 1, shards).astype(f32)
    passed = (part(2).astype(f32) + sent[1]).astype(value.dtype)
    return part(0).astype(f32) + sent[0] + along_seq(passed, 2, shards).astype(f32)


def swap_over(value, axes):
    return lax.all_to_all(value, axes, split_axis=0, concat_axis=0, tiled=True)


def after(value, *others):
    return lax.optimization_barrier((value,) + others)[0]


def on_device(
    shards,
    ranks,
    layer_input,
    doc_ids,
    expert_routes,
    attn_gain,
    query_weight,
    key_projection_weight,
    value_projection_weight,
    out_weight,
    ffn_gain,
    router_weight,
    gate_weight,
    up_weight,
    down_weight,
    out_cotangent,
):
    local = layer_input.shape[0]
    tokens = doc_ids.shape[1]
    copies = ranks // KEY_VALUE_HEADS
    experts = gate_weight.shape[0]
    rows = query_weight.shape[0]
    blocks = tokens // BLOCK
    rank = lax.axis_index("exp")
    me = lax.axis_index("seq")
    head_width = GROUP * HEAD_SIZE
    wide, narrow, half = MODEL_WIDTH // shards, FF // shards, MODEL_WIDTH // 2

    x_row = lax.all_gather(layer_input, "exp", axis=0, tiled=True)

    by_head = jnp.concatenate(
        [
            query_weight.reshape(rows, KEY_VALUE_HEADS, head_width),
            key_projection_weight.reshape(rows, KEY_VALUE_HEADS, HEAD_SIZE),
            value_projection_weight.reshape(rows, KEY_VALUE_HEADS, HEAD_SIZE),
        ],
        axis=2,
    )
    own_width = by_head.shape[2]
    per_row = local * TOPK // rows
    small = jnp.concatenate(
        [
            router_weight,
            attn_gain[:, None],
            ffn_gain[:, None],
            jnp.zeros((rows, -(EXPERTS + 2 + per_row) % LANES), bf16),
            expert_routes.astype(bf16).reshape(rows, per_row),
        ],
        axis=1,
    )
    to_send = jnp.concatenate(
        [
            jnp.repeat(by_head.transpose(1, 0, 2), copies, axis=0),
            jnp.broadcast_to(small[None], (ranks,) + small.shape),
        ],
        axis=2,
    )
    got = swap_over(to_send, "exp").reshape(ranks * rows, -1)
    routes_row = got[:, got.shape[1] - per_row :].reshape(tokens, TOPK)
    routes_row = routes_row.astype(jnp.int32)
    weights = gather_over_seq(got[:, : own_width + LANES], shards).reshape(MODEL_WIDTH, -1)
    own_weight = weights[:, :own_width]
    small_all = weights[:, own_width:]
    gain_one = small_all[:, EXPERTS].astype(f32)[None]
    gain_two = small_all[:, EXPERTS + 1].astype(f32)[None]
    lane = jnp.arange(LANES)[None, :]
    router_mat = jnp.where(lane < EXPERTS, small_all, 0)
    key_part = own_weight[:, head_width : head_width + HEAD_SIZE]
    value_part = own_weight[:, head_width + HEAD_SIZE :]
    wide_weight = jnp.concatenate(
        [own_weight[:, :head_width]] + [key_part] * GROUP + [value_part] * GROUP, axis=1
    )

    left_weight, right_weight = down_weight[:, :, :half], down_weight[:, :, half:]
    near_gate, near_up = along_seq(gate_weight, 1, shards), along_seq(up_weight, 2, shards)

    seg_row = doc_ids[0]
    smaller = jnp.sum(
        (seg_row[None, :] < jnp.arange(DOCS, dtype=jnp.int32)[:, None]).astype(jnp.int32), axis=1
    )
    start = jnp.sum(
        jnp.where(seg_row[None, :] == jnp.arange(DOCS)[:, None], smaller[:, None], 0), axis=0
    ).astype(jnp.int32)
    positions = (jnp.arange(tokens, dtype=jnp.int32) - start).astype(f32)
    half_head = HEAD_SIZE // 2
    inv_freq = rope_base ** (-2.0 * jnp.arange(half_head, dtype=f32) / HEAD_SIZE)
    angles = positions[:, None] * inv_freq[None, :]
    cos_half, sin_half = jnp.cos(angles), jnp.sin(angles)
    cosine = jnp.concatenate([cos_half] * (2 * GROUP), axis=1)
    sine = jnp.concatenate([-sin_half, sin_half] * GROUP, axis=1)
    first_block = start[::BLOCK] // BLOCK
    start_blocks = start.reshape(blocks, 1, BLOCK)

    first_expert = rank * experts
    own_ids = first_expert + jnp.arange(experts, dtype=jnp.int32)
    own_member = jnp.any(routes_row.T[None] == own_ids[:, None, None], axis=1)
    own_member = own_member.reshape(experts, blocks, BLOCK)
    triangle = (jnp.arange(BLOCK)[:, None] <= jnp.arange(BLOCK)[None, :]).astype(bf16)
    counts = jnp.dot(
        own_member.reshape(experts * blocks, BLOCK).astype(bf16),
        triangle,
        preferred_element_type=f32,
    ).reshape(experts, blocks, BLOCK)
    slots = jnp.where(own_member, counts.astype(jnp.int32) - 1, -1)
    group = 2
    slot_rows = (
        slots.reshape(experts, blocks // group, group, BLOCK)
        .transpose(1, 0, 2, 3)
        .reshape(blocks // group, experts * group, BLOCK)
    )
    slot_cols = jnp.pad(
        slots.reshape(experts, tokens).T, ((0, 0), (0, LANES - experts)), constant_values=-1
    )
    place = jnp.stack([first_expert, me])

    key_place = jnp.stack([me, lax.rem(rank, copies)])
    x_row, near_gate, near_up, slot_rows, slot_cols, place, key_place, routes_row = (
        lax.optimization_barrier(
            (x_row, near_gate, near_up, slot_rows, slot_cols, place, key_place, routes_row)
        )
    )
    cot_a = lax.all_gather(after(out_cotangent[:COT_EARLY], got), "exp", axis=0, tiled=True)
    out_rows = lax.all_gather(after(out_weight, got), "exp", axis=0, tiled=True)
    x_row, out_rows = lax.optimization_barrier((x_row, out_rows))
    left_weight, right_weight = lax.optimization_barrier((left_weight, right_weight, near_gate))[:2]
    near_left, near_right = along_seq(left_weight, 1, shards), along_seq(right_weight, 2, shards)
    next_left, next_right = along_seq(left_weight, 2, shards), along_seq(right_weight, 1, shards)

    normed_row, query_low, key_low, value_low, mixed_own, mixed_t, log_total = attention_forward(
        first_block, x_row, wide_weight, gain_one, cosine, sine, start_blocks
    )
    share = tokens // copies
    part = lax.rem(rank, copies) * share
    (
        mixed_own,
        cot_a,
        near_left,
        near_right,
        next_left,
        next_right,
    ) = lax.optimization_barrier(
        (mixed_own, cot_a, near_left, near_right, next_left, next_right)
    )
    mixed_part = lax.dynamic_slice_in_dim(mixed_own, part, share) if copies > 1 else mixed_own
    mixed_row = lax.all_gather(mixed_part, "exp", axis=0, tiled=True)
    cot_b = lax.all_gather(
        after(out_cotangent[COT_EARLY:], mixed_own), "exp", axis=0, tiled=True
    )
    out_mat = gather_over_seq(after(out_rows, mixed_own), shards).reshape(MODEL_WIDTH, -1)
    gate_weight, up_weight = lax.optimization_barrier((gate_weight, up_weight, near_left))[:2]
    next_gate, next_up = along_seq(gate_weight, 2, shards), along_seq(up_weight, 1, shards)
    far_left = along_seq(after(near_left, mixed_own), 2, shards)
    far_right = along_seq(after(near_right, mixed_own), 1, shards)
    mixed_row, out_mat, next_gate, next_up, far_left, far_right = lax.optimization_barrier(
        (mixed_row, out_mat, next_gate, next_up, far_left, far_right)
    )
    far_gate = along_seq(after(near_gate, next_gate), 2, shards)
    far_up = along_seq(after(near_up, next_up), 1, shards)
    mixed_row = mixed_row.reshape(KEY_VALUE_HEADS, tokens, head_width)
    (
        normed_two_row,
        probs_row,
        probs_t,
        middle,
        mixed_home,
        normed_two_home,
        probs_home,
    ) = middle_forward(rank[None], mixed_row, x_row, out_mat, gain_two, router_mat, routes_row)
    normed_two_row, far_gate, far_up = lax.optimization_barrier((normed_two_row, far_gate, far_up))
    weight_all = lax.all_gather(
        (lambda w: lax.dynamic_slice_in_dim(w, lax.rem(rank, copies) * (MODEL_WIDTH // copies), MODEL_WIDTH // copies) if copies > 1 else w)(
            after(own_weight, normed_two_row)
        ),
        "exp",
        axis=0,
        tiled=True,
    ).reshape(KEY_VALUE_HEADS, MODEL_WIDTH, own_width)

    moe_part, row_part, weigh, *kept = expert_rows(
        place,
        normed_two_row,
        cot_a,
        cot_b,
        probs_row,
        probs_t,
        slot_rows,
        slot_cols,
        [gate_weight, near_gate, next_gate, far_gate]
        + [up_weight, next_up, near_up, far_up]
        + [left_weight, near_left, next_left, far_left]
        + [right_weight, next_right, near_right, far_right],
        group,
    )
    mixed_turned = (
        mixed_home.reshape(local, shards, ranks, rows)
        .transpose(0, 2, 1, 3)
        .reshape(local, MODEL_WIDTH)
    )
    row_part, weight_all, mixed_turned = lax.optimization_barrier(
        (row_part, weight_all, mixed_turned)
    )
    row_sum = lax.psum_scatter(row_part, "exp", scatter_dimension=0, tiled=True)
    pieces = expert_weights(place, *kept, shards)
    stay, go = pieces[0::2], pieces[1::2]
    weigh_home = swap_over(
        after(weigh, go[0]).reshape(blocks // group, experts, group, BLOCK)
        .transpose(0, 2, 1, 3)
        .reshape(ranks, experts, local),
        "exp",
    )
    weigh_home = weigh_home.reshape(EXPERTS, local).T

    def first_exchange(piece, since):
        a, b = go[piece], go[3 + piece]
        if since is not None:
            a, b = after(a, since), after(b, since)
        return along_seq(a, 1, shards), along_seq(b, 2, shards)

    come_0 = first_exchange(0, None)
    row_sum, come_0, weigh_home = lax.optimization_barrier(
        (after(row_sum, go[0]), come_0, weigh_home)
    )
    come_1 = first_exchange(1, row_sum)

    out_grad = out_cotangent.astype(f32)
    probs_own = probs_home[:, :EXPERTS]
    logits_low = (
        weigh_home - probs_own * jnp.sum(weigh_home, axis=1, keepdims=True)
    ).astype(bf16)
    router_part = dot_tn(normed_two_home, logits_low)
    normed_two_grad = row_sum.astype(f32) + dot_nt(logits_low, router_mat[:, :EXPERTS])
    scale_two = lax.rsqrt(jnp.mean(middle * middle, axis=-1, keepdims=True) + eps_norm)
    gain_two_part = jnp.sum(normed_two_grad * middle * scale_two, axis=0)
    through = gain_two * normed_two_grad
    middle_grad = (
        out_grad
        + scale_two * through
        - middle * scale_two**3 * jnp.mean(middle * through, axis=-1, keepdims=True)
    )
    branch_low = middle_grad.astype(bf16)
    mixed_grad = dot_nt(branch_low, out_mat).astype(bf16)
    mixed_grad_row = swap_over(
        jnp.repeat(
            mixed_grad.reshape(local, KEY_VALUE_HEADS, head_width).transpose(1, 0, 2), copies, axis=0
        ),
        "exp",
    ).reshape(tokens, head_width)

    out_part = dot_tn(mixed_turned, branch_low).astype(bf16)
    out_part = lax.psum_scatter(out_part, "exp", scatter_dimension=0, tiled=True)
    moe_sum = lax.psum_scatter(
        after(moe_part, mixed_grad_row), "exp", scatter_dimension=0, tiled=True
    )

    mixed_grad_row, come_1 = lax.optimization_barrier((mixed_grad_row, come_1))
    come_2 = first_exchange(2, mixed_grad_row)

    come = [come_0, come_1, come_2]
    add = lambda x, y: x.astype(f32) + y.astype(f32)
    kept_parts = lambda side, n: stay[3 * side + n][0].astype(f32) + come[n][side][0].astype(f32)

    def pass_on(side, pieces, since):
        parts = [
            (stay[3 * side + n][1].astype(f32) + come[n][side][1].astype(f32)).astype(bf16)
            for n in pieces
        ]
        parts = after(jnp.stack(parts) if len(parts) > 1 else parts[0][None], since)
        return along_seq(parts, (2, 1)[side], shards)

    early_a, early_b = pass_on(0, (0,), mixed_grad_row), pass_on(1, (0,), mixed_grad_row)
    small_part = jnp.concatenate(
        [router_part, gain_two_part[:, None], jnp.zeros((MODEL_WIDTH, LANES - EXPERTS - 1), f32)],
        axis=1,
    )
    lin_low, weight_stay, weight_go = attention_backward(
        first_block,
        key_place,
        query_low,
        mixed_grad_row,
        mixed_t,
        log_total,
        start_blocks,
        cosine,
        sine,
        key_low,
        value_low,
        small_part,
        normed_row,
        shards,
        copies,
    )
    lin_home = swap_over(lin_low.reshape(ranks, local, own_width), "exp")
    weight_come = along_seq(weight_go, 1, shards)
    weight_come, come_2, early_a, early_b, out_part = lax.optimization_barrier(
        (weight_come, come_2, early_a, early_b, out_part)
    )
    come[2] = come_2
    weight_pass = along_seq(add(weight_stay[1], weight_come[1]).astype(bf16), 2, shards)
    weight_sum = (
        add(weight_stay[0], weight_come[0]) + weight_pass.astype(f32)
    ).astype(bf16)
    late_a, late_b = pass_on(0, (1, 2), weight_sum), pass_on(1, (1, 2), weight_sum)
    out_weight_grad = sum_over_seq(out_part.reshape(shards, rows, MODEL_WIDTH), shards)
    weight_sum, lin_home = lax.optimization_barrier((weight_sum, lin_home))
    weight_home = swap_over(weight_sum.reshape(ranks, rows, -1), "exp").astype(f32)
    weight_home, late_a, late_b = lax.optimization_barrier((weight_home, late_a, late_b))
    halves = [
        [
            kept_parts(side, n) + passed.astype(f32)
            for n, passed in enumerate((early[0], late[0], late[1]))
        ]
        for side, (early, late) in enumerate(((early_a, late_a), (early_b, late_b)))
    ]
    gate_grad, up_grad = (jnp.concatenate(h[:2], axis=1) for h in halves)
    down_grad = jnp.concatenate([halves[0][2], halves[1][2]], axis=2)
    tail = jnp.sum(weight_home[:, :, own_width:], axis=0)
    router_grad = tail[:, :EXPERTS]
    ffn_gain_grad = tail[:, EXPERTS]
    weight_home = jnp.sum(
        weight_home[:, :, :own_width].reshape(KEY_VALUE_HEADS, copies, rows, own_width), axis=1
    ).transpose(1, 0, 2)
    lin_home = lin_home.reshape(KEY_VALUE_HEADS, copies, local, own_width)[:, 0]
    normed_grad = dot_nt(
        lin_home.transpose(1, 0, 2).reshape(local, -1),
        weight_all.transpose(1, 0, 2).reshape(MODEL_WIDTH, -1),
    )
    inputs = layer_input.astype(f32)
    scale_one = lax.rsqrt(jnp.mean(inputs * inputs, axis=-1, keepdims=True) + eps_norm)
    through_one = gain_one * normed_grad
    input_grad = (
        middle_grad
        + scale_one * through_one
        - inputs * scale_one**3 * jnp.mean(inputs * through_one, axis=-1, keepdims=True)
    )

    query_grad = weight_home[:, :, :head_width].reshape(rows, -1)
    key_grad = weight_home[:, :, head_width : head_width + HEAD_SIZE].reshape(rows, -1)
    value_grad = weight_home[:, :, head_width + HEAD_SIZE :].reshape(rows, -1)
    attn_gain_grad = jnp.sum(weight_home * by_head.astype(f32), axis=(1, 2)) / attn_gain.astype(f32)

    layer_output = (middle + moe_sum.astype(f32)).astype(bf16)
    return (
        layer_output,
        input_grad,
        attn_gain_grad,
        query_grad,
        key_grad,
        value_grad,
        out_weight_grad,
        ffn_gain_grad,
        router_grad,
        gate_grad,
        up_grad,
        down_grad,
    )


def solution(mesh):
    tokens_2d = P(("seq", "exp"), None)
    vector = P(("seq", "exp"))
    expert = P("exp", "seq", None)
    return jax.shard_map(
        functools.partial(on_device, mesh.shape["seq"], mesh.shape["exp"]),
        mesh=mesh,
        in_specs=(
            tokens_2d,
            P("seq", None),
            tokens_2d,
            vector,
            tokens_2d,
            tokens_2d,
            tokens_2d,
            tokens_2d,
            vector,
            tokens_2d,
            expert,
            expert,
            expert,
            tokens_2d,
        ),
        out_specs=(
            tokens_2d,
            tokens_2d,
            vector,
            tokens_2d,
            tokens_2d,
            tokens_2d,
            tokens_2d,
            vector,
            tokens_2d,
            expert,
            expert,
            expert,
        ),
        check_vma=False,
    )
```

```python
import functools

import jax
import jax.numpy as jnp
from jax import lax
from jax.experimental import pallas as pl
from jax.experimental.pallas import tpu as pltpu
from jax.sharding import PartitionSpec as P

MODEL_WIDTH = 1024
QUERY_HEADS = 16
KEY_VALUE_HEADS = 8
HEAD_SIZE = 64
FF = 512
EXPERTS = 32
TOPK = 8
DOCS = 4
CAP = 128

BLOCK = 256
COT_EARLY = 80
MID = 512
SUB = 256
LANES = 128
GROUP = QUERY_HEADS // KEY_VALUE_HEADS
PACK = GROUP * HEAD_SIZE

eps_norm = 1e-06
rope_base = 10000.0
score_masked = -1e30
score_scale = HEAD_SIZE**-0.5
f32 = jnp.float32
bf16 = jnp.bfloat16
VMEM_LIMIT = 60 * 1024 * 1024


def dot_nn(a, b):
    return lax.dot_general(a, b, (((1,), (0,)), ((), ())), preferred_element_type=f32)


def dot_nt(a, b):
    return lax.dot_general(a, b, (((1,), (1,)), ((), ())), preferred_element_type=f32)


def dot_tn(a, b):
    return lax.dot_general(a, b, (((0,), (0,)), ((), ())), preferred_element_type=f32)


def swap_halves(v):
    lane = lax.broadcasted_iota(jnp.int32, v.shape, 1)
    half = HEAD_SIZE // 2
    return jnp.where(
        lane % HEAD_SIZE < half, pltpu.roll(v, PACK - half, 1), pltpu.roll(v, half, 1)
    )


def head_stack(v):
    lane = lax.broadcasted_iota(jnp.int32, v.shape, 1)
    zero = jnp.zeros_like(v)
    return jnp.concatenate(
        [jnp.where(lane < HEAD_SIZE, v, zero), jnp.where(lane >= HEAD_SIZE, v, zero)], axis=0
    )


def visible_from(block_key, block_query, start_row):
    shape = (BLOCK, GROUP * BLOCK)
    key_place = block_key * BLOCK + lax.broadcasted_iota(jnp.int32, shape, 0)
    lane = lax.broadcasted_iota(jnp.int32, shape, 1)
    query_place = block_query * BLOCK + lane % BLOCK
    return (key_place >= start_row) & (key_place <= query_place)


def attention_forward_kernel(
    first_block,
    x_ref,
    weight_ref,
    gain_ref,
    cos_ref,
    sin_ref,
    start_ref,
    normed_ref,
    query_ref,
    key_ref,
    value_ref,
    mixed_ref,
    mixed_t_ref,
    log_ref,
    key_all,
    value_all,
):
    i = pl.program_id(0)
    x = x_ref[...].astype(f32)
    normed = (
        x * lax.rsqrt(jnp.mean(x * x, axis=-1, keepdims=True) + eps_norm) * gain_ref[...]
    ).astype(bf16)
    normed_ref[...] = normed
    lin = dot_nn(normed, weight_ref[...])
    cosine, sine = cos_ref[...], sin_ref[...]
    query_lin, key_lin = lin[:, :PACK], lin[:, PACK : 2 * PACK]
    query = (query_lin * cosine + swap_halves(query_lin) * sine).astype(bf16)
    key = (key_lin * cosine + swap_halves(key_lin) * sine).astype(bf16)
    value = lin[:, 2 * PACK :].astype(bf16)
    query_ref[...] = query
    key_ref[...] = key
    value_ref[...] = value
    rows = pl.ds(pl.multiple_of(i * BLOCK, BLOCK), BLOCK)
    key_all[rows, :] = key
    value_all[rows, :] = value
    query_two = head_stack(query * jnp.asarray(score_scale, bf16))
    start_row = start_ref[0]
    start_two = jnp.concatenate([start_row] * GROUP, axis=1)

    def visit(j, carry):
        run_max, run_sum, acc = carry
        here = pl.ds(pl.multiple_of(j * BLOCK, BLOCK), BLOCK)
        scores = dot_nt(key_all[here, :], query_two)
        scores = jnp.where(visible_from(j, i, start_two), scores, score_masked)
        new_max = jnp.maximum(run_max, jnp.max(scores, axis=0, keepdims=True))
        shrink = jnp.exp(run_max - new_max)
        weights = jnp.exp(scores - new_max)
        run_sum = run_sum * shrink + jnp.sum(weights, axis=0, keepdims=True)
        acc = acc * shrink + dot_tn(value_all[here, :], weights.astype(bf16))
        return new_max, run_sum, acc

    width = GROUP * BLOCK
    run_max, run_sum, acc = lax.fori_loop(
        first_block[i],
        i + 1,
        visit,
        (
            jnp.full((1, width), score_masked, f32),
            jnp.zeros((1, width), f32),
            jnp.zeros((PACK, width), f32),
        ),
    )
    acc = acc * (1.0 / run_sum)
    mixed_t = jnp.concatenate([acc[:HEAD_SIZE, :BLOCK], acc[HEAD_SIZE:, BLOCK:]], axis=0)
    mixed_t_ref[0] = mixed_t
    mixed_ref[...] = mixed_t.T.astype(bf16)
    log_ref[0] = run_max + jnp.log(run_sum)


def attention_forward(first_block, x_row, weight, gain, cosine, sine, start):
    tokens = x_row.shape[0]
    blocks = tokens // BLOCK
    row = lambda i, *_: (i, 0)
    page = lambda i, *_: (i, 0, 0)
    whole = lambda i, *_: (0, 0)
    return pl.pallas_call(
        attention_forward_kernel,
        grid_spec=pltpu.PrefetchScalarGridSpec(
            num_scalar_prefetch=1,
            grid=(blocks,),
            in_specs=[
                pl.BlockSpec((BLOCK, MODEL_WIDTH), row),
                pl.BlockSpec(weight.shape, whole),
                pl.BlockSpec((1, MODEL_WIDTH), whole),
                pl.BlockSpec((BLOCK, PACK), row),
                pl.BlockSpec((BLOCK, PACK), row),
                pl.BlockSpec((1, 1, BLOCK), page),
            ],
            out_specs=[
                pl.BlockSpec((BLOCK, MODEL_WIDTH), row),
                pl.BlockSpec((BLOCK, PACK), row),
                pl.BlockSpec((BLOCK, PACK), row),
                pl.BlockSpec((BLOCK, PACK), row),
                pl.BlockSpec((BLOCK, PACK), row),
                pl.BlockSpec((1, PACK, BLOCK), page),
                pl.BlockSpec((1, 1, GROUP * BLOCK), page),
            ],
            scratch_shapes=[pltpu.VMEM((tokens, PACK), bf16), pltpu.VMEM((tokens, PACK), bf16)],
        ),
        out_shape=[
            jax.ShapeDtypeStruct((tokens, MODEL_WIDTH), bf16),
            jax.ShapeDtypeStruct((tokens, PACK), bf16),
            jax.ShapeDtypeStruct((tokens, PACK), bf16),
            jax.ShapeDtypeStruct((tokens, PACK), bf16),
            jax.ShapeDtypeStruct((tokens, PACK), bf16),
            jax.ShapeDtypeStruct((blocks, PACK, BLOCK), f32),
            jax.ShapeDtypeStruct((blocks, 1, GROUP * BLOCK), f32),
        ],
        cost_estimate=cost(
            tokens * (2 * MODEL_WIDTH * 3 * PACK + 8 * PACK * tokens), tokens * MODEL_WIDTH * 4
        ),
        compiler_params=pltpu.CompilerParams(vmem_limit_bytes=VMEM_LIMIT),
        name="attention_forward",
    )(first_block, x_row, weight, gain, cosine, sine, start)


def attention_backward_kernel(
    shards,
    copies,
    first_block,
    place,
    query_ref,
    grad_ref,
    mixed_t_ref,
    log_ref,
    start_ref,
    cos_ref,
    sin_ref,
    key_ref,
    value_ref,
    small_ref,
    *refs,
):
    normed_refs, (lin_grad_ref, stay_ref, go_ref, key_acc, value_acc) = refs[:shards], refs[shards:]
    i = pl.program_id(0)
    blocks = pl.num_programs(0)

    @pl.when(i == 0)
    def _():
        key_acc[...] = jnp.zeros_like(key_acc)
        value_acc[...] = jnp.zeros_like(value_acc)

    query_two = head_stack(query_ref[...] * jnp.asarray(score_scale, bf16))
    grad = grad_ref[...]
    grad_two = head_stack(grad)
    product = mixed_t_ref[0] * grad.astype(f32).T
    delta = jnp.concatenate(
        [
            jnp.sum(product[:HEAD_SIZE], axis=0, keepdims=True),
            jnp.sum(product[HEAD_SIZE:], axis=0, keepdims=True),
        ],
        axis=1,
    )
    log_total = log_ref[0]
    start_two = jnp.concatenate([start_ref[0]] * GROUP, axis=1)

    def visit(j, query_acc):
        here = pl.ds(pl.multiple_of(j * BLOCK, BLOCK), BLOCK)
        key = key_ref[here, :]
        scores = dot_nt(key, query_two)
        probs = jnp.where(visible_from(j, i, start_two), jnp.exp(scores - log_total), 0.0)
        prob_grad = dot_nt(value_ref[here, :], grad_two)
        score_grad = (probs * (prob_grad - delta)).astype(bf16)
        value_acc[here, :] += dot_nn(probs.astype(bf16), grad_two)
        key_acc[here, :] += dot_nn(score_grad, query_two)
        return query_acc + dot_tn(score_grad, key)

    query_acc = lax.fori_loop(
        first_block[i], i + 1, visit, jnp.zeros((GROUP * BLOCK, PACK), f32)
    )
    lane = lax.broadcasted_iota(jnp.int32, (BLOCK, PACK), 1)
    rotated = jnp.where(lane < HEAD_SIZE, query_acc[:BLOCK], query_acc[BLOCK:]) * score_scale
    rows = pl.ds(pl.multiple_of(i * BLOCK, BLOCK), BLOCK)
    lin_grad_ref[rows, :PACK] = (
        rotated * cos_ref[rows, :] - swap_halves(rotated) * sin_ref[rows, :]
    ).astype(bf16)

    @pl.when(i == blocks - 1)
    def _():
        def finish(b, carry):
            here = pl.ds(pl.multiple_of(b * BLOCK, BLOCK), BLOCK)
            key_sum = key_acc[here, :]
            key_sum = key_sum + pltpu.roll(key_sum, HEAD_SIZE, 1)
            value_sum = value_acc[here, :]
            value_sum = value_sum + pltpu.roll(value_sum, HEAD_SIZE, 1)
            key_lin = key_sum * cos_ref[here, :] - swap_halves(key_sum) * sin_ref[here, :]
            lin_grad_ref[here, PACK:] = jnp.where(lane < HEAD_SIZE, key_lin, value_sum).astype(bf16)
            return carry

        lax.fori_loop(0, blocks, finish, 0)
        share = lin_grad_ref.shape[0] // copies
        own = lin_grad_ref[pl.ds(pl.multiple_of(place[1] * share, share), share), :]
        wide = MODEL_WIDTH // shards
        for n, j in enumerate(exchange_order(shards, 0)):
            out = (stay_ref, go_ref)[n // (shards // 2)]
            at = n % (shards // 2)
            out[at, :, : 2 * PACK] = dot_tn(normed_refs[n][...], own).astype(bf16)
            rows = pl.ds(pl.multiple_of((j ^ place[0]) * wide, wide), wide)
            out[at, :, 2 * PACK :] = small_ref[rows, :].astype(bf16)


def attention_backward(
    first_block,
    place,
    query,
    grad,
    mixed_t,
    log_total,
    start,
    cosine,
    sine,
    key,
    value,
    small,
    normed,
    shards,
    copies,
):
    tokens = query.shape[0]
    wide = MODEL_WIDTH // shards
    part = lambda j: pl.BlockSpec(
        (tokens // copies, wide), lambda i, first, place, j=j: (place[1], j ^ place[0])
    )
    out = (shards // 2, wide, 2 * PACK + LANES)
    blocks = tokens // BLOCK
    row = lambda i, *_: (i, 0)
    page = lambda i, *_: (i, 0, 0)
    whole = lambda i, *_: (0, 0)
    return pl.pallas_call(
        functools.partial(attention_backward_kernel, shards, copies),
        grid_spec=pltpu.PrefetchScalarGridSpec(
            num_scalar_prefetch=2,
            grid=(blocks,),
            in_specs=[
                pl.BlockSpec((BLOCK, PACK), row),
                pl.BlockSpec((BLOCK, PACK), row),
                pl.BlockSpec((1, PACK, BLOCK), page),
                pl.BlockSpec((1, 1, GROUP * BLOCK), page),
                pl.BlockSpec((1, 1, BLOCK), page),
                pl.BlockSpec((tokens, PACK), whole),
                pl.BlockSpec((tokens, PACK), whole),
                pl.BlockSpec((tokens, PACK), whole),
                pl.BlockSpec((tokens, PACK), whole),
                pl.BlockSpec((MODEL_WIDTH, LANES), whole),
            ]
            + [part(j) for j in exchange_order(shards, 0)],
            out_specs=[
                pl.BlockSpec((tokens, 2 * PACK), whole),
                pl.BlockSpec(out, lambda i, *_: (0, 0, 0)),
                pl.BlockSpec(out, lambda i, *_: (0, 0, 0)),
            ],
            scratch_shapes=[pltpu.VMEM((tokens, PACK), f32), pltpu.VMEM((tokens, PACK), f32)],
        ),
        out_shape=[
            jax.ShapeDtypeStruct((tokens, 2 * PACK), bf16),
            jax.ShapeDtypeStruct(out, bf16),
            jax.ShapeDtypeStruct(out, bf16),
        ],
        cost_estimate=cost(20 * tokens * tokens * PACK, tokens * PACK * 28),
        compiler_params=pltpu.CompilerParams(vmem_limit_bytes=VMEM_LIMIT),
        name="attention_backward",
    )(
        first_block,
        place,
        query,
        grad,
        mixed_t,
        log_total,
        start,
        cosine,
        sine,
        key,
        value,
        small,
        *([normed] * shards),
    )


def middle_kernel(
    home,
    mixed_ref,
    x_ref,
    weight_ref,
    gain_ref,
    router_ref,
    routes_ref,
    normed_ref,
    probs_ref,
    probs_t_ref,
    home_middle_ref,
    home_mixed_ref,
    home_normed_ref,
    home_probs_ref,
    keep_middle,
    keep_mixed,
):
    i = pl.program_id(0)
    parts = x_ref.shape[0] // SUB
    lane = lax.broadcasted_iota(jnp.int32, (SUB, LANES), 1)
    for n in range(parts):
        here = slice(n * SUB, (n + 1) * SUB)
        mixed = jnp.concatenate([mixed_ref[h, here] for h in range(KEY_VALUE_HEADS)], axis=1)
        middle = x_ref[here].astype(f32) + dot_nn(mixed, weight_ref[...])
        normed = (
            middle
            * lax.rsqrt(jnp.mean(middle * middle, axis=-1, keepdims=True) + eps_norm)
            * gain_ref[...]
        ).astype(bf16)
        normed_ref[here] = normed
        logits = dot_nn(normed, router_ref[...])
        routes = routes_ref[here]
        member = jnp.zeros_like(logits)
        for k in range(TOPK):
            member = jnp.where(lane == routes[:, k : k + 1], 1.0, member)
        chosen = jnp.where(member > 0, logits, score_masked)
        raised = jnp.exp(chosen - jnp.max(chosen, axis=-1, keepdims=True)) * member
        probs = raised / jnp.sum(raised, axis=-1, keepdims=True)
        probs_ref[here] = probs
        probs_t_ref[:, here] = probs.T[:EXPERTS]
        keep_middle[here] = middle
        keep_mixed[here] = mixed

    @pl.when(i == home[0] * BLOCK // x_ref.shape[0])
    def _():
        at = pl.ds(pl.multiple_of(home[0] * BLOCK % x_ref.shape[0], BLOCK), BLOCK)
        home_middle_ref[...] = keep_middle[at]
        home_mixed_ref[...] = keep_mixed[at]
        home_normed_ref[...] = normed_ref[at]
        home_probs_ref[...] = probs_ref[at]


def middle_forward(home, mixed, x_row, weight, gain, router, routes):
    tokens = x_row.shape[0]
    row = lambda i, *_: (i, 0)
    whole = lambda i, *_: (0, 0)
    return pl.pallas_call(
        middle_kernel,
        grid_spec=pltpu.PrefetchScalarGridSpec(
            num_scalar_prefetch=1,
            grid=(tokens // MID,),
            in_specs=[
                pl.BlockSpec((KEY_VALUE_HEADS, MID, PACK), lambda i, *_: (0, i, 0)),
                pl.BlockSpec((MID, MODEL_WIDTH), row),
                pl.BlockSpec((MODEL_WIDTH, MODEL_WIDTH), whole),
                pl.BlockSpec((1, MODEL_WIDTH), whole),
                pl.BlockSpec((MODEL_WIDTH, LANES), whole),
                pl.BlockSpec((MID, TOPK), row),
            ],
            out_specs=[
                pl.BlockSpec((MID, MODEL_WIDTH), row),
                pl.BlockSpec((MID, LANES), row),
                pl.BlockSpec((EXPERTS, MID), lambda i, *_: (0, i)),
                pl.BlockSpec((BLOCK, MODEL_WIDTH), whole),
                pl.BlockSpec((BLOCK, MODEL_WIDTH), whole),
                pl.BlockSpec((BLOCK, MODEL_WIDTH), whole),
                pl.BlockSpec((BLOCK, LANES), whole),
            ],
            scratch_shapes=[
                pltpu.VMEM((MID, MODEL_WIDTH), f32),
                pltpu.VMEM((MID, MODEL_WIDTH), bf16),
            ],
        ),
        out_shape=[
            jax.ShapeDtypeStruct((tokens, MODEL_WIDTH), bf16),
            jax.ShapeDtypeStruct((tokens, LANES), f32),
            jax.ShapeDtypeStruct((EXPERTS, tokens), f32),
            jax.ShapeDtypeStruct((BLOCK, MODEL_WIDTH), f32),
            jax.ShapeDtypeStruct((BLOCK, MODEL_WIDTH), bf16),
            jax.ShapeDtypeStruct((BLOCK, MODEL_WIDTH), bf16),
            jax.ShapeDtypeStruct((BLOCK, LANES), f32),
        ],
        cost_estimate=cost(
            2 * tokens * MODEL_WIDTH * (MODEL_WIDTH + LANES), tokens * MODEL_WIDTH * 6
        ),
        compiler_params=pltpu.CompilerParams(vmem_limit_bytes=VMEM_LIMIT),
        name="middle_forward",
    )(home, mixed, x_row, weight, gain, router, routes)


def cost(flops, moved):
    return pl.CostEstimate(flops=int(flops), transcendentals=0, bytes_accessed=int(moved))


def column_of(values, lane_wanted):
    lane = lax.broadcasted_iota(jnp.int32, values.shape, 1)
    return jnp.sum(
        jnp.where(lane == lane_wanted, values, jnp.zeros_like(values)), axis=-1, keepdims=True
    )


def expert_rows_kernel(shards, experts, group, place, *refs):
    normed_ref, cot_a_ref, cot_b_ref, probs_ref, probs_t_ref, slot_row_ref, slot_col_ref = refs[:7]
    weight_refs = [refs[7 + n * shards : 7 + (n + 1) * shards] for n in range(4)]
    (
        moe_ref,
        row_ref,
        weigh_ref,
        rows_ref,
        out_grad_ref,
        hidden_ref,
        gate_low_ref,
        up_low_ref,
        gate_all,
        up_all,
        down_all,
        out_all,
        back_all,
        sems,
    ) = refs[7 + 4 * shards :]
    first_expert, me = place[0], place[1]
    wide, narrow = MODEL_WIDTH // shards, FF // shards
    half = MODEL_WIDTH // 2

    def copies(e):
        made = []
        for j in range(shards):
            tall = pl.ds(pl.multiple_of((j ^ me) * wide, wide), wide)
            short = pl.ds(pl.multiple_of((j ^ me) * narrow, narrow), narrow)
            places = (
                gate_all.at[e, tall, :],
                up_all.at[e, tall, :],
                down_all.at[e, short, :half],
                down_all.at[e, short, half:],
            )
            for n in range(4):
                made.append(
                    pltpu.make_async_copy(weight_refs[n][j].at[e], places[n], sems.at[e, 4 * j + n])
                )
        return made

    @pl.when(pl.program_id(0) == 0)
    def _():
        for e in range(experts):
            for copy in copies(e):
                copy.start()

    slot_place = lax.broadcasted_iota(jnp.int32, (CAP, BLOCK), 0)
    slot_lane = lax.broadcasted_iota(jnp.int32, (BLOCK, CAP), 1)
    early, late = COT_EARLY, BLOCK - COT_EARLY
    cots = [
        jnp.concatenate(
            [
                cot_a_ref[b * early : (b + 1) * early, :],
                cot_b_ref[b * late : (b + 1) * late, :],
            ],
            axis=0,
        )
        for b in range(group)
    ]
    for e in range(experts):

        @pl.when(pl.program_id(0) == 0)
        def _():
            for copy in copies(e):
                copy.wait()

        picked, cot_picked = [], []
        hits = []
        for b in range(group):
            hit = slot_place == slot_row_ref[0, e * group + b : e * group + b + 1, :]
            hits.append(hit)
            pick = hit.astype(f32).astype(bf16)
            prob_row = probs_t_ref[pl.ds(first_expert + e, 1), b * BLOCK : (b + 1) * BLOCK]
            prob_slot = jnp.sum(jnp.where(hit, prob_row, 0.0), axis=-1, keepdims=True)
            picked.append(dot_nn(pick, normed_ref[b * BLOCK : (b + 1) * BLOCK, :]).astype(bf16))
            cot_picked.append((dot_nn(pick, cots[b]) * prob_slot).astype(bf16))
        rows = jnp.concatenate(picked, axis=0)
        out_grad = jnp.concatenate(cot_picked, axis=0)
        rows_ref[e] = rows
        out_grad_ref[e] = out_grad
        gate_pre = dot_nn(rows, gate_all[e])
        up_pre = dot_nn(rows, up_all[e])
        hidden_grad = dot_nt(out_grad, down_all[e])
        logistic = 1.0 / (1.0 + jnp.exp(-gate_pre))
        silu = gate_pre * logistic
        hidden = (silu * up_pre).astype(bf16)
        gate_low = (
            hidden_grad * up_pre * (logistic * (1.0 + gate_pre * (1.0 - logistic)))
        ).astype(bf16)
        up_low = (hidden_grad * silu).astype(bf16)
        hidden_ref[e] = hidden
        gate_low_ref[e] = gate_low
        up_low_ref[e] = up_low
        weigh = jnp.sum(hidden_grad * hidden.astype(f32), axis=-1, keepdims=True)
        out = dot_nn(hidden, down_all[e]).astype(bf16)
        row_grad = (dot_nt(gate_low, gate_all[e]) + dot_nt(up_low, up_all[e])).astype(bf16)
        for b in range(group):
            inside = slice(b * CAP, (b + 1) * CAP)
            out_all[b, e * CAP : (e + 1) * CAP, :] = out[inside]
            back_all[b, e * CAP : (e + 1) * CAP, :] = row_grad[inside]
            weigh_ref[0, e * group + b : e * group + b + 1, :] = jnp.sum(
                jnp.where(hits[b], weigh[inside], 0.0), axis=0, keepdims=True
            )
    for b in range(group):
        tokens = slice(b * BLOCK, (b + 1) * BLOCK)
        slot_cols, probs = slot_col_ref[tokens, :], probs_ref[tokens, :]
        plain, scaled = [], []
        for e in range(experts):
            hit = slot_lane == column_of(slot_cols, e)
            plain.append(hit.astype(f32).astype(bf16))
            scaled.append(jnp.where(hit, column_of(probs, first_expert + e), 0.0).astype(bf16))
        moe_ref[tokens, :] = dot_nn(jnp.concatenate(scaled, axis=1), out_all[b]).astype(bf16)
        row_ref[tokens, :] = dot_nn(jnp.concatenate(plain, axis=1), back_all[b]).astype(bf16)


def expert_rows(place, normed, cot_a, cot_b, probs, probs_t, slot_rows, slot_cols, weights, group):
    tokens = normed.shape[0]
    shards, experts = len(weights) // 4, weights[0].shape[0]
    span, slots = group * BLOCK, group * CAP
    steps = tokens // span
    row = lambda g, *_: (g, 0)
    page = lambda g, *_: (g, 0, 0)
    spread = lambda g, *_: (0, g, 0)
    total = tokens // BLOCK * CAP
    return pl.pallas_call(
        functools.partial(expert_rows_kernel, shards, experts, group),
        grid_spec=pltpu.PrefetchScalarGridSpec(
            num_scalar_prefetch=1,
            grid=(steps,),
            in_specs=[
                pl.BlockSpec((span, MODEL_WIDTH), row),
                pl.BlockSpec((group * COT_EARLY, MODEL_WIDTH), row),
                pl.BlockSpec((group * (BLOCK - COT_EARLY), MODEL_WIDTH), row),
                pl.BlockSpec((span, LANES), row),
                pl.BlockSpec((EXPERTS, span), lambda g, *_: (0, g)),
                pl.BlockSpec((1, experts * group, BLOCK), page),
                pl.BlockSpec((span, LANES), row),
            ]
            + [pl.BlockSpec(memory_space=pl.ANY)] * (4 * shards),
            out_specs=[
                pl.BlockSpec((span, MODEL_WIDTH), row),
                pl.BlockSpec((span, MODEL_WIDTH), row),
                pl.BlockSpec((1, experts * group, BLOCK), page),
                pl.BlockSpec((experts, slots, MODEL_WIDTH), spread),
                pl.BlockSpec((experts, slots, MODEL_WIDTH), spread),
                pl.BlockSpec((experts, slots, FF), spread),
                pl.BlockSpec((experts, slots, FF), spread),
                pl.BlockSpec((experts, slots, FF), spread),
            ],
            scratch_shapes=[
                pltpu.VMEM((experts, MODEL_WIDTH, FF), bf16),
                pltpu.VMEM((experts, MODEL_WIDTH, FF), bf16),
                pltpu.VMEM((experts, FF, MODEL_WIDTH), bf16),
                pltpu.VMEM((group, experts * CAP, MODEL_WIDTH), bf16),
                pltpu.VMEM((group, experts * CAP, MODEL_WIDTH), bf16),
                pltpu.SemaphoreType.DMA((experts, 4 * shards)),
            ],
        ),
        out_shape=[
            jax.ShapeDtypeStruct((tokens, MODEL_WIDTH), bf16),
            jax.ShapeDtypeStruct((tokens, MODEL_WIDTH), bf16),
            jax.ShapeDtypeStruct((steps, experts * group, BLOCK), f32),
            jax.ShapeDtypeStruct((experts, total, MODEL_WIDTH), bf16),
            jax.ShapeDtypeStruct((experts, total, MODEL_WIDTH), bf16),
            jax.ShapeDtypeStruct((experts, total, FF), bf16),
            jax.ShapeDtypeStruct((experts, total, FF), bf16),
            jax.ShapeDtypeStruct((experts, total, FF), bf16),
        ],
        cost_estimate=cost(
            12 * experts * total * MODEL_WIDTH * FF + 8 * experts * total * MODEL_WIDTH * BLOCK,
            experts * (3 * MODEL_WIDTH * FF + total * (2 * MODEL_WIDTH + 3 * FF)) * 2
            + tokens * MODEL_WIDTH * 8,
        ),
        compiler_params=pltpu.CompilerParams(vmem_limit_bytes=VMEM_LIMIT),
        name="expert_rows",
    )(place, normed, cot_a, cot_b, probs, probs_t, slot_rows, slot_cols, *weights)


def expert_weights_kernel(shards, place, *refs):
    rows_ref, out_grad_ref, hidden_ref, gate_low_ref, up_low_ref = refs[:5]
    outs, (gate_acc, up_acc, down_acc) = refs[5:17], refs[17:]
    me, c = place[1], pl.program_id(1)
    rows = rows_ref[0]
    for acc, left, right in (
        (gate_acc, rows, gate_low_ref[0]),
        (up_acc, rows, up_low_ref[0]),
        (down_acc, hidden_ref[0], out_grad_ref[0]),
    ):
        part = dot_tn(left, right)

        @pl.when(c == 0)
        def _():
            acc[...] = part

        @pl.when(c > 0)
        def _():
            acc[...] += part

    wide, narrow = MODEL_WIDTH // shards, FF // shards
    half = MODEL_WIDTH // 2

    @pl.when(c == pl.num_programs(1) - 1)
    def _():
        for side in range(2):
            square = (gate_acc, up_acc)[side]
            order = exchange_order(shards, side)
            for n, j in enumerate(order):
                kind, at = divmod(n, shards // 2)
                base = (j ^ me) * wide
                low = pl.ds(pl.multiple_of(base, narrow), narrow)
                high = pl.ds(pl.multiple_of(base + narrow, narrow), narrow)
                short = pl.ds(pl.multiple_of((j ^ me) * narrow, narrow), narrow)
                pieces = (
                    square[low, :],
                    square[high, :],
                    down_acc[short, side * half : (side + 1) * half],
                )
                for piece, value in enumerate(pieces):
                    outs[6 * side + 2 * piece + kind][at, 0] = value.astype(bf16)


def exchange_order(shards, side):
    first = (1, 2)[side]
    stay = [j for j in range(shards) if not j & first]
    return stay + [j ^ first for j in stay]


def expert_weights(place, rows, out_grad, hidden, gate_low, up_low, shards):
    experts, total = rows.shape[:2]
    chunk = min(total, 1024)
    narrow = FF // shards
    spec = lambda width: pl.BlockSpec((1, chunk, width), lambda e, c, *_: (e, c, 0))
    return pl.pallas_call(
        functools.partial(expert_weights_kernel, shards),
        grid_spec=pltpu.PrefetchScalarGridSpec(
            num_scalar_prefetch=1,
            grid=(experts, total // chunk),
            in_specs=[spec(MODEL_WIDTH), spec(MODEL_WIDTH), spec(FF), spec(FF), spec(FF)],
            out_specs=[
                pl.BlockSpec((shards // 2, 1, narrow, FF), lambda e, c, *_: (0, e, 0, 0))
            ]
            * 12,
            scratch_shapes=[
                pltpu.VMEM((MODEL_WIDTH, FF), f32),
                pltpu.VMEM((MODEL_WIDTH, FF), f32),
                pltpu.VMEM((FF, MODEL_WIDTH), f32),
            ],
        ),
        out_shape=[jax.ShapeDtypeStruct((shards // 2, experts, narrow, FF), bf16)] * 12,
        cost_estimate=cost(
            6 * experts * total * MODEL_WIDTH * FF,
            experts * (total * (2 * MODEL_WIDTH + 3 * FF) + 3 * MODEL_WIDTH * FF) * 2,
        ),
        compiler_params=pltpu.CompilerParams(vmem_limit_bytes=VMEM_LIMIT),
        name="expert_weights",
    )(place, rows, out_grad, hidden, gate_low, up_low)


def along_seq(value, distance, shards):
    return lax.ppermute(value, "seq", [(i, i ^ distance) for i in range(shards)])


def gather_over_seq(value, shards):
    me = lax.axis_index("seq")
    held = jnp.stack([value] + [along_seq(value, k, shards) for k in range(1, shards)])
    return jnp.stack(
        [lax.dynamic_index_in_dim(held, s ^ me, 0, keepdims=False) for s in range(shards)]
    )


def sum_over_seq(value, shards):
    me = lax.axis_index("seq")
    part = lambda j: lax.dynamic_index_in_dim(value, j ^ me, 0, keepdims=False)
    sent = along_seq(jnp.stack([part(1), part(3)]), 1, shards).astype(f32)
    passed = (part(2).astype(f32) + sent[1]).astype(value.dtype)
    return part(0).astype(f32) + sent[0] + along_seq(passed, 2, shards).astype(f32)


def swap_over(value, axes):
    return lax.all_to_all(value, axes, split_axis=0, concat_axis=0, tiled=True)


def after(value, *others):
    return lax.optimization_barrier((value,) + others)[0]


def on_device(
    shards,
    ranks,
    layer_input,
    doc_ids,
    expert_routes,
    attn_gain,
    query_weight,
    key_projection_weight,
    value_projection_weight,
    out_weight,
    ffn_gain,
    router_weight,
    gate_weight,
    up_weight,
    down_weight,
    out_cotangent,
):
    local = layer_input.shape[0]
    tokens = doc_ids.shape[1]
    copies = ranks // KEY_VALUE_HEADS
    experts = gate_weight.shape[0]
    rows = query_weight.shape[0]
    blocks = tokens // BLOCK
    rank = lax.axis_index("exp")
    me = lax.axis_index("seq")
    head_width = GROUP * HEAD_SIZE
    wide, narrow, half = MODEL_WIDTH // shards, FF // shards, MODEL_WIDTH // 2

    x_row = lax.all_gather(layer_input, "exp", axis=0, tiled=True)

    by_head = jnp.concatenate(
        [
            query_weight.reshape(rows, KEY_VALUE_HEADS, head_width),
            key_projection_weight.reshape(rows, KEY_VALUE_HEADS, HEAD_SIZE),
            value_projection_weight.reshape(rows, KEY_VALUE_HEADS, HEAD_SIZE),
        ],
        axis=2,
    )
    own_width = by_head.shape[2]
    per_row = local * TOPK // rows
    small = jnp.concatenate(
        [
            router_weight,
            attn_gain[:, None],
            ffn_gain[:, None],
            jnp.zeros((rows, -(EXPERTS + 2 + per_row) % LANES), bf16),
            expert_routes.astype(bf16).reshape(rows, per_row),
        ],
        axis=1,
    )
    to_send = jnp.concatenate(
        [
            jnp.repeat(by_head.transpose(1, 0, 2), copies, axis=0),
            jnp.broadcast_to(small[None], (ranks,) + small.shape),
        ],
        axis=2,
    )
    got = swap_over(to_send, "exp").reshape(ranks * rows, -1)
    routes_row = got[:, got.shape[1] - per_row :].reshape(tokens, TOPK)
    routes_row = routes_row.astype(jnp.int32)
    weights = gather_over_seq(got[:, : own_width + LANES], shards).reshape(MODEL_WIDTH, -1)
    own_weight = weights[:, :own_width]
    small_all = weights[:, own_width:]
    gain_one = small_all[:, EXPERTS].astype(f32)[None]
    gain_two = small_all[:, EXPERTS + 1].astype(f32)[None]
    lane = jnp.arange(LANES)[None, :]
    router_mat = jnp.where(lane < EXPERTS, small_all, 0)
    key_part = own_weight[:, head_width : head_width + HEAD_SIZE]
    value_part = own_weight[:, head_width + HEAD_SIZE :]
    wide_weight = jnp.concatenate(
        [own_weight[:, :head_width]] + [key_part] * GROUP + [value_part] * GROUP, axis=1
    )

    left_weight, right_weight = down_weight[:, :, :half], down_weight[:, :, half:]
    near_gate, near_up = along_seq(gate_weight, 1, shards), along_seq(up_weight, 2, shards)

    seg_row = doc_ids[0]
    smaller = jnp.sum(
        (seg_row[None, :] < jnp.arange(DOCS, dtype=jnp.int32)[:, None]).astype(jnp.int32), axis=1
    )
    start = jnp.sum(
        jnp.where(seg_row[None, :] == jnp.arange(DOCS)[:, None], smaller[:, None], 0), axis=0
    ).astype(jnp.int32)
    positions = (jnp.arange(tokens, dtype=jnp.int32) - start).astype(f32)
    half_head = HEAD_SIZE // 2
    inv_freq = rope_base ** (-2.0 * jnp.arange(half_head, dtype=f32) / HEAD_SIZE)
    angles = positions[:, None] * inv_freq[None, :]
    cos_half, sin_half = jnp.cos(angles), jnp.sin(angles)
    cosine = jnp.concatenate([cos_half] * (2 * GROUP), axis=1)
    sine = jnp.concatenate([-sin_half, sin_half] * GROUP, axis=1)
    first_block = start[::BLOCK] // BLOCK
    start_blocks = start.reshape(blocks, 1, BLOCK)

    first_expert = rank * experts
    own_ids = first_expert + jnp.arange(experts, dtype=jnp.int32)
    own_member = jnp.any(routes_row.T[None] == own_ids[:, None, None], axis=1)
    own_member = own_member.reshape(experts, blocks, BLOCK)
    triangle = (jnp.arange(BLOCK)[:, None] <= jnp.arange(BLOCK)[None, :]).astype(bf16)
    counts = jnp.dot(
        own_member.reshape(experts * blocks, BLOCK).astype(bf16),
        triangle,
        preferred_element_type=f32,
    ).reshape(experts, blocks, BLOCK)
    slots = jnp.where(own_member, counts.astype(jnp.int32) - 1, -1)
    group = 2
    slot_rows = (
        slots.reshape(experts, blocks // group, group, BLOCK)
        .transpose(1, 0, 2, 3)
        .reshape(blocks // group, experts * group, BLOCK)
    )
    slot_cols = jnp.pad(
        slots.reshape(experts, tokens).T, ((0, 0), (0, LANES - experts)), constant_values=-1
    )
    place = jnp.stack([first_expert, me])

    key_place = jnp.stack([me, lax.rem(rank, copies)])
    x_row, near_gate, near_up, slot_rows, slot_cols, place, key_place, routes_row = (
        lax.optimization_barrier(
            (x_row, near_gate, near_up, slot_rows, slot_cols, place, key_place, routes_row)
        )
    )
    cot_a = lax.all_gather(after(out_cotangent[:COT_EARLY], got), "exp", axis=0, tiled=True)
    out_rows = lax.all_gather(after(out_weight, got), "exp", axis=0, tiled=True)
    x_row, out_rows = lax.optimization_barrier((x_row, out_rows))
    left_weight, right_weight = lax.optimization_barrier((left_weight, right_weight, near_gate))[:2]
    near_left, near_right = along_seq(left_weight, 1, shards), along_seq(right_weight, 2, shards)
    next_left, next_right = along_seq(left_weight, 2, shards), along_seq(right_weight, 1, shards)

    normed_row, query_low, key_low, value_low, mixed_own, mixed_t, log_total = attention_forward(
        first_block, x_row, wide_weight, gain_one, cosine, sine, start_blocks
    )
    share = tokens // copies
    part = lax.rem(rank, copies) * share
    (
        mixed_own,
        cot_a,
        near_left,
        near_right,
        next_left,
        next_right,
    ) = lax.optimization_barrier(
        (mixed_own, cot_a, near_left, near_right, next_left, next_right)
    )
    mixed_part = lax.dynamic_slice_in_dim(mixed_own, part, share) if copies > 1 else mixed_own
    mixed_row = lax.all_gather(mixed_part, "exp", axis=0, tiled=True)
    cot_b = lax.all_gather(
        after(out_cotangent[COT_EARLY:], mixed_own), "exp", axis=0, tiled=True
    )
    out_mat = gather_over_seq(after(out_rows, mixed_own), shards).reshape(MODEL_WIDTH, -1)
    gate_weight, up_weight = lax.optimization_barrier((gate_weight, up_weight, near_left))[:2]
    next_gate, next_up = along_seq(gate_weight, 2, shards), along_seq(up_weight, 1, shards)
    far_left = along_seq(after(near_left, mixed_own), 2, shards)
    far_right = along_seq(after(near_right, mixed_own), 1, shards)
    mixed_row, out_mat, next_gate, next_up, far_left, far_right = lax.optimization_barrier(
        (mixed_row, out_mat, next_gate, next_up, far_left, far_right)
    )
    far_gate = along_seq(after(near_gate, next_gate), 2, shards)
    far_up = along_seq(after(near_up, next_up), 1, shards)
    mixed_row = mixed_row.reshape(KEY_VALUE_HEADS, tokens, head_width)
    (
        normed_two_row,
        probs_row,
        probs_t,
        middle,
        mixed_home,
        normed_two_home,
        probs_home,
    ) = middle_forward(rank[None], mixed_row, x_row, out_mat, gain_two, router_mat, routes_row)
    normed_two_row, far_gate, far_up = lax.optimization_barrier((normed_two_row, far_gate, far_up))
    weight_all = lax.all_gather(
        (lambda w: lax.dynamic_slice_in_dim(w, lax.rem(rank, copies) * (MODEL_WIDTH // copies), MODEL_WIDTH // copies) if copies > 1 else w)(
            after(own_weight, normed_two_row)
        ),
        "exp",
        axis=0,
        tiled=True,
    ).reshape(KEY_VALUE_HEADS, MODEL_WIDTH, own_width)

    moe_part, row_part, weigh, *kept = expert_rows(
        place,
        normed_two_row,
        cot_a,
        cot_b,
        probs_row,
        probs_t,
        slot_rows,
        slot_cols,
        [gate_weight, near_gate, next_gate, far_gate]
        + [up_weight, next_up, near_up, far_up]
        + [left_weight, near_left, next_left, far_left]
        + [right_weight, next_right, near_right, far_right],
        group,
    )
    mixed_turned = (
        mixed_home.reshape(local, shards, ranks, rows)
        .transpose(0, 2, 1, 3)
        .reshape(local, MODEL_WIDTH)
    )
    row_part, weight_all, mixed_turned = lax.optimization_barrier(
        (row_part, weight_all, mixed_turned)
    )
    row_sum = lax.psum_scatter(row_part, "exp", scatter_dimension=0, tiled=True)
    pieces = expert_weights(place, *kept, shards)
    stay, go = pieces[0::2], pieces[1::2]
    weigh_home = swap_over(
        after(weigh, go[0]).reshape(blocks // group, experts, group, BLOCK)
        .transpose(0, 2, 1, 3)
        .reshape(ranks, experts, local),
        "exp",
    )
    weigh_home = weigh_home.reshape(EXPERTS, local).T

    def first_exchange(piece, since):
        a, b = go[piece], go[3 + piece]
        if since is not None:
            a, b = after(a, since), after(b, since)
        return along_seq(a, 1, shards), along_seq(b, 2, shards)

    come_0 = first_exchange(0, None)
    row_sum, come_0, weigh_home = lax.optimization_barrier(
        (after(row_sum, go[0]), come_0, weigh_home)
    )
    come_1 = first_exchange(1, row_sum)

    out_grad = out_cotangent.astype(f32)
    probs_own = probs_home[:, :EXPERTS]
    logits_low = (
        weigh_home - probs_own * jnp.sum(weigh_home, axis=1, keepdims=True)
    ).astype(bf16)
    router_part = dot_tn(normed_two_home, logits_low)
    normed_two_grad = row_sum.astype(f32) + dot_nt(logits_low, router_mat[:, :EXPERTS])
    scale_two = lax.rsqrt(jnp.mean(middle * middle, axis=-1, keepdims=True) + eps_norm)
    gain_two_part = jnp.sum(normed_two_grad * middle * scale_two, axis=0)
    through = gain_two * normed_two_grad
    middle_grad = (
        out_grad
        + scale_two * through
        - middle * scale_two**3 * jnp.mean(middle * through, axis=-1, keepdims=True)
    )
    branch_low = middle_grad.astype(bf16)
    mixed_grad = dot_nt(branch_low, out_mat).astype(bf16)
    mixed_grad_row = swap_over(
        jnp.repeat(
            mixed_grad.reshape(local, KEY_VALUE_HEADS, head_width).transpose(1, 0, 2), copies, axis=0
        ),
        "exp",
    ).reshape(tokens, head_width)

    out_part = dot_tn(mixed_turned, branch_low).astype(bf16)
    out_part = lax.psum_scatter(out_part, "exp", scatter_dimension=0, tiled=True)
    moe_sum = lax.psum_scatter(
        after(moe_part, mixed_grad_row), "exp", scatter_dimension=0, tiled=True
    )

    mixed_grad_row, come_1 = lax.optimization_barrier((mixed_grad_row, come_1))
    come_2 = first_exchange(2, mixed_grad_row)

    come = [come_0, come_1, come_2]
    add = lambda x, y: x.astype(f32) + y.astype(f32)
    kept_parts = lambda side, n: stay[3 * side + n][0].astype(f32) + come[n][side][0].astype(f32)

    def pass_on(side, pieces, since):
        parts = [
            (stay[3 * side + n][1].astype(f32) + come[n][side][1].astype(f32)).astype(bf16)
            for n in pieces
        ]
        parts = after(jnp.stack(parts) if len(parts) > 1 else parts[0][None], since)
        return along_seq(parts, (2, 1)[side], shards)

    early_a, early_b = pass_on(0, (0,), mixed_grad_row), pass_on(1, (0,), mixed_grad_row)
    small_part = jnp.concatenate(
        [router_part, gain_two_part[:, None], jnp.zeros((MODEL_WIDTH, LANES - EXPERTS - 1), f32)],
        axis=1,
    )
    lin_low, weight_stay, weight_go = attention_backward(
        first_block,
        key_place,
        query_low,
        mixed_grad_row,
        mixed_t,
        log_total,
        start_blocks,
        cosine,
        sine,
        key_low,
        value_low,
        small_part,
        normed_row,
        shards,
        copies,
    )
    lin_home = swap_over(lin_low.reshape(ranks, local, own_width), "exp")
    weight_come = along_seq(weight_go, 1, shards)
    weight_come, come_2, early_a, early_b, out_part = lax.optimization_barrier(
        (weight_come, come_2, early_a, early_b, out_part)
    )
    come[2] = come_2
    weight_pass = along_seq(add(weight_stay[1], weight_come[1]).astype(bf16), 2, shards)
    weight_sum = (
        add(weight_stay[0], weight_come[0]) + weight_pass.astype(f32)
    ).astype(bf16)
    late_a, late_b = pass_on(0, (1, 2), weight_sum), pass_on(1, (1, 2), weight_sum)
    out_weight_grad = sum_over_seq(out_part.reshape(shards, rows, MODEL_WIDTH), shards)
    weight_sum, lin_home = lax.optimization_barrier((weight_sum, lin_home))
    weight_home = swap_over(weight_sum.reshape(ranks, rows, -1), "exp").astype(f32)
    weight_home, late_a, late_b = lax.optimization_barrier((weight_home, late_a, late_b))
    halves = [
        [
            kept_parts(side, n) + passed.astype(f32)
            for n, passed in enumerate((early[0], late[0], late[1]))
        ]
        for side, (early, late) in enumerate(((early_a, late_a), (early_b, late_b)))
    ]
    gate_grad, up_grad = (jnp.concatenate(h[:2], axis=1) for h in halves)
    down_grad = jnp.concatenate([halves[0][2], halves[1][2]], axis=2)
    tail = jnp.sum(weight_home[:, :, own_width:], axis=0)
    router_grad = tail[:, :EXPERTS]
    ffn_gain_grad = tail[:, EXPERTS]
    weight_home = jnp.sum(
        weight_home[:, :, :own_width].reshape(KEY_VALUE_HEADS, copies, rows, own_width), axis=1
    ).transpose(1, 0, 2)
    lin_home = lin_home.reshape(KEY_VALUE_HEADS, copies, local, own_width)[:, 0]
    normed_grad = dot_nt(
        lin_home.transpose(1, 0, 2).reshape(local, -1),
        weight_all.transpose(1, 0, 2).reshape(MODEL_WIDTH, -1),
    )
    inputs = layer_input.astype(f32)
    scale_one = lax.rsqrt(jnp.mean(inputs * inputs, axis=-1, keepdims=True) + eps_norm)
    through_one = gain_one * normed_grad
    input_grad = (
        middle_grad
        + scale_one * through_one
        - inputs * scale_one**3 * jnp.mean(inputs * through_one, axis=-1, keepdims=True)
    )

    query_grad = weight_home[:, :, :head_width].reshape(rows, -1)
    key_grad = weight_home[:, :, head_width : head_width + HEAD_SIZE].reshape(rows, -1)
    value_grad = weight_home[:, :, head_width + HEAD_SIZE :].reshape(rows, -1)
    attn_gain_grad = jnp.sum(weight_home * by_head.astype(f32), axis=(1, 2)) / attn_gain.astype(f32)

    layer_output = (middle + moe_sum.astype(f32)).astype(bf16)
    return (
        layer_output,
        input_grad,
        attn_gain_grad,
        query_grad,
        key_grad,
        value_grad,
        out_weight_grad,
        ffn_gain_grad,
        router_grad,
        gate_grad,
        up_grad,
        down_grad,
    )


def solution(mesh):
    tokens_2d = P(("seq", "exp"), None)
    vector = P(("seq", "exp"))
    expert = P("exp", "seq", None)
    return jax.shard_map(
        functools.partial(on_device, mesh.shape["seq"], mesh.shape["exp"]),
        mesh=mesh,
        in_specs=(
            tokens_2d,
            P("seq", None),
            tokens_2d,
            vector,
            tokens_2d,
            tokens_2d,
            tokens_2d,
            tokens_2d,
            vector,
            tokens_2d,
            expert,
            expert,
            expert,
            tokens_2d,
        ),
        out_specs=(
            tokens_2d,
            tokens_2d,
            vector,
            tokens_2d,
            tokens_2d,
            tokens_2d,
            tokens_2d,
            vector,
            tokens_2d,
            expert,
            expert,
            expert,
        ),
        check_vma=False,
    )
```

```python
import functools

import jax
import jax.numpy as jnp
from jax import lax
from jax.experimental import pallas as pl
from jax.experimental.pallas import tpu as pltpu
from jax.sharding import PartitionSpec as P

MODEL_WIDTH = 1024
QUERY_HEADS = 16
KEY_VALUE_HEADS = 8
HEAD_SIZE = 64
FF = 512
EXPERTS = 32
TOPK = 8
DOCS = 4
CAP = 128

BLOCK = 256
COT_EARLY = 64
MID = 512
SUB = 256
LANES = 128
GROUP = QUERY_HEADS // KEY_VALUE_HEADS
PACK = GROUP * HEAD_SIZE

eps_norm = 1e-06
rope_base = 10000.0
score_masked = -1e30
score_scale = HEAD_SIZE**-0.5
f32 = jnp.float32
bf16 = jnp.bfloat16
VMEM_LIMIT = 60 * 1024 * 1024


def dot_nn(a, b):
    return lax.dot_general(a, b, (((1,), (0,)), ((), ())), preferred_element_type=f32)


def dot_nt(a, b):
    return lax.dot_general(a, b, (((1,), (1,)), ((), ())), preferred_element_type=f32)


def dot_tn(a, b):
    return lax.dot_general(a, b, (((0,), (0,)), ((), ())), preferred_element_type=f32)


def swap_halves(v):
    lane = lax.broadcasted_iota(jnp.int32, v.shape, 1)
    half = HEAD_SIZE // 2
    return jnp.where(
        lane % HEAD_SIZE < half, pltpu.roll(v, PACK - half, 1), pltpu.roll(v, half, 1)
    )


def head_stack(v):
    lane = lax.broadcasted_iota(jnp.int32, v.shape, 1)
    zero = jnp.zeros_like(v)
    return jnp.concatenate(
        [jnp.where(lane < HEAD_SIZE, v, zero), jnp.where(lane >= HEAD_SIZE, v, zero)], axis=0
    )


def visible_from(block_key, block_query, start_row):
    shape = (BLOCK, GROUP * BLOCK)
    key_place = block_key * BLOCK + lax.broadcasted_iota(jnp.int32, shape, 0)
    lane = lax.broadcasted_iota(jnp.int32, shape, 1)
    query_place = block_query * BLOCK + lane % BLOCK
    return (key_place >= start_row) & (key_place <= query_place)


def attention_forward_kernel(
    first_block,
    x_ref,
    weight_ref,
    gain_ref,
    cos_ref,
    sin_ref,
    start_ref,
    normed_ref,
    query_ref,
    key_ref,
    value_ref,
    mixed_ref,
    mixed_t_ref,
    log_ref,
    key_all,
    value_all,
):
    i = pl.program_id(0)
    x = x_ref[...].astype(f32)
    normed = (
        x * lax.rsqrt(jnp.mean(x * x, axis=-1, keepdims=True) + eps_norm) * gain_ref[...]
    ).astype(bf16)
    normed_ref[...] = normed
    lin = dot_nn(normed, weight_ref[...])
    cosine, sine = cos_ref[...], sin_ref[...]
    query_lin, key_lin = lin[:, :PACK], lin[:, PACK : 2 * PACK]
    query = (query_lin * cosine + swap_halves(query_lin) * sine).astype(bf16)
    key = (key_lin * cosine + swap_halves(key_lin) * sine).astype(bf16)
    value = lin[:, 2 * PACK :].astype(bf16)
    query_ref[...] = query
    key_ref[...] = key
    value_ref[...] = value
    rows = pl.ds(pl.multiple_of(i * BLOCK, BLOCK), BLOCK)
    key_all[rows, :] = key
    value_all[rows, :] = value
    query_two = head_stack(query * jnp.asarray(score_scale, bf16))
    start_row = start_ref[0]
    start_two = jnp.concatenate([start_row] * GROUP, axis=1)

    def visit(j, carry):
        run_max, run_sum, acc = carry
        here = pl.ds(pl.multiple_of(j * BLOCK, BLOCK), BLOCK)
        scores = dot_nt(key_all[here, :], query_two)
        scores = jnp.where(visible_from(j, i, start_two), scores, score_masked)
        new_max = jnp.maximum(run_max, jnp.max(scores, axis=0, keepdims=True))
        shrink = jnp.exp(run_max - new_max)
        weights = jnp.exp(scores - new_max)
        run_sum = run_sum * shrink + jnp.sum(weights, axis=0, keepdims=True)
        acc = acc * shrink + dot_tn(value_all[here, :], weights.astype(bf16))
        return new_max, run_sum, acc

    width = GROUP * BLOCK
    run_max, run_sum, acc = lax.fori_loop(
        first_block[i],
        i + 1,
        visit,
        (
            jnp.full((1, width), score_masked, f32),
            jnp.zeros((1, width), f32),
            jnp.zeros((PACK, width), f32),
        ),
    )
    acc = acc * (1.0 / run_sum)
    mixed_t = jnp.concatenate([acc[:HEAD_SIZE, :BLOCK], acc[HEAD_SIZE:, BLOCK:]], axis=0)
    mixed_t_ref[0] = mixed_t
    mixed_ref[...] = mixed_t.T.astype(bf16)
    log_ref[0] = run_max + jnp.log(run_sum)


def attention_forward(first_block, x_row, weight, gain, cosine, sine, start):
    tokens = x_row.shape[0]
    blocks = tokens // BLOCK
    row = lambda i, *_: (i, 0)
    page = lambda i, *_: (i, 0, 0)
    whole = lambda i, *_: (0, 0)
    return pl.pallas_call(
        attention_forward_kernel,
        grid_spec=pltpu.PrefetchScalarGridSpec(
            num_scalar_prefetch=1,
            grid=(blocks,),
            in_specs=[
                pl.BlockSpec((BLOCK, MODEL_WIDTH), row),
                pl.BlockSpec(weight.shape, whole),
                pl.BlockSpec((1, MODEL_WIDTH), whole),
                pl.BlockSpec((BLOCK, PACK), row),
                pl.BlockSpec((BLOCK, PACK), row),
                pl.BlockSpec((1, 1, BLOCK), page),
            ],
            out_specs=[
                pl.BlockSpec((BLOCK, MODEL_WIDTH), row),
                pl.BlockSpec((BLOCK, PACK), row),
                pl.BlockSpec((BLOCK, PACK), row),
                pl.BlockSpec((BLOCK, PACK), row),
                pl.BlockSpec((BLOCK, PACK), row),
                pl.BlockSpec((1, PACK, BLOCK), page),
                pl.BlockSpec((1, 1, GROUP * BLOCK), page),
            ],
            scratch_shapes=[pltpu.VMEM((tokens, PACK), bf16), pltpu.VMEM((tokens, PACK), bf16)],
        ),
        out_shape=[
            jax.ShapeDtypeStruct((tokens, MODEL_WIDTH), bf16),
            jax.ShapeDtypeStruct((tokens, PACK), bf16),
            jax.ShapeDtypeStruct((tokens, PACK), bf16),
            jax.ShapeDtypeStruct((tokens, PACK), bf16),
            jax.ShapeDtypeStruct((tokens, PACK), bf16),
            jax.ShapeDtypeStruct((blocks, PACK, BLOCK), f32),
            jax.ShapeDtypeStruct((blocks, 1, GROUP * BLOCK), f32),
        ],
        cost_estimate=cost(
            tokens * (2 * MODEL_WIDTH * 3 * PACK + 8 * PACK * tokens), tokens * MODEL_WIDTH * 4
        ),
        compiler_params=pltpu.CompilerParams(vmem_limit_bytes=VMEM_LIMIT),
        name="attention_forward",
    )(first_block, x_row, weight, gain, cosine, sine, start)


def attention_backward_kernel(
    shards,
    copies,
    first_block,
    place,
    query_ref,
    grad_ref,
    mixed_t_ref,
    log_ref,
    start_ref,
    cos_ref,
    sin_ref,
    key_ref,
    value_ref,
    small_ref,
    *refs,
):
    normed_refs, (lin_grad_ref, stay_ref, go_ref, key_acc, value_acc) = refs[:shards], refs[shards:]
    i = pl.program_id(0)
    blocks = pl.num_programs(0)

    @pl.when(i == 0)
    def _():
        key_acc[...] = jnp.zeros_like(key_acc)
        value_acc[...] = jnp.zeros_like(value_acc)

    query_two = head_stack(query_ref[...] * jnp.asarray(score_scale, bf16))
    grad = grad_ref[...]
    grad_two = head_stack(grad)
    product = mixed_t_ref[0] * grad.astype(f32).T
    delta = jnp.concatenate(
        [
            jnp.sum(product[:HEAD_SIZE], axis=0, keepdims=True),
            jnp.sum(product[HEAD_SIZE:], axis=0, keepdims=True),
        ],
        axis=1,
    )
    log_total = log_ref[0]
    start_two = jnp.concatenate([start_ref[0]] * GROUP, axis=1)

    def visit(j, query_acc):
        here = pl.ds(pl.multiple_of(j * BLOCK, BLOCK), BLOCK)
        key = key_ref[here, :]
        scores = dot_nt(key, query_two)
        probs = jnp.where(visible_from(j, i, start_two), jnp.exp(scores - log_total), 0.0)
        prob_grad = dot_nt(value_ref[here, :], grad_two)
        score_grad = (probs * (prob_grad - delta)).astype(bf16)
        value_acc[here, :] += dot_nn(probs.astype(bf16), grad_two)
        key_acc[here, :] += dot_nn(score_grad, query_two)
        return query_acc + dot_tn(score_grad, key)

    query_acc = lax.fori_loop(
        first_block[i], i + 1, visit, jnp.zeros((GROUP * BLOCK, PACK), f32)
    )
    lane = lax.broadcasted_iota(jnp.int32, (BLOCK, PACK), 1)
    rotated = jnp.where(lane < HEAD_SIZE, query_acc[:BLOCK], query_acc[BLOCK:]) * score_scale
    rows = pl.ds(pl.multiple_of(i * BLOCK, BLOCK), BLOCK)
    lin_grad_ref[rows, :PACK] = (
        rotated * cos_ref[rows, :] - swap_halves(rotated) * sin_ref[rows, :]
    ).astype(bf16)

    @pl.when(i == blocks - 1)
    def _():
        def finish(b, carry):
            here = pl.ds(pl.multiple_of(b * BLOCK, BLOCK), BLOCK)
            key_sum = key_acc[here, :]
            key_sum = key_sum + pltpu.roll(key_sum, HEAD_SIZE, 1)
            value_sum = value_acc[here, :]
            value_sum = value_sum + pltpu.roll(value_sum, HEAD_SIZE, 1)
            key_lin = key_sum * cos_ref[here, :] - swap_halves(key_sum) * sin_ref[here, :]
            lin_grad_ref[here, PACK:] = jnp.where(lane < HEAD_SIZE, key_lin, value_sum).astype(bf16)
            return carry

        lax.fori_loop(0, blocks, finish, 0)
        share = lin_grad_ref.shape[0] // copies
        own = lin_grad_ref[pl.ds(pl.multiple_of(place[1] * share, share), share), :]
        wide = MODEL_WIDTH // shards
        for n, j in enumerate(exchange_order(shards, 0)):
            out = (stay_ref, go_ref)[n // (shards // 2)]
            at = n % (shards // 2)
            out[at, :, : 2 * PACK] = dot_tn(normed_refs[n][...], own).astype(bf16)
            rows = pl.ds(pl.multiple_of((j ^ place[0]) * wide, wide), wide)
            out[at, :, 2 * PACK :] = small_ref[rows, :].astype(bf16)


def attention_backward(
    first_block,
    place,
    query,
    grad,
    mixed_t,
    log_total,
    start,
    cosine,
    sine,
    key,
    value,
    small,
    normed,
    shards,
    copies,
):
    tokens = query.shape[0]
    wide = MODEL_WIDTH // shards
    part = lambda j: pl.BlockSpec(
        (tokens // copies, wide), lambda i, first, place, j=j: (place[1], j ^ place[0])
    )
    out = (shards // 2, wide, 2 * PACK + LANES)
    blocks = tokens // BLOCK
    row = lambda i, *_: (i, 0)
    page = lambda i, *_: (i, 0, 0)
    whole = lambda i, *_: (0, 0)
    return pl.pallas_call(
        functools.partial(attention_backward_kernel, shards, copies),
        grid_spec=pltpu.PrefetchScalarGridSpec(
            num_scalar_prefetch=2,
            grid=(blocks,),
            in_specs=[
                pl.BlockSpec((BLOCK, PACK), row),
                pl.BlockSpec((BLOCK, PACK), row),
                pl.BlockSpec((1, PACK, BLOCK), page),
                pl.BlockSpec((1, 1, GROUP * BLOCK), page),
                pl.BlockSpec((1, 1, BLOCK), page),
                pl.BlockSpec((tokens, PACK), whole),
                pl.BlockSpec((tokens, PACK), whole),
                pl.BlockSpec((tokens, PACK), whole),
                pl.BlockSpec((tokens, PACK), whole),
                pl.BlockSpec((MODEL_WIDTH, LANES), whole),
            ]
            + [part(j) for j in exchange_order(shards, 0)],
            out_specs=[
                pl.BlockSpec((tokens, 2 * PACK), whole),
                pl.BlockSpec(out, lambda i, *_: (0, 0, 0)),
                pl.BlockSpec(out, lambda i, *_: (0, 0, 0)),
            ],
            scratch_shapes=[pltpu.VMEM((tokens, PACK), f32), pltpu.VMEM((tokens, PACK), f32)],
        ),
        out_shape=[
            jax.ShapeDtypeStruct((tokens, 2 * PACK), bf16),
            jax.ShapeDtypeStruct(out, bf16),
            jax.ShapeDtypeStruct(out, bf16),
        ],
        cost_estimate=cost(20 * tokens * tokens * PACK, tokens * PACK * 28),
        compiler_params=pltpu.CompilerParams(vmem_limit_bytes=VMEM_LIMIT),
        name="attention_backward",
    )(
        first_block,
        place,
        query,
        grad,
        mixed_t,
        log_total,
        start,
        cosine,
        sine,
        key,
        value,
        small,
        *([normed] * shards),
    )


def middle_kernel(
    home,
    mixed_ref,
    x_ref,
    weight_ref,
    gain_ref,
    router_ref,
    routes_ref,
    normed_ref,
    probs_ref,
    probs_t_ref,
    home_middle_ref,
    home_mixed_ref,
    home_normed_ref,
    home_probs_ref,
    keep_middle,
    keep_mixed,
):
    i = pl.program_id(0)
    parts = x_ref.shape[0] // SUB
    lane = lax.broadcasted_iota(jnp.int32, (SUB, LANES), 1)
    for n in range(parts):
        here = slice(n * SUB, (n + 1) * SUB)
        mixed = jnp.concatenate([mixed_ref[h, here] for h in range(KEY_VALUE_HEADS)], axis=1)
        middle = x_ref[here].astype(f32) + dot_nn(mixed, weight_ref[...])
        normed = (
            middle
            * lax.rsqrt(jnp.mean(middle * middle, axis=-1, keepdims=True) + eps_norm)
            * gain_ref[...]
        ).astype(bf16)
        normed_ref[here] = normed
        logits = dot_nn(normed, router_ref[...])
        routes = routes_ref[here]
        member = jnp.zeros_like(logits)
        for k in range(TOPK):
            member = jnp.where(lane == routes[:, k : k + 1], 1.0, member)
        chosen = jnp.where(member > 0, logits, score_masked)
        raised = jnp.exp(chosen - jnp.max(chosen, axis=-1, keepdims=True)) * member
        probs = raised / jnp.sum(raised, axis=-1, keepdims=True)
        probs_ref[here] = probs
        probs_t_ref[:, here] = probs.T[:EXPERTS]
        keep_middle[here] = middle
        keep_mixed[here] = mixed

    @pl.when(i == home[0] * BLOCK // x_ref.shape[0])
    def _():
        at = pl.ds(pl.multiple_of(home[0] * BLOCK % x_ref.shape[0], BLOCK), BLOCK)
        home_middle_ref[...] = keep_middle[at]
        home_mixed_ref[...] = keep_mixed[at]
        home_normed_ref[...] = normed_ref[at]
        home_probs_ref[...] = probs_ref[at]


def middle_forward(home, mixed, x_row, weight, gain, router, routes):
    tokens = x_row.shape[0]
    row = lambda i, *_: (i, 0)
    whole = lambda i, *_: (0, 0)
    return pl.pallas_call(
        middle_kernel,
        grid_spec=pltpu.PrefetchScalarGridSpec(
            num_scalar_prefetch=1,
            grid=(tokens // MID,),
            in_specs=[
                pl.BlockSpec((KEY_VALUE_HEADS, MID, PACK), lambda i, *_: (0, i, 0)),
                pl.BlockSpec((MID, MODEL_WIDTH), row),
                pl.BlockSpec((MODEL_WIDTH, MODEL_WIDTH), whole),
                pl.BlockSpec((1, MODEL_WIDTH), whole),
                pl.BlockSpec((MODEL_WIDTH, LANES), whole),
                pl.BlockSpec((MID, TOPK), row),
            ],
            out_specs=[
                pl.BlockSpec((MID, MODEL_WIDTH), row),
                pl.BlockSpec((MID, LANES), row),
                pl.BlockSpec((EXPERTS, MID), lambda i, *_: (0, i)),
                pl.BlockSpec((BLOCK, MODEL_WIDTH), whole),
                pl.BlockSpec((BLOCK, MODEL_WIDTH), whole),
                pl.BlockSpec((BLOCK, MODEL_WIDTH), whole),
                pl.BlockSpec((BLOCK, LANES), whole),
            ],
            scratch_shapes=[
                pltpu.VMEM((MID, MODEL_WIDTH), f32),
                pltpu.VMEM((MID, MODEL_WIDTH), bf16),
            ],
        ),
        out_shape=[
            jax.ShapeDtypeStruct((tokens, MODEL_WIDTH), bf16),
            jax.ShapeDtypeStruct((tokens, LANES), f32),
            jax.ShapeDtypeStruct((EXPERTS, tokens), f32),
            jax.ShapeDtypeStruct((BLOCK, MODEL_WIDTH), f32),
            jax.ShapeDtypeStruct((BLOCK, MODEL_WIDTH), bf16),
            jax.ShapeDtypeStruct((BLOCK, MODEL_WIDTH), bf16),
            jax.ShapeDtypeStruct((BLOCK, LANES), f32),
        ],
        cost_estimate=cost(
            2 * tokens * MODEL_WIDTH * (MODEL_WIDTH + LANES), tokens * MODEL_WIDTH * 6
        ),
        compiler_params=pltpu.CompilerParams(vmem_limit_bytes=VMEM_LIMIT),
        name="middle_forward",
    )(home, mixed, x_row, weight, gain, router, routes)


def cost(flops, moved):
    return pl.CostEstimate(flops=int(flops), transcendentals=0, bytes_accessed=int(moved))


def column_of(values, lane_wanted):
    lane = lax.broadcasted_iota(jnp.int32, values.shape, 1)
    return jnp.sum(
        jnp.where(lane == lane_wanted, values, jnp.zeros_like(values)), axis=-1, keepdims=True
    )


def expert_rows_kernel(shards, experts, group, place, *refs):
    normed_ref, cot_a_ref, cot_b_ref, probs_ref, probs_t_ref, slot_row_ref, slot_col_ref = refs[:7]
    weight_refs = [refs[7 + n * shards : 7 + (n + 1) * shards] for n in range(4)]
    (
        moe_ref,
        row_ref,
        weigh_ref,
        rows_ref,
        out_grad_ref,
        hidden_ref,
        gate_low_ref,
        up_low_ref,
        gate_all,
        up_all,
        down_all,
        out_all,
        back_all,
        sems,
    ) = refs[7 + 4 * shards :]
    first_expert, me = place[0], place[1]
    wide, narrow = MODEL_WIDTH // shards, FF // shards
    half = MODEL_WIDTH // 2

    def copies(e):
        made = []
        for j in range(shards):
            tall = pl.ds(pl.multiple_of((j ^ me) * wide, wide), wide)
            short = pl.ds(pl.multiple_of((j ^ me) * narrow, narrow), narrow)
            places = (
                gate_all.at[e, tall, :],
                up_all.at[e, tall, :],
                down_all.at[e, short, :half],
                down_all.at[e, short, half:],
            )
            for n in range(4):
                made.append(
                    pltpu.make_async_copy(weight_refs[n][j].at[e], places[n], sems.at[e, 4 * j + n])
                )
        return made

    @pl.when(pl.program_id(0) == 0)
    def _():
        for e in range(experts):
            for copy in copies(e):
                copy.start()

    slot_place = lax.broadcasted_iota(jnp.int32, (CAP, BLOCK), 0)
    slot_lane = lax.broadcasted_iota(jnp.int32, (BLOCK, CAP), 1)
    early, late = COT_EARLY, BLOCK - COT_EARLY
    cots = [
        jnp.concatenate(
            [
                cot_a_ref[b * early : (b + 1) * early, :],
                cot_b_ref[b * late : (b + 1) * late, :],
            ],
            axis=0,
        )
        for b in range(group)
    ]
    for e in range(experts):

        @pl.when(pl.program_id(0) == 0)
        def _():
            for copy in copies(e):
                copy.wait()

        picked, cot_picked = [], []
        hits = []
        for b in range(group):
            hit = slot_place == slot_row_ref[0, e * group + b : e * group + b + 1, :]
            hits.append(hit)
            pick = hit.astype(f32).astype(bf16)
            prob_row = probs_t_ref[pl.ds(first_expert + e, 1), b * BLOCK : (b + 1) * BLOCK]
            prob_slot = jnp.sum(jnp.where(hit, prob_row, 0.0), axis=-1, keepdims=True)
            picked.append(dot_nn(pick, normed_ref[b * BLOCK : (b + 1) * BLOCK, :]).astype(bf16))
            cot_picked.append((dot_nn(pick, cots[b]) * prob_slot).astype(bf16))
        rows = jnp.concatenate(picked, axis=0)
        out_grad = jnp.concatenate(cot_picked, axis=0)
        rows_ref[e] = rows
        out_grad_ref[e] = out_grad
        gate_pre = dot_nn(rows, gate_all[e])
        up_pre = dot_nn(rows, up_all[e])
        hidden_grad = dot_nt(out_grad, down_all[e])
        logistic = 1.0 / (1.0 + jnp.exp(-gate_pre))
        silu = gate_pre * logistic
        hidden = (silu * up_pre).astype(bf16)
        gate_low = (
            hidden_grad * up_pre * (logistic * (1.0 + gate_pre * (1.0 - logistic)))
        ).astype(bf16)
        up_low = (hidden_grad * silu).astype(bf16)
        hidden_ref[e] = hidden
        gate_low_ref[e] = gate_low
        up_low_ref[e] = up_low
        weigh = jnp.sum(hidden_grad * hidden.astype(f32), axis=-1, keepdims=True)
        out = dot_nn(hidden, down_all[e]).astype(bf16)
        row_grad = (dot_nt(gate_low, gate_all[e]) + dot_nt(up_low, up_all[e])).astype(bf16)
        for b in range(group):
            inside = slice(b * CAP, (b + 1) * CAP)
            out_all[b, e * CAP : (e + 1) * CAP, :] = out[inside]
            back_all[b, e * CAP : (e + 1) * CAP, :] = row_grad[inside]
            weigh_ref[0, e * group + b : e * group + b + 1, :] = jnp.sum(
                jnp.where(hits[b], weigh[inside], 0.0), axis=0, keepdims=True
            )
    for b in range(group):
        tokens = slice(b * BLOCK, (b + 1) * BLOCK)
        slot_cols, probs = slot_col_ref[tokens, :], probs_ref[tokens, :]
        plain, scaled = [], []
        for e in range(experts):
            hit = slot_lane == column_of(slot_cols, e)
            plain.append(hit.astype(f32).astype(bf16))
            scaled.append(jnp.where(hit, column_of(probs, first_expert + e), 0.0).astype(bf16))
        moe_ref[tokens, :] = dot_nn(jnp.concatenate(scaled, axis=1), out_all[b]).astype(bf16)
        row_ref[tokens, :] = dot_nn(jnp.concatenate(plain, axis=1), back_all[b]).astype(bf16)


def expert_rows(place, normed, cot_a, cot_b, probs, probs_t, slot_rows, slot_cols, weights, group):
    tokens = normed.shape[0]
    shards, experts = len(weights) // 4, weights[0].shape[0]
    span, slots = group * BLOCK, group * CAP
    steps = tokens // span
    row = lambda g, *_: (g, 0)
    page = lambda g, *_: (g, 0, 0)
    spread = lambda g, *_: (0, g, 0)
    total = tokens // BLOCK * CAP
    return pl.pallas_call(
        functools.partial(expert_rows_kernel, shards, experts, group),
        grid_spec=pltpu.PrefetchScalarGridSpec(
            num_scalar_prefetch=1,
            grid=(steps,),
            in_specs=[
                pl.BlockSpec((span, MODEL_WIDTH), row),
                pl.BlockSpec((group * COT_EARLY, MODEL_WIDTH), row),
                pl.BlockSpec((group * (BLOCK - COT_EARLY), MODEL_WIDTH), row),
                pl.BlockSpec((span, LANES), row),
                pl.BlockSpec((EXPERTS, span), lambda g, *_: (0, g)),
                pl.BlockSpec((1, experts * group, BLOCK), page),
                pl.BlockSpec((span, LANES), row),
            ]
            + [pl.BlockSpec(memory_space=pl.ANY)] * (4 * shards),
            out_specs=[
                pl.BlockSpec((span, MODEL_WIDTH), row),
                pl.BlockSpec((span, MODEL_WIDTH), row),
                pl.BlockSpec((1, experts * group, BLOCK), page),
                pl.BlockSpec((experts, slots, MODEL_WIDTH), spread),
                pl.BlockSpec((experts, slots, MODEL_WIDTH), spread),
                pl.BlockSpec((experts, slots, FF), spread),
                pl.BlockSpec((experts, slots, FF), spread),
                pl.BlockSpec((experts, slots, FF), spread),
            ],
            scratch_shapes=[
                pltpu.VMEM((experts, MODEL_WIDTH, FF), bf16),
                pltpu.VMEM((experts, MODEL_WIDTH, FF), bf16),
                pltpu.VMEM((experts, FF, MODEL_WIDTH), bf16),
                pltpu.VMEM((group, experts * CAP, MODEL_WIDTH), bf16),
                pltpu.VMEM((group, experts * CAP, MODEL_WIDTH), bf16),
                pltpu.SemaphoreType.DMA((experts, 4 * shards)),
            ],
        ),
        out_shape=[
            jax.ShapeDtypeStruct((tokens, MODEL_WIDTH), bf16),
            jax.ShapeDtypeStruct((tokens, MODEL_WIDTH), bf16),
            jax.ShapeDtypeStruct((steps, experts * group, BLOCK), f32),
            jax.ShapeDtypeStruct((experts, total, MODEL_WIDTH), bf16),
            jax.ShapeDtypeStruct((experts, total, MODEL_WIDTH), bf16),
            jax.ShapeDtypeStruct((experts, total, FF), bf16),
            jax.ShapeDtypeStruct((experts, total, FF), bf16),
            jax.ShapeDtypeStruct((experts, total, FF), bf16),
        ],
        cost_estimate=cost(
            12 * experts * total * MODEL_WIDTH * FF + 8 * experts * total * MODEL_WIDTH * BLOCK,
            experts * (3 * MODEL_WIDTH * FF + total * (2 * MODEL_WIDTH + 3 * FF)) * 2
            + tokens * MODEL_WIDTH * 8,
        ),
        compiler_params=pltpu.CompilerParams(vmem_limit_bytes=VMEM_LIMIT),
        name="expert_rows",
    )(place, normed, cot_a, cot_b, probs, probs_t, slot_rows, slot_cols, *weights)


def expert_weights_kernel(shards, place, *refs):
    rows_ref, out_grad_ref, hidden_ref, gate_low_ref, up_low_ref = refs[:5]
    outs, (gate_acc, up_acc, down_acc) = refs[5:17], refs[17:]
    me, c = place[1], pl.program_id(1)
    rows = rows_ref[0]
    for acc, left, right in (
        (gate_acc, rows, gate_low_ref[0]),
        (up_acc, rows, up_low_ref[0]),
        (down_acc, hidden_ref[0], out_grad_ref[0]),
    ):
        part = dot_tn(left, right)

        @pl.when(c == 0)
        def _():
            acc[...] = part

        @pl.when(c > 0)
        def _():
            acc[...] += part

    wide, narrow = MODEL_WIDTH // shards, FF // shards
    half = MODEL_WIDTH // 2

    @pl.when(c == pl.num_programs(1) - 1)
    def _():
        for side in range(2):
            square = (gate_acc, up_acc)[side]
            order = exchange_order(shards, side)
            for n, j in enumerate(order):
                kind, at = divmod(n, shards // 2)
                base = (j ^ me) * wide
                low = pl.ds(pl.multiple_of(base, narrow), narrow)
                high = pl.ds(pl.multiple_of(base + narrow, narrow), narrow)
                short = pl.ds(pl.multiple_of((j ^ me) * narrow, narrow), narrow)
                pieces = (
                    square[low, :],
                    square[high, :],
                    down_acc[short, side * half : (side + 1) * half],
                )
                for piece, value in enumerate(pieces):
                    outs[6 * side + 2 * piece + kind][at, 0] = value.astype(bf16)


def exchange_order(shards, side):
    first = (1, 2)[side]
    stay = [j for j in range(shards) if not j & first]
    return stay + [j ^ first for j in stay]


def expert_weights(place, rows, out_grad, hidden, gate_low, up_low, shards):
    experts, total = rows.shape[:2]
    chunk = min(total, 1024)
    narrow = FF // shards
    spec = lambda width: pl.BlockSpec((1, chunk, width), lambda e, c, *_: (e, c, 0))
    return pl.pallas_call(
        functools.partial(expert_weights_kernel, shards),
        grid_spec=pltpu.PrefetchScalarGridSpec(
            num_scalar_prefetch=1,
            grid=(experts, total // chunk),
            in_specs=[spec(MODEL_WIDTH), spec(MODEL_WIDTH), spec(FF), spec(FF), spec(FF)],
            out_specs=[
                pl.BlockSpec((shards // 2, 1, narrow, FF), lambda e, c, *_: (0, e, 0, 0))
            ]
            * 12,
            scratch_shapes=[
                pltpu.VMEM((MODEL_WIDTH, FF), f32),
                pltpu.VMEM((MODEL_WIDTH, FF), f32),
                pltpu.VMEM((FF, MODEL_WIDTH), f32),
            ],
        ),
        out_shape=[jax.ShapeDtypeStruct((shards // 2, experts, narrow, FF), bf16)] * 12,
        cost_estimate=cost(
            6 * experts * total * MODEL_WIDTH * FF,
            experts * (total * (2 * MODEL_WIDTH + 3 * FF) + 3 * MODEL_WIDTH * FF) * 2,
        ),
        compiler_params=pltpu.CompilerParams(vmem_limit_bytes=VMEM_LIMIT),
        name="expert_weights",
    )(place, rows, out_grad, hidden, gate_low, up_low)


def along_seq(value, distance, shards):
    return lax.ppermute(value, "seq", [(i, i ^ distance) for i in range(shards)])


def gather_over_seq(value, shards):
    me = lax.axis_index("seq")
    held = jnp.stack([value] + [along_seq(value, k, shards) for k in range(1, shards)])
    return jnp.stack(
        [lax.dynamic_index_in_dim(held, s ^ me, 0, keepdims=False) for s in range(shards)]
    )


def sum_over_seq(value, shards):
    me = lax.axis_index("seq")
    part = lambda j: lax.dynamic_index_in_dim(value, j ^ me, 0, keepdims=False)
    sent = along_seq(jnp.stack([part(1), part(3)]), 1, shards).astype(f32)
    passed = (part(2).astype(f32) + sent[1]).astype(value.dtype)
    return part(0).astype(f32) + sent[0] + along_seq(passed, 2, shards).astype(f32)


def swap_over(value, axes):
    return lax.all_to_all(value, axes, split_axis=0, concat_axis=0, tiled=True)


def after(value, *others):
    return lax.optimization_barrier((value,) + others)[0]


def on_device(
    shards,
    ranks,
    layer_input,
    doc_ids,
    expert_routes,
    attn_gain,
    query_weight,
    key_projection_weight,
    value_projection_weight,
    out_weight,
    ffn_gain,
    router_weight,
    gate_weight,
    up_weight,
    down_weight,
    out_cotangent,
):
    local = layer_input.shape[0]
    tokens = doc_ids.shape[1]
    copies = ranks // KEY_VALUE_HEADS
    experts = gate_weight.shape[0]
    rows = query_weight.shape[0]
    blocks = tokens // BLOCK
    rank = lax.axis_index("exp")
    me = lax.axis_index("seq")
    head_width = GROUP * HEAD_SIZE
    wide, narrow, half = MODEL_WIDTH // shards, FF // shards, MODEL_WIDTH // 2

    x_row = lax.all_gather(layer_input, "exp", axis=0, tiled=True)

    by_head = jnp.concatenate(
        [
            query_weight.reshape(rows, KEY_VALUE_HEADS, head_width),
            key_projection_weight.reshape(rows, KEY_VALUE_HEADS, HEAD_SIZE),
            value_projection_weight.reshape(rows, KEY_VALUE_HEADS, HEAD_SIZE),
        ],
        axis=2,
    )
    own_width = by_head.shape[2]
    per_row = local * TOPK // rows
    small = jnp.concatenate(
        [
            router_weight,
            attn_gain[:, None],
            ffn_gain[:, None],
            jnp.zeros((rows, -(EXPERTS + 2 + per_row) % LANES), bf16),
            expert_routes.astype(bf16).reshape(rows, per_row),
        ],
        axis=1,
    )
    to_send = jnp.concatenate(
        [
            jnp.repeat(by_head.transpose(1, 0, 2), copies, axis=0),
            jnp.broadcast_to(small[None], (ranks,) + small.shape),
        ],
        axis=2,
    )
    got = swap_over(to_send, "exp").reshape(ranks * rows, -1)
    routes_row = got[:, got.shape[1] - per_row :].reshape(tokens, TOPK)
    routes_row = routes_row.astype(jnp.int32)
    weights = gather_over_seq(got[:, : own_width + LANES], shards).reshape(MODEL_WIDTH, -1)
    own_weight = weights[:, :own_width]
    small_all = weights[:, own_width:]
    gain_one = small_all[:, EXPERTS].astype(f32)[None]
    gain_two = small_all[:, EXPERTS + 1].astype(f32)[None]
    lane = jnp.arange(LANES)[None, :]
    router_mat = jnp.where(lane < EXPERTS, small_all, 0)
    key_part = own_weight[:, head_width : head_width + HEAD_SIZE]
    value_part = own_weight[:, head_width + HEAD_SIZE :]
    wide_weight = jnp.concatenate(
        [own_weight[:, :head_width]] + [key_part] * GROUP + [value_part] * GROUP, axis=1
    )

    left_weight, right_weight = down_weight[:, :, :half], down_weight[:, :, half:]
    near_gate, near_up = along_seq(gate_weight, 1, shards), along_seq(up_weight, 2, shards)

    seg_row = doc_ids[0]
    smaller = jnp.sum(
        (seg_row[None, :] < jnp.arange(DOCS, dtype=jnp.int32)[:, None]).astype(jnp.int32), axis=1
    )
    start = jnp.sum(
        jnp.where(seg_row[None, :] == jnp.arange(DOCS)[:, None], smaller[:, None], 0), axis=0
    ).astype(jnp.int32)
    positions = (jnp.arange(tokens, dtype=jnp.int32) - start).astype(f32)
    half_head = HEAD_SIZE // 2
    inv_freq = rope_base ** (-2.0 * jnp.arange(half_head, dtype=f32) / HEAD_SIZE)
    angles = positions[:, None] * inv_freq[None, :]
    cos_half, sin_half = jnp.cos(angles), jnp.sin(angles)
    cosine = jnp.concatenate([cos_half] * (2 * GROUP), axis=1)
    sine = jnp.concatenate([-sin_half, sin_half] * GROUP, axis=1)
    first_block = start[::BLOCK] // BLOCK
    start_blocks = start.reshape(blocks, 1, BLOCK)

    first_expert = rank * experts
    own_ids = first_expert + jnp.arange(experts, dtype=jnp.int32)
    own_member = jnp.any(routes_row.T[None] == own_ids[:, None, None], axis=1)
    own_member = own_member.reshape(experts, blocks, BLOCK)
    triangle = (jnp.arange(BLOCK)[:, None] <= jnp.arange(BLOCK)[None, :]).astype(bf16)
    counts = jnp.dot(
        own_member.reshape(experts * blocks, BLOCK).astype(bf16),
        triangle,
        preferred_element_type=f32,
    ).reshape(experts, blocks, BLOCK)
    slots = jnp.where(own_member, counts.astype(jnp.int32) - 1, -1)
    group = 2
    slot_rows = (
        slots.reshape(experts, blocks // group, group, BLOCK)
        .transpose(1, 0, 2, 3)
        .reshape(blocks // group, experts * group, BLOCK)
    )
    slot_cols = jnp.pad(
        slots.reshape(experts, tokens).T, ((0, 0), (0, LANES - experts)), constant_values=-1
    )
    place = jnp.stack([first_expert, me])

    key_place = jnp.stack([me, lax.rem(rank, copies)])
    x_row, near_gate, near_up, slot_rows, slot_cols, place, key_place, routes_row = (
        lax.optimization_barrier(
            (x_row, near_gate, near_up, slot_rows, slot_cols, place, key_place, routes_row)
        )
    )
    cot_a = lax.all_gather(after(out_cotangent[:COT_EARLY], got), "exp", axis=0, tiled=True)
    out_rows = lax.all_gather(after(out_weight, got), "exp", axis=0, tiled=True)
    x_row, out_rows = lax.optimization_barrier((x_row, out_rows))
    left_weight, right_weight = lax.optimization_barrier((left_weight, right_weight, near_gate))[:2]
    near_left, near_right = along_seq(left_weight, 1, shards), along_seq(right_weight, 2, shards)
    next_left, next_right = along_seq(left_weight, 2, shards), along_seq(right_weight, 1, shards)

    normed_row, query_low, key_low, value_low, mixed_own, mixed_t, log_total = attention_forward(
        first_block, x_row, wide_weight, gain_one, cosine, sine, start_blocks
    )
    share = tokens // copies
    part = lax.rem(rank, copies) * share
    (
        mixed_own,
        cot_a,
        near_left,
        near_right,
        next_left,
        next_right,
    ) = lax.optimization_barrier(
        (mixed_own, cot_a, near_left, near_right, next_left, next_right)
    )
    mixed_part = lax.dynamic_slice_in_dim(mixed_own, part, share) if copies > 1 else mixed_own
    mixed_row = lax.all_gather(mixed_part, "exp", axis=0, tiled=True)
    cot_b = lax.all_gather(
        after(out_cotangent[COT_EARLY:], mixed_own), "exp", axis=0, tiled=True
    )
    out_mat = gather_over_seq(after(out_rows, mixed_own), shards).reshape(MODEL_WIDTH, -1)
    gate_weight, up_weight = lax.optimization_barrier((gate_weight, up_weight, near_left))[:2]
    next_gate, next_up = along_seq(gate_weight, 2, shards), along_seq(up_weight, 1, shards)
    far_left = along_seq(after(near_left, mixed_own), 2, shards)
    far_right = along_seq(after(near_right, mixed_own), 1, shards)
    mixed_row, out_mat, next_gate, next_up, far_left, far_right = lax.optimization_barrier(
        (mixed_row, out_mat, next_gate, next_up, far_left, far_right)
    )
    far_gate = along_seq(after(near_gate, next_gate), 2, shards)
    far_up = along_seq(after(near_up, next_up), 1, shards)
    mixed_row = mixed_row.reshape(KEY_VALUE_HEADS, tokens, head_width)
    (
        normed_two_row,
        probs_row,
        probs_t,
        middle,
        mixed_home,
        normed_two_home,
        probs_home,
    ) = middle_forward(rank[None], mixed_row, x_row, out_mat, gain_two, router_mat, routes_row)
    normed_two_row, far_gate, far_up = lax.optimization_barrier((normed_two_row, far_gate, far_up))
    weight_all = lax.all_gather(
        (lambda w: lax.dynamic_slice_in_dim(w, lax.rem(rank, copies) * (MODEL_WIDTH // copies), MODEL_WIDTH // copies) if copies > 1 else w)(
            after(own_weight, normed_two_row)
        ),
        "exp",
        axis=0,
        tiled=True,
    ).reshape(KEY_VALUE_HEADS, MODEL_WIDTH, own_width)

    moe_part, row_part, weigh, *kept = expert_rows(
        place,
        normed_two_row,
        cot_a,
        cot_b,
        probs_row,
        probs_t,
        slot_rows,
        slot_cols,
        [gate_weight, near_gate, next_gate, far_gate]
        + [up_weight, next_up, near_up, far_up]
        + [left_weight, near_left, next_left, far_left]
        + [right_weight, next_right, near_right, far_right],
        group,
    )
    mixed_turned = (
        mixed_home.reshape(local, shards, ranks, rows)
        .transpose(0, 2, 1, 3)
        .reshape(local, MODEL_WIDTH)
    )
    row_part, weight_all, mixed_turned = lax.optimization_barrier(
        (row_part, weight_all, mixed_turned)
    )
    row_sum = lax.psum_scatter(row_part, "exp", scatter_dimension=0, tiled=True)
    pieces = expert_weights(place, *kept, shards)
    stay, go = pieces[0::2], pieces[1::2]
    weigh_home = swap_over(
        after(weigh, go[0]).reshape(blocks // group, experts, group, BLOCK)
        .transpose(0, 2, 1, 3)
        .reshape(ranks, experts, local),
        "exp",
    )
    weigh_home = weigh_home.reshape(EXPERTS, local).T

    def first_exchange(piece, since):
        a, b = go[piece], go[3 + piece]
        if since is not None:
            a, b = after(a, since), after(b, since)
        return along_seq(a, 1, shards), along_seq(b, 2, shards)

    come_0 = first_exchange(0, None)
    row_sum, come_0, weigh_home = lax.optimization_barrier(
        (after(row_sum, go[0]), come_0, weigh_home)
    )
    come_1 = first_exchange(1, row_sum)

    out_grad = out_cotangent.astype(f32)
    probs_own = probs_home[:, :EXPERTS]
    logits_low = (
        weigh_home - probs_own * jnp.sum(weigh_home, axis=1, keepdims=True)
    ).astype(bf16)
    router_part = dot_tn(normed_two_home, logits_low)
    normed_two_grad = row_sum.astype(f32) + dot_nt(logits_low, router_mat[:, :EXPERTS])
    scale_two = lax.rsqrt(jnp.mean(middle * middle, axis=-1, keepdims=True) + eps_norm)
    gain_two_part = jnp.sum(normed_two_grad * middle * scale_two, axis=0)
    through = gain_two * normed_two_grad
    middle_grad = (
        out_grad
        + scale_two * through
        - middle * scale_two**3 * jnp.mean(middle * through, axis=-1, keepdims=True)
    )
    branch_low = middle_grad.astype(bf16)
    mixed_grad = dot_nt(branch_low, out_mat).astype(bf16)
    mixed_grad_row = swap_over(
        jnp.repeat(
            mixed_grad.reshape(local, KEY_VALUE_HEADS, head_width).transpose(1, 0, 2), copies, axis=0
        ),
        "exp",
    ).reshape(tokens, head_width)

    out_part = dot_tn(mixed_turned, branch_low).astype(bf16)
    out_part = lax.psum_scatter(out_part, "exp", scatter_dimension=0, tiled=True)
    moe_sum = lax.psum_scatter(
        after(moe_part, mixed_grad_row), "exp", scatter_dimension=0, tiled=True
    )

    mixed_grad_row, come_1 = lax.optimization_barrier((mixed_grad_row, come_1))
    come_2 = first_exchange(2, mixed_grad_row)

    come = [come_0, come_1, come_2]
    add = lambda x, y: x.astype(f32) + y.astype(f32)
    kept_parts = lambda side, n: stay[3 * side + n][0].astype(f32) + come[n][side][0].astype(f32)

    def pass_on(side, pieces, since):
        parts = [
            (stay[3 * side + n][1].astype(f32) + come[n][side][1].astype(f32)).astype(bf16)
            for n in pieces
        ]
        parts = after(jnp.stack(parts) if len(parts) > 1 else parts[0][None], since)
        return along_seq(parts, (2, 1)[side], shards)

    early_a, early_b = pass_on(0, (0,), mixed_grad_row), pass_on(1, (0,), mixed_grad_row)
    small_part = jnp.concatenate(
        [router_part, gain_two_part[:, None], jnp.zeros((MODEL_WIDTH, LANES - EXPERTS - 1), f32)],
        axis=1,
    )
    lin_low, weight_stay, weight_go = attention_backward(
        first_block,
        key_place,
        query_low,
        mixed_grad_row,
        mixed_t,
        log_total,
        start_blocks,
        cosine,
        sine,
        key_low,
        value_low,
        small_part,
        normed_row,
        shards,
        copies,
    )
    lin_home = swap_over(lin_low.reshape(ranks, local, own_width), "exp")
    weight_come = along_seq(weight_go, 1, shards)
    weight_come, come_2, early_a, early_b, out_part = lax.optimization_barrier(
        (weight_come, come_2, early_a, early_b, out_part)
    )
    come[2] = come_2
    weight_pass = along_seq(add(weight_stay[1], weight_come[1]).astype(bf16), 2, shards)
    weight_sum = (
        add(weight_stay[0], weight_come[0]) + weight_pass.astype(f32)
    ).astype(bf16)
    late_a, late_b = pass_on(0, (1, 2), weight_sum), pass_on(1, (1, 2), weight_sum)
    out_weight_grad = sum_over_seq(out_part.reshape(shards, rows, MODEL_WIDTH), shards)
    weight_sum, lin_home = lax.optimization_barrier((weight_sum, lin_home))
    weight_home = swap_over(weight_sum.reshape(ranks, rows, -1), "exp").astype(f32)
    weight_home, late_a, late_b = lax.optimization_barrier((weight_home, late_a, late_b))
    halves = [
        [
            kept_parts(side, n) + passed.astype(f32)
            for n, passed in enumerate((early[0], late[0], late[1]))
        ]
        for side, (early, late) in enumerate(((early_a, late_a), (early_b, late_b)))
    ]
    gate_grad, up_grad = (jnp.concatenate(h[:2], axis=1) for h in halves)
    down_grad = jnp.concatenate([halves[0][2], halves[1][2]], axis=2)
    tail = jnp.sum(weight_home[:, :, own_width:], axis=0)
    router_grad = tail[:, :EXPERTS]
    ffn_gain_grad = tail[:, EXPERTS]
    weight_home = jnp.sum(
        weight_home[:, :, :own_width].reshape(KEY_VALUE_HEADS, copies, rows, own_width), axis=1
    ).transpose(1, 0, 2)
    lin_home = lin_home.reshape(KEY_VALUE_HEADS, copies, local, own_width)[:, 0]
    normed_grad = dot_nt(
        lin_home.transpose(1, 0, 2).reshape(local, -1),
        weight_all.transpose(1, 0, 2).reshape(MODEL_WIDTH, -1),
    )
    inputs = layer_input.astype(f32)
    scale_one = lax.rsqrt(jnp.mean(inputs * inputs, axis=-1, keepdims=True) + eps_norm)
    through_one = gain_one * normed_grad
    input_grad = (
        middle_grad
        + scale_one * through_one
        - inputs * scale_one**3 * jnp.mean(inputs * through_one, axis=-1, keepdims=True)
    )

    query_grad = weight_home[:, :, :head_width].reshape(rows, -1)
    key_grad = weight_home[:, :, head_width : head_width + HEAD_SIZE].reshape(rows, -1)
    value_grad = weight_home[:, :, head_width + HEAD_SIZE :].reshape(rows, -1)
    attn_gain_grad = jnp.sum(weight_home * by_head.astype(f32), axis=(1, 2)) / attn_gain.astype(f32)

    layer_output = (middle + moe_sum.astype(f32)).astype(bf16)
    return (
        layer_output,
        input_grad,
        attn_gain_grad,
        query_grad,
        key_grad,
        value_grad,
        out_weight_grad,
        ffn_gain_grad,
        router_grad,
        gate_grad,
        up_grad,
        down_grad,
    )


def solution(mesh):
    tokens_2d = P(("seq", "exp"), None)
    vector = P(("seq", "exp"))
    expert = P("exp", "seq", None)
    return jax.shard_map(
        functools.partial(on_device, mesh.shape["seq"], mesh.shape["exp"]),
        mesh=mesh,
        in_specs=(
            tokens_2d,
            P("seq", None),
            tokens_2d,
            vector,
            tokens_2d,
            tokens_2d,
            tokens_2d,
            tokens_2d,
            vector,
            tokens_2d,
            expert,
            expert,
            expert,
            tokens_2d,
        ),
        out_specs=(
            tokens_2d,
            tokens_2d,
            vector,
            tokens_2d,
            tokens_2d,
            tokens_2d,
            tokens_2d,
            vector,
            tokens_2d,
            expert,
            expert,
            expert,
        ),
        check_vma=False,
    )
```
